32 devices in a mesh: ulysses: 4 (over x, core), blk: 8 (over z, y).
Axes of the slice: x: 2, y: 2, z: 4, core: 2. Of those that a mesh axis runs over, the one named last changes fastest.
Arguments:
- inputs: bfloat16 [8, 512, 1024], P('blk', 'ulysses'), may hold values from -6 to 6
- cotangent: bfloat16 [8, 512, 1024], P('blk', 'ulysses'), may hold values from -6 to 6
- segment_ids: int32 [8, 512], replicated, may hold values from 0 to 30, as said below
- bucket_table: int32 [257], replicated, may hold values from 0 to 31, as said below
- gain_attention: float32 [1024], replicated, may hold values from 0.5 to 1.5
- query_weight: bfloat16 [1024, 1024], P(('ulysses', 'blk')), may hold values from -0.046875 to 0.046875
- key_weight: bfloat16 [1024, 1024], P(('ulysses', 'blk')), may hold values from -0.1875 to 0.1875
- value_weight: bfloat16 [1024, 1024], P(('ulysses', 'blk')), may hold values from -0.1875 to 0.1875
- output_weight: bfloat16 [1024, 1024], P(('ulysses', 'blk')), may hold values from -0.75 to 0.75
- bucket_bias: float32 [32, 16], replicated, may hold values from -3 to 3
- gain_feedforward: float32 [1024], replicated, may hold values from 0.5 to 1.5
- gate_weight: bfloat16 [2816, 1024], P(('ulysses', 'blk')), may hold values from -0.1875 to 0.1875
- up_weight: bfloat16 [2816, 1024], P(('ulysses', 'blk')), may hold values from -0.1875 to 0.1875
- down_weight: bfloat16 [2816, 1024], P(('ulysses', 'blk')), may hold values from -0.109375 to 0.109375
Outputs:
- layer_out: bfloat16 [8, 512, 1024], P('blk', 'ulysses')
- grad_inputs: bfloat16 [8, 512, 1024], P('blk', 'ulysses')
- grad_gain_attention: float32 [1024], replicated
- grad_query_weight: float32 [1024, 1024], P(('ulysses', 'blk'))
- grad_key_weight: float32 [1024, 1024], P(('ulysses', 'blk'))
- grad_value_weight: float32 [1024, 1024], P(('ulysses', 'blk'))
- grad_output_weight: float32 [1024, 1024], P(('ulysses', 'blk'))
- grad_bucket_bias: float32 [32, 16], replicated
- grad_gain_feedforward: float32 [1024], replicated
- grad_gate_weight: float32 [2816, 1024], P(('ulysses', 'blk'))
- grad_up_weight: float32 [2816, 1024], P(('ulysses', 'blk'))
- grad_down_weight: float32 [2816, 1024], P(('ulysses', 'blk'))
The draws below stay inside these ranges and needn't reach their ends.
Inputs may be any that keep to these rules, and one draw needn't show every extreme that they name: bucket_table[128 + o] is the bucket of a key o positions after its query, for o from -128 to 128 (farther keys take the end entries): 0 at o = 0, 1 to 15 for keys before the query, 16 to 31 for keys after it, never falling as |o| grows, 15 and 31 at the two ends. `segment_ids`: never falling along the sequence. Positions 256 * w to 256 * w + 255 form window w; window 0 is block 0, every later window w holds exactly the two non-empty blocks 2 w - 1 and 2 w.
All inputs are finite; a program needn't handle non-finite values.
Results may differ from the reference program's by a relative error of at most 0.025.
Values may be sent and summed in bfloat16 or wider, within the bound.
No kernel may reach another device: no remote copies, remote signals or barrier semaphores. Data moves between devices by JAX's collectives and lax.ppermute only.
A program may use at most 192 MiB of HBM per device.

```python
import math
import jax
import jax.numpy as jnp
from jax import lax

D = 1024
H = 16
FF = 2816
NB = 32
MAXD = 128
SEG_MOST = 256
RUN = 512
RUNS = 8


def draw_bucket_table(key, part):
    half_count = NB // 2
    places = jnp.arange(MAXD, dtype=jnp.int32)
    before_side = jnp.sort(jax.random.randint(jax.random.fold_in(key, 11), (MAXD,), 1, half_count, dtype=jnp.int32))
    after_side = jnp.sort(jax.random.randint(jax.random.fold_in(key, 12), (MAXD,), 0, half_count, dtype=jnp.int32))
    before_side = jnp.where(places == MAXD - 1, half_count - 1, before_side)
    after_side = jnp.where(places == MAXD - 1, half_count - 1, after_side)
    middle_zero = jnp.zeros((1,), jnp.int32)
    return jnp.concatenate((before_side[::-1], middle_zero, half_count + after_side)).astype(jnp.int32)


def draw_segment_ids(key, part):
    length = RUNS * RUN
    windows = length // SEG_MOST
    cuts_drawn = jax.random.randint(jax.random.fold_in(key, 21), (windows,), 1, SEG_MOST, dtype=jnp.int32)
    places = jnp.arange(length, dtype=jnp.int32)
    window_of = places // SEG_MOST
    inside = places % SEG_MOST
    later_ids = jnp.where(inside < cuts_drawn[window_of], 2 * window_of - 1, 2 * window_of)
    block_ids = jnp.where(window_of == 0, 0, later_ids)
    return block_ids.reshape(RUNS, RUN).astype(jnp.int32)


def steps_of(key, extent, cuts, least, high):
    factor_of, own = 1.0, jax.random.fold_in(key, 6)
    for axis_at, parts in cuts:
        heights = jnp.exp(jax.random.uniform(jax.random.fold_in(own, axis_at), (parts,), jnp.float32, least / len(cuts), high / len(cuts)))
        factor_of = factor_of * jnp.repeat(heights, extent[axis_at] // parts).reshape([-1 if axis == axis_at else 1 for axis in range(len(extent))])
    return factor_of


def bell_draw(own_key, shape, width, bound, split=(), kind=jnp.bfloat16):
    values = width * jax.random.normal(own_key, shape, jnp.float32)
    if split:
        values = values * steps_of(own_key, shape, split, -0.22, 0.18)
    return jnp.clip(values, -bound, bound).astype(kind)


def setup_inputs(seed: int = 0) -> dict:
    splits = jax.random.split(jax.random.key(seed), 15)
    return {
        "inputs": bell_draw(splits[0], (RUNS, RUN, D), 1.0, 6.0, ((0, 8), (1, 4))),
        "cotangent": bell_draw(splits[1], (RUNS, RUN, D), 1.0, 6.0, ((0, 8), (1, 4))),
        "segment_ids": draw_segment_ids(jax.random.fold_in(splits[14], 71), 0),
        "bucket_table": draw_bucket_table(jax.random.fold_in(splits[14], 71), 0),
        "gain_attention": jnp.clip(1.0 + 0.1 * jax.random.normal(splits[4], (D,), jnp.float32), 0.5, 1.5),
        "query_weight": bell_draw(splits[5], (D, D), (16 * D) ** -0.5, 0.046875, ((0, 32),)),
        "key_weight": bell_draw(splits[6], (D, D), D ** -0.5, 0.1875, ((0, 32),)),
        "value_weight": bell_draw(splits[7], (D, D), D ** -0.5, 0.1875, ((0, 32),)),
        "output_weight": bell_draw(splits[8], (D, D), (D // 16) ** -0.5, 0.75, ((0, 32),)),
        "bucket_bias": bell_draw(splits[9], (NB, H), 0.5, 3.0, (), jnp.float32),
        "gain_feedforward": jnp.clip(1.0 + 0.1 * jax.random.normal(splits[10], (D,), jnp.float32), 0.5, 1.5),
        "gate_weight": bell_draw(splits[11], (FF, D), D ** -0.5, 0.1875, ((0, 32),)),
        "up_weight": bell_draw(splits[12], (FF, D), D ** -0.5, 0.1875, ((0, 32),)),
        "down_weight": bell_draw(splits[13], (FF, D), FF ** -0.5, 0.109375, ((0, 32),)),
    }


EPSILON = 1e-06
NEGATIVE = -1e+30
HIGHEST = lax.Precision.HIGHEST

@jax.custom_vjp
def low(v):
    return lax.optimization_barrier(v.astype(jnp.bfloat16)).astype(jnp.float32)

@jax.custom_vjp
def low_back(v):
    return v

def low_keep(v):
    return (low(v), None)

def low_pass(kept, grad):
    return (grad,)

def back_keep(v):
    return (v, None)

def back_low(kept, grad):
    return (low(grad),)
low.defvjp(low_keep, low_pass)
low_back.defvjp(back_keep, back_low)

def root_norm(values, gain_vec):
    return values * lax.rsqrt(lax.optimization_barrier(jnp.mean(values * values, axis=-1, keepdims=True)) + EPSILON) * gain_vec

def attention(queries, keys_all, values_all, bias_table, segment_flat):
    length = keys_all.shape[0]
    block_rows = math.gcd(length, 128)
    block_count = length // block_rows
    head_count = bias_table.shape[1]
    head_dim = queries.shape[1] // head_count
    positions = jnp.arange(length, dtype=jnp.int32)
    keys_heads = keys_all.reshape(length, head_count, head_dim)
    values_heads = values_all.reshape(length, head_count, head_dim)

    def one_block(pieces):
        query_block, query_pos, query_seg = pieces
        bucket_index = jnp.clip(positions[None, :] - query_pos[:, None], -MAXD, MAXD) + MAXD
        bias_values = jnp.transpose(bias_table[bucket_index], (2, 0, 1))
        raw_scores = jnp.einsum('qhd,khd->hqk', query_block.reshape(block_rows, head_count, head_dim), keys_heads, precision=HIGHEST) + bias_values
        scores = low_back(raw_scores)
        allowed = segment_flat[None, :] <= query_seg[:, None]
        weights = jax.nn.softmax(jnp.where(allowed[None, :, :], scores, NEGATIVE), axis=-1)
        mixed_rows = jnp.einsum('hqk,khd->qhd', low(weights), values_heads, precision=HIGHEST)
        return mixed_rows.reshape(block_rows, head_count * head_dim)
    stacked = lax.map(jax.checkpoint(one_block), (queries.reshape(block_count, block_rows, queries.shape[1]), positions.reshape(block_count, block_rows), segment_flat.reshape(block_count, block_rows)))
    return stacked.reshape(length, queries.shape[1])

def reference(inputs, cotangent, segment_ids, bucket_table, gain_attention, query_weight, key_weight, value_weight, output_weight, bucket_bias, gain_feedforward, gate_weight, up_weight, down_weight):
    length = inputs.shape[0] * inputs.shape[1]
    width_all = inputs.shape[2]
    flat_inputs = inputs.reshape(length, width_all).astype(jnp.float32)
    flat_cot = cotangent.reshape(length, width_all).astype(jnp.float32)
    segment_flat = segment_ids.reshape(length).astype(jnp.int32)
    onehot = (bucket_table[:, None] == jnp.arange(NB, dtype=jnp.int32)[None, :]).astype(jnp.float32)

    def forward(hidden_in, gain_first, query_mat, key_mat, value_mat, output_mat, bucket_mat, gain_second, gate_mat, up_mat, down_mat):
        normed = low(root_norm(hidden_in, gain_first))
        queries = low(low_back(jnp.dot(normed, query_mat.T, precision=HIGHEST)))
        keys_all = low(low_back(jnp.dot(normed, key_mat.T, precision=HIGHEST)))
        values_all = low(low_back(jnp.dot(normed, value_mat.T, precision=HIGHEST)))
        bias_table = jnp.dot(onehot, bucket_mat, precision=HIGHEST)
        attended = low(low_back(attention(queries, keys_all, values_all, bias_table, segment_flat)))
        middle = hidden_in + low_back(jnp.dot(attended, output_mat, precision=HIGHEST))
        normed_mid = low(root_norm(middle, gain_second))
        gate_act = low_back(jnp.dot(normed_mid, gate_mat.T, precision=HIGHEST))
        up_act = low_back(jnp.dot(normed_mid, up_mat.T, precision=HIGHEST))
        hidden = low(jax.nn.gelu(gate_act, approximate=True) * up_act)
        return middle + low_back(jnp.dot(hidden, down_mat, precision=HIGHEST))
    result, pullback = jax.vjp(forward, flat_inputs, gain_attention.astype(jnp.float32), query_weight.astype(jnp.float32), key_weight.astype(jnp.float32), value_weight.astype(jnp.float32), output_weight.astype(jnp.float32), bucket_bias.astype(jnp.float32), gain_feedforward.astype(jnp.float32), gate_weight.astype(jnp.float32), up_weight.astype(jnp.float32), down_weight.astype(jnp.float32))
    gradients = pullback(flat_cot)
    layer_out = result.astype(jnp.bfloat16).reshape(inputs.shape)
    grad_inputs = gradients[0].astype(jnp.bfloat16).reshape(inputs.shape)
    return (layer_out, grad_inputs, gradients[1], gradients[2], gradients[3], gradients[4], gradients[5], gradients[6], gradients[7], gradients[8], gradients[9], gradients[10])
```

```python
import functools

import jax
import jax.numpy as jnp
from jax import lax
from jax.experimental import pallas as pl
from jax.experimental.pallas import tpu as pltpu
from jax.sharding import Mesh
from jax.sharding import PartitionSpec as P

EPSILON = 1e-06
NEGATIVE = -1e30
HIGHEST = lax.Precision.HIGHEST
F32 = jnp.float32
BF16 = jnp.bfloat16
VMEM_LIMIT = 60 * 1024 * 1024
SQUARE = ("x", "y")
HEADS_GROUP = ("x", "c", "y", "r")
UNITS_GROUP = ("c", "z", "r")
EVERY = ("x", "c", "z", "y", "r")


def norm_scale(values):
    return lax.rsqrt(jnp.mean(values * values, axis=-1, keepdims=True) + EPSILON)


def norm_back(values, scaling, gain_vec, upstream):
    inner_sum = jnp.mean(values * gain_vec * upstream, axis=-1, keepdims=True)
    return scaling * gain_vec * upstream - values * scaling * scaling * scaling * inner_sum


def nt(left, right):
    return lax.dot_general(left, right, (((1,), (1,)), ((), ())), preferred_element_type=F32)


def nn(left, right):
    return lax.dot_general(left, right, (((1,), (0,)), ((), ())), preferred_element_type=F32)


def tn(left, right):
    return lax.dot_general(left, right, (((0,), (0,)), ((), ())), preferred_element_type=F32)


def swap(value, axis, mask):
    size = lax.axis_size(axis)
    return lax.ppermute(value, axis, [(at, at ^ mask) for at in range(size)])


def from_group(value, axis):
    return [value] + [swap(value, axis, mask) for mask in (1, 2, 3)]


def to_group(values, axis):
    return [values[0]] + [swap(values[mask], axis, mask) for mask in (1, 2, 3)]


def kernel_call(body, out_shapes, inputs, scratch=(), scalars=1):
    in_specs = [pl.BlockSpec(memory_space=pltpu.SMEM)] * scalars
    in_specs += [pl.BlockSpec(memory_space=pltpu.VMEM)] * (len(inputs) - scalars)
    return pl.pallas_call(
        body,
        out_shape=out_shapes,
        in_specs=in_specs,
        out_specs=jax.tree.map(lambda _: pl.BlockSpec(memory_space=pltpu.VMEM), out_shapes),
        scratch_shapes=list(scratch),
        compiler_params=pltpu.CompilerParams(vmem_limit_bytes=VMEM_LIMIT),
    )(*inputs)


def shape(dims, dtype):
    return jax.ShapeDtypeStruct(dims, dtype)


def qkv_body(hd, coords, *refs):
    blocks, (wa, wb), pieces = refs[:4], refs[4:6], refs[6:10]
    rows_all, weights = refs[10:12]
    x_at, c_at, y_at = coords[0], coords[1], coords[3]
    tokens, width = blocks[0].shape
    for at in range(4):
        rows_all[at * tokens : (at + 1) * tokens, :] = blocks[at][...]
    for dest in range(4):
        base = pl.multiple_of((x_at ^ (dest >> 1)) * hd, hd)
        other = (y_at ^ (dest & 1)) ^ c_at

        def put(source, base=base, dest=dest):
            for kind, start in ((0, 8 * hd + dest * hd), (1, dest * 2 * hd), (2, dest * 2 * hd + hd)):
                weights[start : start + hd, :] = source[
                    pl.ds(base, hd), kind * width : (kind + 1) * width
                ]

        pl.when(other == 0)(functools.partial(put, wa))
        pl.when(other == 1)(functools.partial(put, wb))
    normed = rows_all[...]
    pairs = nt(normed, weights[0 : 8 * hd, :]).astype(BF16)
    queries = nt(weights[8 * hd : 12 * hd, :], normed).astype(BF16)
    for dest in range(4):
        pieces[dest][0 : 4 * tokens, :] = pairs[:, dest * 2 * hd : (dest + 1) * 2 * hd]
        for at in range(4):
            pieces[dest][4 * tokens + at * hd : 4 * tokens + (at + 1) * hd, :] = queries[
                dest * hd : (dest + 1) * hd, at * tokens : (at + 1) * tokens
            ]


def bias_tiles(hvec, tokens):
    tiles = {}
    for at, diff in enumerate((-1, 0, 1)):
        spread = jnp.broadcast_to(hvec[at : at + 1, :], (tokens, 2 * tokens))
        tiles[diff] = pltpu.roll(spread, 0, 1, stride=1, stride_axis=0)[:, :tokens]
    return tiles


def fill_bias(hvec_ref, bias, c_at, tokens):
    tiles = bias_tiles(hvec_ref[...], tokens)
    zero = jnp.zeros((tokens, tokens), F32)
    for rows in range(8):
        for half in range(2):
            diff = rows - 4 - 2 * half
            even, odd = tiles.get(diff, zero), tiles.get(diff - 1, zero)
            bias[rows * tokens : (rows + 1) * tokens, half * tokens : (half + 1) * tokens] = (
                jnp.where(c_at == 0, even, odd)
            )


def allowed_mask(cuts, run, c_at, tokens):
    rows, cols = 4 * tokens, 2 * tokens
    key_at = lax.broadcasted_iota(jnp.int32, (rows, cols), 0)
    query_at = lax.broadcasted_iota(jnp.int32, (rows, cols), 1)
    key_window = key_at >= 2 * tokens
    query_window = query_at >= tokens
    key_in = jnp.where(key_window, key_at - 2 * tokens, key_at)
    query_in = jnp.where(query_window, query_at - tokens, query_at) + c_at * tokens
    cut = jnp.where(query_window, cuts[2 * run + 1], cuts[2 * run])
    inside = (key_in < cut) | (query_in >= cut)
    before = jnp.logical_and(jnp.logical_not(key_window), query_window)
    same = key_window == query_window
    return before | (same & inside)


def fold_rows(values, how):
    rows, cols = values.shape
    return how(values.reshape(rows // 8, 8, cols), axis=0)


def attend_body(tokens, hd, repeat, coords, cuts, hvec, *refs):
    pieces, own, other = refs[:4], refs[4:8], refs[8:12]
    if repeat == 1:
        pieces = refs[:4]
        own, other, refs = refs[:4], refs[4:8], refs[8:]
    else:
        refs = refs[12:]
    out, out_near, lse, attended, keys, keys_t, queries, scores, bias = refs
    x_at, c_at, z_at, y_at, r_at = (coords[at] for at in range(5))
    block = 4 * tokens
    for dest in range(4):
        x_from, y_from = x_at ^ (dest >> 1), y_at ^ (dest & 1)
        for at in range(4):
            place = (z_at ^ at) * 2 + y_from
            for rep in range(repeat):
                run = place * repeat + rep
                base = run * block + x_from * 2 * tokens
                source = slice(rep * block + at * tokens, rep * block + (at + 1) * tokens)
                keys[pl.ds(pl.multiple_of(base + c_at * tokens, tokens), tokens), :] = own[dest][
                    source, :
                ]
                keys[pl.ds(pl.multiple_of(base + (1 - c_at) * tokens, tokens), tokens), :] = other[
                    dest
                ][source, :]
            start = block + at * hd
            queries[place, :, pl.ds(pl.multiple_of(x_from * tokens, tokens), tokens)] = pieces[
                dest
            ][start : start + hd, :]
    fill_bias(hvec, bias, c_at, tokens)

    def turn(at, carry):
        rows = pl.ds(pl.multiple_of(at * block, block), block)
        keys_t[at] = keys[rows, :].T
        return carry

    lax.fori_loop(0, keys.shape[0] // block, turn, 0)

    def one_block(place, carry):
        run = place * repeat + r_at
        query_t = queries[place]
        query_pad = jnp.concatenate([query_t, jnp.zeros_like(query_t)], axis=0)

        def raw(at):
            return nn(keys[pl.ds(pl.multiple_of(at * block, block), block), :], query_pad)

        def far(at, peak):
            values = raw(at)
            scores[at] = values
            return jnp.maximum(peak, fold_rows(values, jnp.max))

        def near(at, peak):
            values = raw(at) + bias[0:block, :]
            scores[at] = values
            return jnp.maximum(peak, fold_rows(values, jnp.max))

        last = raw(run) + bias[block:, :]
        last = jnp.where(allowed_mask(cuts, run, c_at, tokens), last, NEGATIVE)
        scores[run] = last
        peak = fold_rows(last, jnp.max)
        peak = lax.fori_loop(jnp.maximum(run - 1, 0), run, near, peak)
        peak = lax.fori_loop(0, run - 1, far, peak)
        top = jnp.max(peak, axis=0, keepdims=True)

        def mix(at, state):
            total, mixed = state
            weights = jnp.exp(scores[at] - top)
            total = total + fold_rows(weights, jnp.sum)
            mixed = mixed + nn(keys_t[at, hd:, :], weights.astype(BF16))
            return total, mixed

        start = (jnp.zeros((8, 2 * tokens), F32), jnp.zeros((hd, 2 * tokens), F32))
        total, mixed = lax.fori_loop(0, run + 1, mix, start)
        total = jnp.sum(total, axis=0, keepdims=True)
        mixed = mixed / total
        attended[place] = mixed
        lse[place] = jnp.broadcast_to(top + jnp.log(total), (8, 2 * tokens))
        low = mixed.astype(BF16)
        z_to, y_to = place >> 1, place & 1
        for half in range(2):
            part = low[:, half * tokens : (half + 1) * tokens]
            out[half * 8 + y_to * 4 + z_to] = part
            out_near[((x_at ^ half) * 2 + (y_to ^ y_at)) * 4 + (z_to ^ z_at)] = part
        return carry

    lax.fori_loop(0, queries.shape[0], one_block, 0)


def attend_back_body(tokens, hd, repeat, coords, cuts, hvec, *refs):
    arrived, queries, keys, keys_t, attended, lse = refs[:6]
    grad_own, grad_other, grad_q, table_out, far_out = refs[6:11]
    bias, grad_keys, table_acc = refs[11:]
    x_at, c_at, z_at, y_at, r_at = (coords[at] for at in range(5))
    block = 4 * tokens
    fill_bias(hvec, bias, c_at, tokens)
    grad_keys[...] = jnp.zeros_like(grad_keys)
    table_acc[...] = jnp.zeros_like(table_acc)
    far_out[...] = jnp.zeros_like(far_out)

    def one_block(place, carry):
        run = place * repeat + r_at
        z_to, y_to = place >> 1, place & 1
        query_t = queries[place]
        upstream_t = jnp.concatenate(
            [arrived[half * 8 + y_to * 4 + z_to] for half in range(2)], axis=1
        )
        zero = jnp.zeros_like(query_t)
        query_pad = jnp.concatenate([query_t, zero], axis=0)
        upstream_pad = jnp.concatenate([zero, upstream_t], axis=0)
        query_rows = query_pad.T
        upstream_rows = upstream_pad.T
        shift = lse[place][0:1, :]
        delta = jnp.sum(upstream_t.astype(F32) * attended[place], axis=0, keepdims=True)

        def finish(at, values, mask=None):
            rows = pl.ds(pl.multiple_of(at * block, block), block)
            probs = jnp.exp(values - shift)
            if mask is not None:
                probs = jnp.where(mask, probs, 0.0)
            grad_probs = nn(keys[rows, :], upstream_pad)
            grad_scores = probs * (grad_probs - delta)
            grad_low = grad_scores.astype(BF16)
            grad_keys[rows, :] += nn(grad_low, query_rows) + nn(probs.astype(BF16), upstream_rows)
            return grad_low, nn(keys_t[at, :hd, :], grad_low)

        def raw(at):
            return nn(keys[pl.ds(pl.multiple_of(at * block, block), block), :], query_pad)

        def far(at, grad_query):
            grad_low, step = finish(at, raw(at))
            far_out[...] += fold_rows(grad_low.astype(F32), jnp.sum)
            return grad_query + step

        def near(at, grad_query):
            grad_low, step = finish(at, raw(at) + bias[0:block, :])
            table_acc[0:block, :] += grad_low.astype(F32)
            return grad_query + step

        grad_low, grad_query = finish(
            run, raw(run) + bias[block:, :], allowed_mask(cuts, run, c_at, tokens)
        )
        table_acc[block:, :] += grad_low.astype(F32)
        grad_query = lax.fori_loop(jnp.maximum(run - 1, 0), run, near, grad_query)
        grad_query = lax.fori_loop(0, run - 1, far, grad_query)
        low = grad_query.astype(BF16)
        for half in range(2):
            part = low[:, half * tokens : (half + 1) * tokens]
            grad_q[((x_at ^ half) * 2 + (y_to ^ y_at)) * 4 + (z_to ^ z_at)] = part
        return carry

    lax.fori_loop(0, queries.shape[0], one_block, 0)

    for dest in range(4):
        x_from, y_from = x_at ^ (dest >> 1), y_at ^ (dest & 1)
        for at in range(4):
            place = (z_at ^ at) * 2 + y_from
            for rep in range(repeat):
                base = (place * repeat + rep) * block + x_from * 2 * tokens
                start = (dest * repeat + rep) * block + at * tokens
                target = slice(start, start + tokens)
                grad_own[target, :] = grad_keys[
                    pl.ds(pl.multiple_of(base + c_at * tokens, tokens), tokens), :
                ]
                grad_other[target, :] = grad_keys[
                    pl.ds(pl.multiple_of(base + (1 - c_at) * tokens, tokens), tokens), :
                ].astype(BF16)

    def tile_at(rows, half):
        return table_acc[
            rows * tokens : (rows + 1) * tokens, half * tokens : (half + 1) * tokens
        ]

    spots = [(rows, half) for rows in range(8) for half in range(2)]
    flip = (
        lax.broadcasted_iota(jnp.int32, (tokens, tokens), 0)
        + lax.broadcasted_iota(jnp.int32, (tokens, tokens), 1)
        == tokens - 1
    ).astype(F32)
    far_even = jnp.zeros((tokens, tokens), F32)
    far_odd = jnp.zeros((tokens, tokens), F32)
    for rows, half in spots:
        diff = rows - 4 - 2 * half
        if diff <= -2:
            far_even += tile_at(rows, half)
        if diff - 1 <= -2:
            far_odd += tile_at(rows, half)
    extra = fold_rows(jnp.where(c_at == 0, far_even, far_odd), jnp.sum)
    far_out[:, :tokens] += extra
    table_out[...] = jnp.zeros_like(table_out)
    for index, diff in enumerate((-1, 0, 1)):
        even = sum(tile_at(rows, half) for rows, half in spots if rows - 4 - 2 * half == diff)
        odd = sum(tile_at(rows, half) for rows, half in spots if rows - 5 - 2 * half == diff)
        tile = jnp.where(c_at == 0, even, odd)
        turned = jnp.dot(flip, tile, precision=HIGHEST, preferred_element_type=F32)
        wide = jnp.concatenate([turned, jnp.zeros_like(turned)], axis=1)
        wide = pltpu.roll(wide, tokens + 1, 1, stride=1, stride_axis=0)
        table_out[index : index + 1, :] = jnp.sum(wide, axis=0, keepdims=True)


def project_back_body(hd, coords, *refs):
    pieces, (rows_all, weights, gain), outs = refs[:4], refs[4:7], refs[7:11]
    weight_out, gain_out = refs[11:13]
    pairs, pairs_t, queries, queries_t = refs[13:]
    x_at, c_at, y_at = coords[0], coords[1], coords[3]
    tokens, width = outs[0].shape
    for dest in range(4):
        lanes = slice(dest * 2 * hd, (dest + 1) * 2 * hd)
        part = pieces[dest][0 : 4 * tokens, :]
        pairs[:, lanes] = part
        pairs_t[lanes, :] = part.T
        for at in range(4):
            queries_t[dest * hd : (dest + 1) * hd, at * tokens : (at + 1) * tokens] = pieces[dest][
                4 * tokens + at * hd : 4 * tokens + (at + 1) * hd, :
            ]
    queries[...] = queries_t[...].T
    normed = rows_all[...]
    grad = nn(pairs[...], weights[0 : 8 * hd, :]) + nn(queries[...], weights[8 * hd :, :])
    unit = normed.astype(F32) / gain[...]
    gain_out[...] = fold_rows(grad * unit, jnp.sum)
    for at in range(4):
        outs[at][...] = grad[at * tokens : (at + 1) * tokens, :].astype(BF16)
    pair_rows = nn(pairs_t[...], normed).astype(BF16)
    query_rows = nn(queries_t[...], normed).astype(BF16)
    for dest in range(4):
        head = (x_at ^ (dest >> 1)) * 2 + (y_at ^ (dest & 1))
        rows = pl.ds(pl.multiple_of(head * hd, hd), hd)
        weight_out[rows, 0:width] = query_rows[dest * hd : (dest + 1) * hd, :]
        start = dest * 2 * hd
        weight_out[rows, width : 2 * width] = pair_rows[start : start + hd, :]
        weight_out[rows, 2 * width : 3 * width] = pair_rows[start + hd : start + 2 * hd, :]


def output_back_body(hd, coords, *refs):
    pieces, blocks, weight_out, rows_all, features = refs[:4], refs[4:8], refs[8], refs[9], refs[10]
    x_at, y_at = coords[0], coords[3]
    tokens = blocks[0].shape[0]
    for at in range(4):
        rows_all[at * tokens : (at + 1) * tokens, :] = blocks[at][...]
    for dest in range(4):
        for at in range(4):
            features[dest * hd : (dest + 1) * hd, at * tokens : (at + 1) * tokens] = pieces[dest][at]
    result = nn(features[...], rows_all[...]).astype(BF16)
    for dest in range(4):
        head = (x_at ^ (dest >> 1)) * 2 + (y_at ^ (dest & 1))
        weight_out[pl.ds(pl.multiple_of(head * hd, hd), hd), :] = result[
            dest * hd : (dest + 1) * hd, :
        ]


def gated(gate_act, up_act):
    return jax.nn.gelu(gate_act, approximate=True) * up_act


def body(
    inputs,
    cotangent,
    segment_ids,
    bucket_table,
    gain_attention,
    query_weight,
    key_weight,
    value_weight,
    output_weight,
    bucket_bias,
    gain_feedforward,
    gate_weight,
    up_weight,
    down_weight,
):
    tokens, width = inputs.shape[1:]
    repeat = lax.axis_size("r")
    x_at, c_at, z_at, y_at, r_at = (lax.axis_index(name) for name in EVERY)
    coords = jnp.stack([x_at, c_at, z_at, y_at, r_at]).astype(jnp.int32)
    bucket_count, head_count = bucket_bias.shape
    hd = width // head_count
    block = 4 * tokens
    length = segment_ids.size
    reach = (bucket_table.shape[0] - 1) // 2
    assert reach == tokens and lax.axis_size("x") == lax.axis_size("c") == 2

    hidden_in = inputs[0].astype(F32)
    cot_own = cotangent[0]
    scale_first = norm_scale(hidden_in)
    normed = (hidden_in * scale_first * gain_attention).astype(BF16)
    normed_parts = from_group(normed, "z")

    joined = jnp.concatenate([query_weight, key_weight, value_weight, output_weight], axis=1)
    head_rows = lax.all_gather(joined, ("x", "y", "r"), axis=0, tiled=True)
    head_rows_other = swap(head_rows, "c", 1)
    out_z = lax.all_gather(head_rows[:, 3 * width :], "z", axis=0, tiled=False)
    out_z_other = swap(out_z, "c", 1)
    out_first = jnp.where(c_at == 0, out_z, out_z_other).reshape(4, 2, hd, width)
    out_second = jnp.where(c_at == 0, out_z_other, out_z).reshape(4, 2, hd, width)
    out_full = jnp.stack([out_first, out_second]).transpose(2, 0, 1, 3, 4).reshape(width, width)
    units = jnp.concatenate([gate_weight, up_weight, down_weight], axis=1)
    unit_rows = lax.all_gather(units, UNITS_GROUP, axis=0, tiled=True)
    gate_piece, up_piece, down_piece = (
        unit_rows[:, at * width : (at + 1) * width] for at in range(3)
    )
    cot_all = jnp.concatenate(from_group(cot_own, SQUARE), axis=0)

    windows = segment_ids.reshape(-1, 2 * tokens)
    cuts = jnp.sum((windows < windows[:, -1:]).astype(jnp.int32), axis=1)
    turned = bucket_table[::-1]
    low_half, high_half = turned[reach : 2 * reach], turned[:reach]
    spots = jnp.concatenate(
        [
            jnp.broadcast_to(bucket_table[:1], (reach,)),
            low_half,
            low_half,
            high_half,
            high_half,
            jnp.broadcast_to(bucket_table[2 * reach :], (reach,)),
        ]
    )
    buckets = jnp.arange(bucket_count, dtype=jnp.int32)
    onehot = (spots[:, None] == buckets[None, :]).astype(F32)
    far_onehot = (bucket_table[0] == buckets).astype(F32)
    head_at = (x_at * 2 + y_at) * 4 + z_at
    bias_col = lax.dynamic_slice_in_dim(bucket_bias, head_at, 1, 1)[:, 0]
    diag = jnp.dot(onehot, bias_col, precision=HIGHEST) - jnp.sum(far_onehot * bias_col)
    hvec = jnp.pad(diag.reshape(3, 2 * reach), ((0, 5), (0, 0)))

    made = kernel_call(
        functools.partial(qkv_body, hd),
        [shape((block + 4 * hd, 2 * hd), BF16)] * 4
        + [shape((block, width), BF16), shape((12 * hd, width), BF16)],
        [coords, *normed_parts, head_rows[:, : 3 * width], head_rows_other[:, : 3 * width]],
    )
    pieces, (normed_all, group_weights) = made[:4], made[4:]
    pieces = to_group(pieces, SQUARE)
    own = [piece[:block] for piece in pieces]
    other = swap(jnp.concatenate(own, axis=0), "c", 1)
    other = [other[at * block : (at + 1) * block] for at in range(4)]
    if repeat == 1:
        arrays = [*pieces, *other]
    else:
        own = [lax.all_gather(part, "r", axis=0, tiled=True) for part in own]
        other = [lax.all_gather(part, "r", axis=0, tiled=True) for part in other]
        arrays = [*pieces, *own, *other]
    places = 8
    out_t, out_near, lse, attended, keys, keys_t, queries = kernel_call(
        functools.partial(attend_body, tokens, hd, repeat),
        [
            shape((16, hd, tokens), BF16),
            shape((16, hd, tokens), BF16),
            shape((places, 8, 2 * tokens), F32),
            shape((places, hd, 2 * tokens), F32),
            shape((length, 2 * hd), BF16),
            shape((length // block, 2 * hd, block), BF16),
            shape((places, hd, 2 * tokens), BF16),
        ],
        [coords, cuts, hvec, *arrays],
        [
            pltpu.VMEM((length // block, block, 2 * tokens), F32),
            pltpu.VMEM((2 * block, 2 * tokens), F32),
        ],
        scalars=2,
    )
    arrived = lax.all_to_all(out_t, ("x", "y", "z"), split_axis=0, concat_axis=0, tiled=True)
    near = to_group(
        [out_near[4 * at : 4 * at + 4].reshape(4 * hd, tokens) for at in range(4)], SQUARE
    )

    middle = hidden_in + tn(arrived.reshape(width, tokens), out_full)
    scale_second = norm_scale(middle)
    normed_mid = (middle * scale_second * gain_feedforward).astype(BF16)
    mid_all = jnp.concatenate(from_group(normed_mid, SQUARE), axis=0)

    gate_act = nt(mid_all, gate_piece)
    up_act = nt(mid_all, up_piece)
    hidden_val, pullback = jax.vjp(gated, gate_act, up_act)
    hidden = hidden_val.astype(BF16)
    grad_gate, grad_up = pullback(nt(cot_all, down_piece))
    gate_low, up_low = grad_gate.astype(BF16), grad_up.astype(BF16)
    grad_norm = (nn(gate_low, gate_piece) + nn(up_low, up_piece)).astype(BF16)
    grad_parts = to_group(
        [grad_norm[at * tokens : (at + 1) * tokens] for at in range(4)], SQUARE
    )
    grad_norm_mid = sum(part.astype(F32) for part in grad_parts)
    feed = nn(hidden, down_piece).astype(BF16)
    feed_parts = to_group([feed[at * tokens : (at + 1) * tokens] for at in range(4)], SQUARE)
    layer_out = (middle + sum(part.astype(F32) for part in feed_parts)).astype(BF16)

    grad_middle = cot_own.astype(F32) + norm_back(
        middle, scale_second, gain_feedforward, grad_norm_mid
    )
    gain_second_term = jnp.sum(grad_norm_mid * middle * scale_second, axis=0)
    grad_mid_low = grad_middle.astype(BF16)
    grad_attended = nt(out_full, grad_mid_low).astype(BF16)
    grad_arrived = lax.all_to_all(
        grad_attended.reshape(16, hd, tokens),
        ("x", "y", "z"),
        split_axis=0,
        concat_axis=0,
        tiled=True,
    )
    unit_grads = jnp.concatenate(
        [tn(gate_low, mid_all), tn(up_low, mid_all), tn(hidden, cot_all)], axis=1
    ).astype(BF16)
    unit_grads = lax.psum_scatter(unit_grads, UNITS_GROUP, scatter_dimension=0, tiled=True)

    grad_own, grad_other, grad_q, table_out, far_out = kernel_call(
        functools.partial(attend_back_body, tokens, hd, repeat),
        [
            shape((4 * repeat * block, 2 * hd), F32),
            shape((4 * repeat * block, 2 * hd), BF16),
            shape((16, hd, tokens), BF16),
            shape((8, 2 * tokens), F32),
            shape((8, 2 * tokens), F32),
        ],
        [coords, cuts, hvec, grad_arrived, queries, keys, keys_t, attended, lse],
        [
            pltpu.VMEM((2 * block, 2 * tokens), F32),
            pltpu.VMEM((length, 2 * hd), F32),
            pltpu.VMEM((2 * block, 2 * tokens), F32),
        ],
        scalars=2,
    )
    grad_pairs = (grad_own + swap(grad_other, "c", 1).astype(F32)).astype(BF16)
    grad_pairs = [
        grad_pairs[at * repeat * block : (at + 1) * repeat * block] for at in range(4)
    ]
    if repeat > 1:
        grad_pairs = [
            lax.psum_scatter(part, "r", scatter_dimension=0, tiled=True) for part in grad_pairs
        ]
    grad_pieces = [
        jnp.concatenate([grad_pairs[at], grad_q[4 * at : 4 * at + 4].reshape(4 * hd, tokens)])
        for at in range(4)
    ]
    grad_pieces = to_group(grad_pieces, SQUARE)

    made = kernel_call(
        functools.partial(project_back_body, hd),
        [shape((tokens, width), BF16)] * 4
        + [shape((4 * hd, 3 * width), BF16), shape((8, width), F32)],
        [coords, *grad_pieces, normed_all, group_weights, gain_attention.reshape(1, width)],
        [
            pltpu.VMEM((block, 8 * hd), BF16),
            pltpu.VMEM((8 * hd, block), BF16),
            pltpu.VMEM((block, 4 * hd), BF16),
            pltpu.VMEM((4 * hd, block), BF16),
        ],
    )
    normed_grads, head_grads, gain_first_rows = made[:4], made[4], made[5]
    grad_normed = sum(part.astype(F32) for part in to_group(normed_grads, "z"))
    grad_inputs = (
        grad_middle + norm_back(hidden_in, scale_first, gain_attention, grad_normed)
    ).astype(BF16)

    mid_parts = from_group(grad_mid_low, "z")
    out_grads = kernel_call(
        functools.partial(output_back_body, hd),
        shape((4 * hd, width), BF16),
        [coords, *[part.reshape(4, hd, tokens) for part in near], *mid_parts],
        [pltpu.VMEM((block, width), BF16), pltpu.VMEM((4 * hd, block), BF16)],
    )
    out_grads = lax.psum_scatter(out_grads, HEADS_GROUP, scatter_dimension=0, tiled=True)
    head_grads = lax.psum_scatter(head_grads, HEADS_GROUP, scatter_dimension=0, tiled=True)

    bucket_grad = jnp.dot(table_out[:3].reshape(1, -1), onehot, precision=HIGHEST)[0]
    bucket_grad = bucket_grad + far_onehot * jnp.sum(far_out)
    head_mark = (jnp.arange(head_count) == head_at).astype(F32)
    bias_term = bucket_grad[:, None] * head_mark[None, :]
    gain_first_grad, gain_second_grad, bias_grad = lax.psum(
        (jnp.sum(gain_first_rows, axis=0), gain_second_term, bias_term), EVERY
    )
    head_grads = head_grads.astype(F32)
    unit_grads = unit_grads.astype(F32)
    return (
        layer_out[None],
        grad_inputs[None],
        gain_first_grad,
        head_grads[:, :width],
        head_grads[:, width : 2 * width],
        head_grads[:, 2 * width :],
        out_grads.astype(F32),
        bias_grad,
        gain_second_grad,
        unit_grads[:, :width],
        unit_grads[:, width : 2 * width],
        unit_grads[:, 2 * width :],
    )


def solution(mesh):
    owners, runs = mesh.shape["ulysses"], mesh.shape["blk"]
    fine = Mesh(mesh.devices.reshape(2, owners // 2, 4, 2, runs // 8), EVERY)
    tokens = P(("z", "y", "r"), ("x", "c"), None)
    rows = P(EVERY, None)
    return jax.shard_map(
        body,
        mesh=fine,
        in_specs=(tokens, tokens) + (P(),) * 3 + (rows,) * 4 + (P(),) * 2 + (rows,) * 3,
        out_specs=(tokens, tokens, P()) + (rows,) * 4 + (P(),) * 2 + (rows,) * 3,
        check_vma=False,
    )
```

```python
import functools

import jax
import jax.numpy as jnp
from jax import lax
from jax.experimental import pallas as pl
from jax.experimental.pallas import tpu as pltpu
from jax.sharding import Mesh
from jax.sharding import PartitionSpec as P

EPSILON = 1e-06
NEGATIVE = -1e30
HIGHEST = lax.Precision.HIGHEST
F32 = jnp.float32
BF16 = jnp.bfloat16
VMEM_LIMIT = 60 * 1024 * 1024
SQUARE = ("x", "y")
UNITS_GROUP = ("z", "c", "r")
EVERY = ("x", "c", "z", "y", "r")


def norm_scale(values):
    return lax.rsqrt(jnp.mean(values * values, axis=-1, keepdims=True) + EPSILON)


def norm_back(values, scaling, gain_vec, upstream):
    inner_sum = jnp.mean(values * gain_vec * upstream, axis=-1, keepdims=True)
    return scaling * gain_vec * upstream - values * scaling * scaling * scaling * inner_sum


def nt(left, right):
    return lax.dot_general(left, right, (((1,), (1,)), ((), ())), preferred_element_type=F32)


def nn(left, right):
    return lax.dot_general(left, right, (((1,), (0,)), ((), ())), preferred_element_type=F32)


def tn(left, right):
    return lax.dot_general(left, right, (((0,), (0,)), ((), ())), preferred_element_type=F32)


def swap(value, axis, mask):
    size = lax.axis_size(axis)
    return lax.ppermute(value, axis, [(at, at ^ mask) for at in range(size)])


def from_group(value, axis):
    return [value] + [swap(value, axis, mask) for mask in (1, 2, 3)]


def to_group(values, axis):
    return [values[0]] + [swap(values[mask], axis, mask) for mask in (1, 2, 3)]


def sum_everywhere(value, axis):
    first, second, third, fourth = from_group(value, axis)
    return (first + second) + (third + fourth)


def kernel_call(body, out_shapes, inputs, scratch=(), scalars=1, micros=4):
    in_specs = [pl.BlockSpec(memory_space=pltpu.SMEM)] * scalars
    in_specs += [pl.BlockSpec(memory_space=pltpu.VMEM)] * (len(inputs) - scalars)
    return pl.pallas_call(
        body,
        out_shape=out_shapes,
        in_specs=in_specs,
        out_specs=jax.tree.map(lambda _: pl.BlockSpec(memory_space=pltpu.VMEM), out_shapes),
        scratch_shapes=list(scratch),
        compiler_params=pltpu.CompilerParams(vmem_limit_bytes=VMEM_LIMIT),
        cost_estimate=pl.CostEstimate(
            flops=int(micros * 1.15e9), bytes_accessed=1 << 20, transcendentals=0
        ),
    )(*inputs)


def shape(dims, dtype):
    return jax.ShapeDtypeStruct(dims, dtype)


def qkv_body(hd, coords, *refs):
    blocks, parts, other_rows, pieces = refs[:4], refs[4:8], refs[8], refs[9:13]
    rows_all, weights = refs[13:15]
    c_at, y_at = coords[1], coords[3]
    tokens, width = blocks[0].shape
    half = hd // 2
    for at in range(4):
        rows_all[at * tokens : (at + 1) * tokens, :] = blocks[at][...]
    for core in range(2):
        for dest in range(4):
            column = y_at ^ c_at ^ core
            place = (dest >> 1) * 2 + column
            shift = pl.multiple_of((y_at ^ (dest & 1)) * half, half)
            source = other_rows.at[dest * half : (dest + 1) * half] if core else parts[dest]
            for kind, first, step in ((0, 8 * hd, hd), (1, 0, 2 * hd), (2, hd, 2 * hd)):
                start = pl.multiple_of(first + place * step + shift, half)
                weights[pl.ds(start, half), :] = source[:, kind * width : (kind + 1) * width]
    normed = rows_all[...]
    pairs = nt(normed, weights[0 : 8 * hd, :]).astype(BF16)
    queries = nt(weights[8 * hd : 12 * hd, :], normed).astype(BF16)
    for dest in range(4):
        pieces[dest][0 : 4 * tokens, :] = pairs[:, dest * 2 * hd : (dest + 1) * 2 * hd]
        for at in range(4):
            pieces[dest][4 * tokens + at * hd : 4 * tokens + (at + 1) * hd, :] = queries[
                dest * hd : (dest + 1) * hd, at * tokens : (at + 1) * tokens
            ]


def bias_tiles(hvec, tokens):
    tiles = {}
    for at, diff in enumerate((-1, 0, 1)):
        spread = jnp.broadcast_to(hvec[at : at + 1, :], (tokens, 2 * tokens))
        tiles[diff] = pltpu.roll(spread, 0, 1, stride=1, stride_axis=0)[:, :tokens]
    return tiles


def fill_bias(hvec_ref, bias, c_at, tokens):
    tiles = bias_tiles(hvec_ref[...], tokens)
    zero = jnp.zeros((tokens, tokens), F32)
    for rows in range(8):
        for half in range(2):
            diff = rows - 4 - 2 * half
            even, odd = tiles.get(diff, zero), tiles.get(diff - 1, zero)
            bias[rows * tokens : (rows + 1) * tokens, half * tokens : (half + 1) * tokens] = (
                jnp.where(c_at == 0, even, odd)
            )


def allowed_mask(cuts, run, c_at, tokens):
    rows, cols = 4 * tokens, 2 * tokens
    key_at = lax.broadcasted_iota(jnp.int32, (rows, cols), 0)
    query_at = lax.broadcasted_iota(jnp.int32, (rows, cols), 1)
    key_window = key_at >= 2 * tokens
    query_window = query_at >= tokens
    key_in = jnp.where(key_window, key_at - 2 * tokens, key_at)
    query_in = jnp.where(query_window, query_at - tokens, query_at) + c_at * tokens
    cut = jnp.where(query_window, cuts[2 * run + 1], cuts[2 * run])
    inside = (key_in < cut) | (query_in >= cut)
    before = jnp.logical_and(jnp.logical_not(key_window), query_window)
    same = key_window == query_window
    return before | (same & inside)


def fold_rows(values, how):
    rows, cols = values.shape
    return how(values.reshape(rows // 8, 8, cols), axis=0)


def attend_body(tokens, hd, repeat, coords, cuts, hvec, *refs):
    pieces, own, other = refs[:4], refs[4:8], refs[8:12]
    if repeat == 1:
        pieces = refs[:4]
        own, other, refs = refs[:4], refs[4:8], refs[8:]
    else:
        refs = refs[12:]
    out, lse, attended, keys, keys_t, queries, scores, bias = refs
    x_at, c_at, z_at, y_at, r_at = (coords[at] for at in range(5))
    block = 4 * tokens
    for dest in range(4):
        x_from, y_from = x_at ^ (dest >> 1), y_at ^ (dest & 1)
        for at in range(4):
            place = (z_at ^ at) * 2 + y_from
            for rep in range(repeat):
                run = place * repeat + rep
                base = run * block + x_from * 2 * tokens
                source = slice(rep * block + at * tokens, rep * block + (at + 1) * tokens)
                keys[pl.ds(pl.multiple_of(base + c_at * tokens, tokens), tokens), :] = own[dest][
                    source, :
                ]
                keys[pl.ds(pl.multiple_of(base + (1 - c_at) * tokens, tokens), tokens), :] = other[
                    dest
                ][source, :]
            start = block + at * hd
            queries[place, :, pl.ds(pl.multiple_of(x_from * tokens, tokens), tokens)] = pieces[
                dest
            ][start : start + hd, :]
    fill_bias(hvec, bias, c_at, tokens)

    def turn(at, carry):
        rows = pl.ds(pl.multiple_of(at * block, block), block)
        keys_t[at] = keys[rows, :].T
        return carry

    lax.fori_loop(0, keys.shape[0] // block, turn, 0)

    def one_block(place, carry):
        run = place * repeat + r_at
        query_t = queries[place]
        query_pad = jnp.concatenate([query_t, jnp.zeros_like(query_t)], axis=0)

        def raw(at):
            return nn(keys[pl.ds(pl.multiple_of(at * block, block), block), :], query_pad)

        def far(at, peak):
            values = raw(at)
            scores[at] = values
            return jnp.maximum(peak, fold_rows(values, jnp.max))

        def near(at, peak):
            values = raw(at) + bias[0:block, :]
            scores[at] = values
            return jnp.maximum(peak, fold_rows(values, jnp.max))

        last = raw(run) + bias[block:, :]
        last = jnp.where(allowed_mask(cuts, run, c_at, tokens), last, NEGATIVE)
        scores[run] = last
        peak = fold_rows(last, jnp.max)
        peak = lax.fori_loop(jnp.maximum(run - 1, 0), run, near, peak)
        peak = lax.fori_loop(0, run - 1, far, peak)
        top = jnp.max(peak, axis=0, keepdims=True)

        def mix(at, state):
            total, mixed = state
            weights = jnp.exp(scores[at] - top)
            total = total + fold_rows(weights, jnp.sum)
            mixed = mixed + nn(keys_t[at, hd:, :], weights.astype(BF16))
            return total, mixed

        start = (jnp.zeros((8, 2 * tokens), F32), jnp.zeros((hd, 2 * tokens), F32))
        total, mixed = lax.fori_loop(0, run + 1, mix, start)
        total = jnp.sum(total, axis=0, keepdims=True)
        mixed = mixed / total
        attended[place] = mixed
        lse[place] = jnp.broadcast_to(top + jnp.log(total), (8, 2 * tokens))
        low = mixed.astype(BF16)
        z_to, y_to = place >> 1, place & 1
        for half in range(2):
            part = low[:, half * tokens : (half + 1) * tokens]
            out[half * 8 + y_to * 4 + z_to] = part
        return carry

    lax.fori_loop(0, queries.shape[0], one_block, 0)


def attend_back_body(tokens, hd, repeat, coords, cuts, hvec, *refs):
    arrived, queries, keys, keys_t, attended, lse = refs[:6]
    grad_own, grad_other, grad_q, table_out, far_out = refs[6:11]
    bias, grad_keys, table_acc = refs[11:]
    x_at, c_at, z_at, y_at, r_at = (coords[at] for at in range(5))
    block = 4 * tokens
    fill_bias(hvec, bias, c_at, tokens)
    grad_keys[...] = jnp.zeros_like(grad_keys)
    table_acc[...] = jnp.zeros_like(table_acc)
    far_out[...] = jnp.zeros_like(far_out)

    def one_block(place, carry):
        run = place * repeat + r_at
        z_to, y_to = place >> 1, place & 1
        query_t = queries[place]
        upstream_t = jnp.concatenate(
            [arrived[half * 8 + y_to * 4 + z_to] for half in range(2)], axis=1
        )
        zero = jnp.zeros_like(query_t)
        query_pad = jnp.concatenate([query_t, zero], axis=0)
        upstream_pad = jnp.concatenate([zero, upstream_t], axis=0)
        query_rows = query_pad.T
        upstream_rows = upstream_pad.T
        shift = lse[place][0:1, :]
        delta = jnp.sum(upstream_t.astype(F32) * attended[place], axis=0, keepdims=True)

        def finish(at, values, mask=None):
            rows = pl.ds(pl.multiple_of(at * block, block), block)
            probs = jnp.exp(values - shift)
            if mask is not None:
                probs = jnp.where(mask, probs, 0.0)
            grad_probs = nn(keys[rows, :], upstream_pad)
            grad_scores = probs * (grad_probs - delta)
            grad_low = grad_scores.astype(BF16)
            grad_keys[rows, :] += nn(grad_low, query_rows) + nn(probs.astype(BF16), upstream_rows)
            return grad_low, nn(keys_t[at, :hd, :], grad_low)

        def raw(at):
            return nn(keys[pl.ds(pl.multiple_of(at * block, block), block), :], query_pad)

        def far(at, grad_query):
            grad_low, step = finish(at, raw(at))
            far_out[...] += fold_rows(grad_low.astype(F32), jnp.sum)
            return grad_query + step

        def near(at, grad_query):
            grad_low, step = finish(at, raw(at) + bias[0:block, :])
            table_acc[0:block, :] += grad_low.astype(F32)
            return grad_query + step

        grad_low, grad_query = finish(
            run, raw(run) + bias[block:, :], allowed_mask(cuts, run, c_at, tokens)
        )
        table_acc[block:, :] += grad_low.astype(F32)
        grad_query = lax.fori_loop(jnp.maximum(run - 1, 0), run, near, grad_query)
        grad_query = lax.fori_loop(0, run - 1, far, grad_query)
        low = grad_query.astype(BF16)
        for half in range(2):
            part = low[:, half * tokens : (half + 1) * tokens]
            grad_q[((x_at ^ half) * 2 + (y_to ^ y_at)) * 4 + (z_to ^ z_at)] = part
        return carry

    lax.fori_loop(0, queries.shape[0], one_block, 0)

    for dest in range(4):
        x_from, y_from = x_at ^ (dest >> 1), y_at ^ (dest & 1)
        for at in range(4):
            place = (z_at ^ at) * 2 + y_from
            for rep in range(repeat):
                base = (place * repeat + rep) * block + x_from * 2 * tokens
                start = (dest * repeat + rep) * block + at * tokens
                target = slice(start, start + tokens)
                grad_own[target, :] = grad_keys[
                    pl.ds(pl.multiple_of(base + c_at * tokens, tokens), tokens), :
                ]
                grad_other[target, :] = grad_keys[
                    pl.ds(pl.multiple_of(base + (1 - c_at) * tokens, tokens), tokens), :
                ].astype(BF16)

    def tile_at(rows, half):
        return table_acc[
            rows * tokens : (rows + 1) * tokens, half * tokens : (half + 1) * tokens
        ]

    spots = [(rows, half) for rows in range(8) for half in range(2)]
    flip = (
        lax.broadcasted_iota(jnp.int32, (tokens, tokens), 0)
        + lax.broadcasted_iota(jnp.int32, (tokens, tokens), 1)
        == tokens - 1
    ).astype(F32)
    far_even = jnp.zeros((tokens, tokens), F32)
    far_odd = jnp.zeros((tokens, tokens), F32)
    for rows, half in spots:
        diff = rows - 4 - 2 * half
        if diff <= -2:
            far_even += tile_at(rows, half)
        if diff - 1 <= -2:
            far_odd += tile_at(rows, half)
    extra = fold_rows(jnp.where(c_at == 0, far_even, far_odd), jnp.sum)
    far_out[:, :tokens] += extra
    table_out[...] = jnp.zeros_like(table_out)
    for index, diff in enumerate((-1, 0, 1)):
        even = sum(tile_at(rows, half) for rows, half in spots if rows - 4 - 2 * half == diff)
        odd = sum(tile_at(rows, half) for rows, half in spots if rows - 5 - 2 * half == diff)
        tile = jnp.where(c_at == 0, even, odd)
        turned = jnp.dot(flip, tile, precision=HIGHEST, preferred_element_type=F32)
        wide = jnp.concatenate([turned, jnp.zeros_like(turned)], axis=1)
        wide = pltpu.roll(wide, tokens + 1, 1, stride=1, stride_axis=0)
        table_out[index : index + 1, :] = jnp.sum(wide, axis=0, keepdims=True)


def project_back_body(hd, coords, *refs):
    pieces, (rows_all, weights, gain), out = refs[:4], refs[4:7], refs[7]
    gain_out, pairs_t, queries_t, pairs, queries = refs[8:]
    tokens, width = out.shape[1:]
    z_at = coords[2]
    for dest in range(4):
        lanes = slice(dest * 2 * hd, (dest + 1) * 2 * hd)
        part = pieces[dest][0 : 4 * tokens, :]
        pairs[:, lanes] = part
        pairs_t[lanes, :] = part.T
        for at in range(4):
            queries_t[dest * hd : (dest + 1) * hd, at * tokens : (at + 1) * tokens] = pieces[dest][
                4 * tokens + at * hd : 4 * tokens + (at + 1) * hd, :
            ]
    queries[...] = queries_t[...].T
    grad = nn(pairs[...], weights[0 : 8 * hd, :]) + nn(queries[...], weights[8 * hd :, :])
    unit = rows_all[...].astype(F32) / gain[...]
    gain_out[...] = fold_rows(grad * unit, jnp.sum)
    for at in range(4):
        out[z_at ^ at] = grad[at * tokens : (at + 1) * tokens, :].astype(BF16)


def head_grads_body(hd, coords, pairs_t, queries_t, rows_all, keep, send):
    c_at, y_at = coords[1], coords[3]
    width = rows_all.shape[1]
    half = hd // 2
    normed = rows_all[...]
    pair_rows = nn(pairs_t[...], normed).astype(BF16)
    query_rows = nn(queries_t[...], normed).astype(BF16)
    for dest in range(4):
        other = (y_at ^ (dest & 1)) ^ c_at

        def put(target, dest=dest):
            for part in range(2):
                place = (dest >> 1) * 2 + (y_at ^ part)
                for kind, rows, first in (
                    (0, query_rows, dest * hd),
                    (1, pair_rows, dest * 2 * hd),
                    (2, pair_rows, dest * 2 * hd + hd),
                ):
                    first += part * half
                    target[place, :, kind * width : (kind + 1) * width] = rows[
                        first : first + half, :
                    ]

        pl.when(other == 0)(functools.partial(put, keep))
        pl.when(other == 1)(functools.partial(put, send))


def output_body(hd, coords, *refs):
    arrived, own_in, gain, parts, middle_out, normed_out, weights, features = refs
    x_at, y_at = coords[0], coords[3]
    half, tokens = hd // 2, arrived.shape[1]
    for z_of in range(4):
        for c_of in range(2):
            for dest in range(4):
                head = ((x_at ^ (dest >> 1)) * 2 + c_of) * 4 + z_of
                start = pl.multiple_of(head * hd + (y_at ^ (dest & 1)) * half, half)
                weights[pl.ds(start, half), :] = parts[
                    z_of * 2 + c_of, dest * half : (dest + 1) * half, :
                ]
    for dest in range(4):
        for z_of in range(4):
            for c_of in range(2):
                head = ((x_at ^ (dest >> 1)) * 2 + c_of) * 4 + z_of
                start = pl.multiple_of(head * hd + (y_at ^ (dest & 1)) * half, half)
                lanes = slice((z_of * 2 + c_of) * tokens, (z_of * 2 + c_of + 1) * tokens)
                features[dest, :, lanes] = arrived[pl.ds(start, half), :]
    middle = own_in[...].astype(F32) + nn(arrived[...].T, weights[...])
    middle_out[...] = middle
    normed_out[...] = (middle * norm_scale(middle) * gain[...]).astype(BF16)


def finish_body(*refs):
    parts, own_in, grad_middle, gain, out = refs
    values = own_in[...].astype(F32)
    grad = sum(parts[at].astype(F32) for at in range(4))
    out[...] = (
        grad_middle[...] + norm_back(values, norm_scale(values), gain[...], grad)
    ).astype(BF16)


def gated(gate_act, up_act):
    return jax.nn.gelu(gate_act, approximate=True) * up_act


def body(
    inputs,
    cotangent,
    segment_ids,
    bucket_table,
    gain_attention,
    query_weight,
    key_weight,
    value_weight,
    output_weight,
    bucket_bias,
    gain_feedforward,
    gate_weight,
    up_weight,
    down_weight,
):
    tokens, width = inputs.shape[1:]
    repeat = lax.axis_size("r")
    x_at, c_at, z_at, y_at, r_at = (lax.axis_index(name) for name in EVERY)
    coords = jnp.stack([x_at, c_at, z_at, y_at, r_at]).astype(jnp.int32)
    bucket_count, head_count = bucket_bias.shape
    hd = width // head_count
    block = 4 * tokens
    length = segment_ids.size
    reach = (bucket_table.shape[0] - 1) // 2
    assert reach == tokens and lax.axis_size("x") == lax.axis_size("c") == 2

    hidden_in = inputs[0].astype(F32)
    cot_own = cotangent[0]
    scale_first = norm_scale(hidden_in)
    normed = (hidden_in * scale_first * gain_attention).astype(BF16)
    normed_parts = from_group(normed, "z")

    joined = jnp.concatenate([query_weight, key_weight, value_weight, output_weight], axis=1)
    if repeat > 1:
        joined = lax.all_gather(joined, "r", axis=0, tiled=True)
    head_rows = from_group(joined, SQUARE)
    other_rows = swap(jnp.concatenate([part[:, : 3 * width] for part in head_rows]), "c", 1)
    out_rows = jnp.concatenate([part[:, 3 * width :] for part in head_rows])
    units = jnp.concatenate([gate_weight, up_weight, down_weight], axis=1)
    unit_rows = lax.all_gather(units, UNITS_GROUP, axis=0, tiled=True)
    gate_piece, up_piece, down_piece = (
        unit_rows[:, at * width : (at + 1) * width] for at in range(3)
    )

    windows = segment_ids.reshape(-1, 2 * tokens)
    cuts = jnp.sum((windows < windows[:, -1:]).astype(jnp.int32), axis=1)
    turned = bucket_table[::-1]
    low_half, high_half = turned[reach : 2 * reach], turned[:reach]
    spots = jnp.concatenate(
        [
            jnp.broadcast_to(bucket_table[:1], (reach,)),
            low_half,
            low_half,
            high_half,
            high_half,
            jnp.broadcast_to(bucket_table[2 * reach :], (reach,)),
        ]
    )
    buckets = jnp.arange(bucket_count, dtype=jnp.int32)
    onehot = (spots[:, None] == buckets[None, :]).astype(F32)
    far_onehot = (bucket_table[0] == buckets).astype(F32)
    head_at = (x_at * 2 + y_at) * 4 + z_at
    bias_col = lax.dynamic_slice_in_dim(bucket_bias, head_at, 1, 1)[:, 0]
    diag = jnp.dot(onehot, bias_col, precision=HIGHEST) - jnp.sum(far_onehot * bias_col)
    hvec = jnp.pad(diag.reshape(3, 2 * reach), ((0, 5), (0, 0)))

    normed_parts, hvec, cuts, coords, out_rows = lax.optimization_barrier(
        (normed_parts, hvec, cuts, coords, out_rows)
    )
    made = kernel_call(
        functools.partial(qkv_body, hd),
        [shape((block + 4 * hd, 2 * hd), BF16)] * 4
        + [shape((block, width), BF16), shape((12 * hd, width), BF16)],
        [coords, *normed_parts, *head_rows, other_rows],
    )
    pieces, (normed_all, group_weights) = made[:4], made[4:]
    pieces = to_group(pieces, SQUARE)

    out_all = lax.all_gather(out_rows, ("z", "c"), axis=0, tiled=False)
    own = [piece[:block] for piece in pieces]
    other = swap(jnp.concatenate(own, axis=0), "c", 1)
    other = [other[at * block : (at + 1) * block] for at in range(4)]
    if repeat == 1:
        arrays = [*pieces, *other]
    else:
        own = [lax.all_gather(part, "r", axis=0, tiled=True) for part in own]
        other = [lax.all_gather(part, "r", axis=0, tiled=True) for part in other]
        arrays = [*pieces, *own, *other]
    places = 8
    out_t, lse, attended, keys, keys_t, queries = kernel_call(
        functools.partial(attend_body, tokens, hd, repeat),
        [
            shape((16, hd, tokens), BF16),
            shape((places, 8, 2 * tokens), F32),
            shape((places, hd, 2 * tokens), F32),
            shape((length, 2 * hd), BF16),
            shape((length // block, 2 * hd, block), BF16),
            shape((places, hd, 2 * tokens), BF16),
        ],
        [coords, cuts, hvec, *arrays],
        [
            pltpu.VMEM((length // block, block, 2 * tokens), F32),
            pltpu.VMEM((2 * block, 2 * tokens), F32),
        ],
        scalars=2,
        micros=20,
    )
    cot_sent, _ = lax.optimization_barrier((cot_own, other))
    cot_parts, out_t = lax.optimization_barrier((from_group(cot_sent, SQUARE), out_t))
    cot_all = jnp.concatenate(cot_parts, axis=0)
    arrived = lax.all_to_all(out_t, ("x", "y", "z"), split_axis=0, concat_axis=0, tiled=True)

    middle, normed_mid, out_full, features = kernel_call(
        functools.partial(output_body, hd),
        [
            shape((tokens, width), F32),
            shape((tokens, width), BF16),
            shape((width, width), BF16),
            shape((4, hd // 2, 8 * tokens), BF16),
        ],
        [
            coords,
            arrived.reshape(width, tokens),
            inputs[0],
            gain_feedforward.reshape(1, width),
            out_all,
        ],
    )
    scale_second = norm_scale(middle)
    mid_all = jnp.concatenate(from_group(normed_mid, SQUARE), axis=0)

    gate_act = nt(mid_all, gate_piece)
    up_act = nt(mid_all, up_piece)
    hidden_val, pullback = jax.vjp(gated, gate_act, up_act)
    hidden = hidden_val.astype(BF16)
    grad_gate, grad_up = pullback(nt(cot_all, down_piece))
    gate_low, up_low = grad_gate.astype(BF16), grad_up.astype(BF16)
    grad_norm = (nn(gate_low, gate_piece) + nn(up_low, up_piece)).astype(BF16)
    grad_parts = to_group(
        [grad_norm[at * tokens : (at + 1) * tokens] for at in range(4)], SQUARE
    )
    unit_grads = jnp.concatenate(
        [tn(gate_low, mid_all), tn(up_low, mid_all), tn(hidden, cot_all)], axis=1
    ).astype(BF16)
    feed = nn(hidden, down_piece).astype(BF16)
    grad_parts, unit_grads, feed = lax.optimization_barrier((grad_parts, unit_grads, feed))
    grad_norm_mid = sum(part.astype(F32) for part in grad_parts)

    grad_middle = cot_own.astype(F32) + norm_back(
        middle, scale_second, gain_feedforward, grad_norm_mid
    )
    gain_second_term = jnp.sum(grad_norm_mid * middle * scale_second, axis=0)
    grad_mid_low = grad_middle.astype(BF16)
    grad_attended = nt(out_full, grad_mid_low).astype(BF16)
    grad_arrived = lax.all_to_all(
        grad_attended.reshape(16, hd, tokens),
        ("x", "y", "z"),
        split_axis=0,
        concat_axis=0,
        tiled=True,
    )
    grad_arrived, grad_mid_low, unit_grads = lax.optimization_barrier(
        (grad_arrived, grad_mid_low, unit_grads)
    )
    grad_units = lax.psum_scatter(unit_grads, UNITS_GROUP, scatter_dimension=0, tiled=True)
    mixed = to_group(
        [
            jnp.concatenate(
                [
                    feed[at * tokens : (at + 1) * tokens],
                    grad_mid_low,
                    features[at],
                ]
            )
            for at in range(4)
        ],
        SQUARE,
    )

    grad_own, grad_other, grad_q, table_out, far_out = kernel_call(
        functools.partial(attend_back_body, tokens, hd, repeat),
        [
            shape((4 * repeat * block, 2 * hd), F32),
            shape((4 * repeat * block, 2 * hd), BF16),
            shape((16, hd, tokens), BF16),
            shape((8, 2 * tokens), F32),
            shape((8, 2 * tokens), F32),
        ],
        [coords, cuts, hvec, grad_arrived, queries, keys, keys_t, attended, lse],
        [
            pltpu.VMEM((2 * block, 2 * tokens), F32),
            pltpu.VMEM((length, 2 * hd), F32),
            pltpu.VMEM((2 * block, 2 * tokens), F32),
        ],
        scalars=2,
        micros=20,
    )
    mixed, grad_own = lax.optimization_barrier((mixed, grad_own))
    grad_pairs = (grad_own + swap(grad_other, "c", 1).astype(F32)).astype(BF16)
    grad_pairs = [
        grad_pairs[at * repeat * block : (at + 1) * repeat * block] for at in range(4)
    ]
    if repeat > 1:
        grad_pairs = [
            lax.psum_scatter(part, "r", scatter_dimension=0, tiled=True) for part in grad_pairs
        ]
    grad_pieces = [
        jnp.concatenate([grad_pairs[at], grad_q[4 * at : 4 * at + 4].reshape(4 * hd, tokens)])
        for at in range(4)
    ]
    mixed, grad_pieces = lax.optimization_barrier((mixed, grad_pieces))
    grad_pieces = to_group(grad_pieces, SQUARE)

    made = kernel_call(
        functools.partial(project_back_body, hd),
        [
            shape((4, tokens, width), BF16),
            shape((8, width), F32),
            shape((8 * hd, block), BF16),
            shape((4 * hd, block), BF16),
        ],
        [coords, *grad_pieces, normed_all, group_weights, gain_attention.reshape(1, width)],
        [pltpu.VMEM((block, 8 * hd), BF16), pltpu.VMEM((block, 4 * hd), BF16)],
    )
    normed_grads, gain_first_rows, pairs_t, queries_t = made
    normed_grads = lax.all_to_all(normed_grads, "z", split_axis=0, concat_axis=0, tiled=True)
    keep, send = kernel_call(
        functools.partial(head_grads_body, hd),
        [shape((4, hd // 2, 3 * width), BF16)] * 2,
        [coords, pairs_t, queries_t, normed_all],
    )
    layer_out = (middle + sum(part[:tokens].astype(F32) for part in mixed)).astype(BF16)
    grad_mid_all = jnp.concatenate([part[tokens : 2 * tokens] for part in mixed], axis=0)
    near = jnp.stack([part[2 * tokens :] for part in mixed]).reshape(4, hd // 2, 8, tokens)
    near = near.transpose(2, 1, 0, 3).reshape(4 * hd, block)
    out_grads = nn(near, grad_mid_all).astype(BF16)

    table_out, far_out, keep, send, grad_units, out_grads = lax.optimization_barrier(
        (table_out, far_out, keep, send, grad_units, out_grads)
    )
    out_grads = lax.psum_scatter(out_grads, UNITS_GROUP, scatter_dimension=0, tiled=True)
    head_grads = (keep.astype(F32) + swap(send, "c", 1).astype(F32)).astype(BF16)
    bucket_grad = jnp.dot(table_out[:3].reshape(1, -1), onehot, precision=HIGHEST)[0]
    bucket_grad = bucket_grad + far_onehot * jnp.sum(far_out)
    head_mark = (jnp.arange(head_count) == head_at).astype(F32)
    bias_term = bucket_grad[:, None] * head_mark[None, :]
    sums = jnp.concatenate([jnp.sum(gain_first_rows, axis=0), gain_second_term, bias_term.ravel()])
    sums = sums + swap(sums, "c", 1)
    sums = sum_everywhere(sums, SQUARE)
    normed_grads, head_grads, sums = lax.optimization_barrier((normed_grads, head_grads, sums))
    sums = sum_everywhere(sums, "z")
    head_grads = to_group([head_grads[at] for at in range(4)], SQUARE)
    head_grads = sum(part.astype(F32) for part in head_grads)
    if repeat > 1:
        head_grads = lax.psum_scatter(
            head_grads.astype(BF16), "r", scatter_dimension=0, tiled=True
        ).astype(F32)

    if repeat > 1:
        sums = lax.psum(sums, "r")
    gain_first_grad, gain_second_grad = sums[:width], sums[width : 2 * width]
    bias_grad = sums[2 * width :].reshape(bucket_count, head_count)

    grad_inputs = kernel_call(
        finish_body,
        shape((tokens, width), BF16),
        [normed_grads, inputs[0], grad_middle, gain_attention.reshape(1, width)],
        scalars=0,
        micros=100,
    )
    unit_grads = grad_units.astype(F32)
    return (
        layer_out[None],
        grad_inputs[None],
        gain_first_grad,
        head_grads[:, :width],
        head_grads[:, width : 2 * width],
        head_grads[:, 2 * width :],
        out_grads.astype(F32),
        bias_grad,
        gain_second_grad,
        unit_grads[:, :width],
        unit_grads[:, width : 2 * width],
        unit_grads[:, 2 * width :],
    )


def solution(mesh):
    owners, runs = mesh.shape["ulysses"], mesh.shape["blk"]
    fine = Mesh(mesh.devices.reshape(2, owners // 2, 4, 2, runs // 8), EVERY)
    tokens = P(("z", "y", "r"), ("x", "c"), None)
    rows = P(EVERY, None)
    return jax.shard_map(
        body,
        mesh=fine,
        in_specs=(tokens, tokens) + (P(),) * 3 + (rows,) * 4 + (P(),) * 2 + (rows,) * 3,
        out_specs=(tokens, tokens, P()) + (rows,) * 4 + (P(),) * 2 + (rows,) * 3,
        check_vma=False,
    )
```

```python
import functools

import jax
import jax.numpy as jnp
from jax import lax
from jax.experimental import pallas as pl
from jax.experimental.pallas import tpu as pltpu
from jax.sharding import Mesh
from jax.sharding import PartitionSpec as P

EPSILON = 1e-06
NEGATIVE = -1e30
HIGHEST = lax.Precision.HIGHEST
F32 = jnp.float32
BF16 = jnp.bfloat16
VMEM_LIMIT = 60 * 1024 * 1024
SQUARE = ("x", "y")
UNITS_GROUP = ("z", "c", "r")
EVERY = ("x", "c", "z", "y", "r")


def norm_scale(values):
    return lax.rsqrt(jnp.mean(values * values, axis=-1, keepdims=True) + EPSILON)


def norm_back(values, scaling, gain_vec, upstream):
    inner_sum = jnp.mean(values * gain_vec * upstream, axis=-1, keepdims=True)
    return scaling * gain_vec * upstream - values * scaling * scaling * scaling * inner_sum


def nt(left, right):
    return lax.dot_general(left, right, (((1,), (1,)), ((), ())), preferred_element_type=F32)


def nn(left, right):
    return lax.dot_general(left, right, (((1,), (0,)), ((), ())), preferred_element_type=F32)


def tn(left, right):
    return lax.dot_general(left, right, (((0,), (0,)), ((), ())), preferred_element_type=F32)


def swap(value, axis, mask):
    size = lax.axis_size(axis)
    return lax.ppermute(value, axis, [(at, at ^ mask) for at in range(size)])


def from_group(value, axis):
    return [value] + [swap(value, axis, mask) for mask in (1, 2, 3)]


def to_group(values, axis):
    return [values[0]] + [swap(values[mask], axis, mask) for mask in (1, 2, 3)]


def sum_everywhere(value, axis):
    first, second, third, fourth = from_group(value, axis)
    return (first + second) + (third + fourth)


def sum_over_z(rows, values):
    width = rows.shape[-1]
    lines = -(-values.size // width)
    padded = jnp.pad(values, (0, lines * width - values.size)).reshape(lines, width)
    high = lax.reduce_precision(padded, 8, 7)
    extra = jnp.concatenate([high, padded - high]).astype(BF16)
    extra = jnp.pad(extra, ((0, -2 * lines % 8), (0, 0)))
    arrived = to_group([jnp.concatenate([rows[at], extra]) for at in range(4)], "z")
    arrived = [part.astype(F32) for part in arrived]
    count = rows.shape[1]
    tails = [part[count : count + lines] + part[count + lines : count + 2 * lines] for part in arrived]
    total = (tails[0] + tails[1]) + (tails[2] + tails[3])
    return sum(part[:count] for part in arrived), total.ravel()[: values.size]


def kernel_call(body, out_shapes, inputs, scratch=(), scalars=1, micros=4):
    in_specs = [pl.BlockSpec(memory_space=pltpu.SMEM)] * scalars
    in_specs += [pl.BlockSpec(memory_space=pltpu.VMEM)] * (len(inputs) - scalars)
    return pl.pallas_call(
        body,
        out_shape=out_shapes,
        in_specs=in_specs,
        out_specs=jax.tree.map(lambda _: pl.BlockSpec(memory_space=pltpu.VMEM), out_shapes),
        scratch_shapes=list(scratch),
        compiler_params=pltpu.CompilerParams(vmem_limit_bytes=VMEM_LIMIT),
        cost_estimate=pl.CostEstimate(
            flops=int(micros * 1.15e9), bytes_accessed=1 << 20, transcendentals=0
        ),
    )(*inputs)


def shape(dims, dtype):
    return jax.ShapeDtypeStruct(dims, dtype)


def qkv_body(hd, coords, *refs):
    blocks, parts, other_rows, pieces = refs[:4], refs[4:8], refs[8], refs[9:13]
    rows_all, weights = refs[13:15]
    c_at, y_at = coords[1], coords[3]
    tokens, width = blocks[0].shape
    half = hd // 2
    for at in range(4):
        rows_all[at * tokens : (at + 1) * tokens, :] = blocks[at][...]
    for core in range(2):
        for dest in range(4):
            column = y_at ^ c_at ^ core
            place = (dest >> 1) * 2 + column
            shift = pl.multiple_of((y_at ^ (dest & 1)) * half, half)
            source = other_rows.at[dest * half : (dest + 1) * half] if core else parts[dest]
            for kind, first, step in ((0, 8 * hd, hd), (1, 0, 2 * hd), (2, hd, 2 * hd)):
                start = pl.multiple_of(first + place * step + shift, half)
                weights[pl.ds(start, half), :] = source[:, kind * width : (kind + 1) * width]
    normed = rows_all[...]
    pairs = nt(normed, weights[0 : 8 * hd, :]).astype(BF16)
    queries = nt(weights[8 * hd : 12 * hd, :], normed).astype(BF16)
    for dest in range(4):
        pieces[dest][0 : 4 * tokens, :] = pairs[:, dest * 2 * hd : (dest + 1) * 2 * hd]
        for at in range(4):
            pieces[dest][4 * tokens + at * hd : 4 * tokens + (at + 1) * hd, :] = queries[
                dest * hd : (dest + 1) * hd, at * tokens : (at + 1) * tokens
            ]


def bias_tiles(hvec, tokens):
    tiles = {}
    for at, diff in enumerate((-1, 0, 1)):
        spread = jnp.broadcast_to(hvec[at : at + 1, :], (tokens, 2 * tokens))
        tiles[diff] = pltpu.roll(spread, 0, 1, stride=1, stride_axis=0)[:, :tokens]
    return tiles


def fill_bias(hvec_ref, bias, c_at, tokens):
    tiles = bias_tiles(hvec_ref[...], tokens)
    zero = jnp.zeros((tokens, tokens), F32)
    for rows in range(8):
        for half in range(2):
            diff = rows - 4 - 2 * half
            even, odd = tiles.get(diff, zero), tiles.get(diff - 1, zero)
            bias[rows * tokens : (rows + 1) * tokens, half * tokens : (half + 1) * tokens] = (
                jnp.where(c_at == 0, even, odd)
            )


def allowed_mask(cuts, run, c_at, tokens):
    rows, cols = 4 * tokens, 2 * tokens
    key_at = lax.broadcasted_iota(jnp.int32, (rows, cols), 0)
    query_at = lax.broadcasted_iota(jnp.int32, (rows, cols), 1)
    key_window = key_at >= 2 * tokens
    query_window = query_at >= tokens
    key_in = jnp.where(key_window, key_at - 2 * tokens, key_at)
    query_in = jnp.where(query_window, query_at - tokens, query_at) + c_at * tokens
    cut = jnp.where(query_window, cuts[2 * run + 1], cuts[2 * run])
    inside = (key_in < cut) | (query_in >= cut)
    before = jnp.logical_and(jnp.logical_not(key_window), query_window)
    same = key_window == query_window
    return before | (same & inside)


def sweep(first, last, step, carry):
    if isinstance(first, int) and isinstance(last, int):
        for at in range(first, last):
            carry = step(at, carry)
        return carry
    return lax.fori_loop(first, last, step, carry)


def each_run(places, repeat, r_at, step):
    if repeat == 1:
        for place in range(places):
            step(place, place)
    else:

        def one(place, carry):
            step(place, place * repeat + r_at)
            return carry

        lax.fori_loop(0, places, one, 0)


def at_least(value, bound):
    return max(value, bound) if isinstance(value, int) else jnp.maximum(value, bound)


def chunk(at, block):
    start = at * block
    return pl.ds(start if isinstance(at, int) else pl.multiple_of(start, block), block)


def fold_rows(values, how):
    rows, cols = values.shape
    return how(values.reshape(rows // 8, 8, cols), axis=0)


def attend_body(tokens, hd, repeat, coords, cuts, hvec, *refs):
    pieces, own, other = refs[:4], refs[4:8], refs[8:12]
    if repeat == 1:
        pieces = refs[:4]
        own, other, refs = refs[:4], refs[4:8], refs[8:]
    else:
        refs = refs[12:]
    out, lse, attended, keys, keys_t, queries, scores, bias = refs
    x_at, c_at, z_at, y_at, r_at = (coords[at] for at in range(5))
    block = 4 * tokens
    for dest in range(4):
        x_from, y_from = x_at ^ (dest >> 1), y_at ^ (dest & 1)
        for at in range(4):
            place = (z_at ^ at) * 2 + y_from
            for rep in range(repeat):
                run = place * repeat + rep
                base = run * block + x_from * 2 * tokens
                source = slice(rep * block + at * tokens, rep * block + (at + 1) * tokens)
                keys[pl.ds(pl.multiple_of(base + c_at * tokens, tokens), tokens), :] = own[dest][
                    source, :
                ]
                keys[pl.ds(pl.multiple_of(base + (1 - c_at) * tokens, tokens), tokens), :] = other[
                    dest
                ][source, :]
            start = block + at * hd
            queries[place, :, pl.ds(pl.multiple_of(x_from * tokens, tokens), tokens)] = pieces[
                dest
            ][start : start + hd, :]
    fill_bias(hvec, bias, c_at, tokens)

    def turn(at, carry):
        rows = pl.ds(pl.multiple_of(at * block, block), block)
        keys_t[at] = keys[rows, :].T
        return carry

    lax.fori_loop(0, keys.shape[0] // block, turn, 0)

    def one_block(place, run):
        query_t = queries[place]
        query_pad = jnp.concatenate([query_t, jnp.zeros_like(query_t)], axis=0)

        def raw(at):
            return nn(keys[chunk(at, block), :], query_pad)

        def far(at, peak):
            values = raw(at)
            scores[at] = values
            return jnp.maximum(peak, fold_rows(values, jnp.max))

        def near(at, peak):
            values = raw(at) + bias[0:block, :]
            scores[at] = values
            return jnp.maximum(peak, fold_rows(values, jnp.max))

        last = raw(run) + bias[block:, :]
        last = jnp.where(allowed_mask(cuts, run, c_at, tokens), last, NEGATIVE)
        scores[run] = last
        peak = fold_rows(last, jnp.max)
        peak = sweep(at_least(run - 1, 0), run, near, peak)
        peak = sweep(0, run - 1, far, peak)
        top = jnp.max(peak, axis=0, keepdims=True)

        def mix(at, state):
            total, mixed = state
            weights = jnp.exp(scores[at] - top)
            total = total + fold_rows(weights, jnp.sum)
            mixed = mixed + nn(keys_t[at, hd:, :], weights.astype(BF16))
            return total, mixed

        start = (jnp.zeros((8, 2 * tokens), F32), jnp.zeros((hd, 2 * tokens), F32))
        total, mixed = sweep(0, run + 1, mix, start)
        total = jnp.sum(total, axis=0, keepdims=True)
        mixed = mixed / total
        attended[place] = mixed
        lse[place] = jnp.broadcast_to(top + jnp.log(total), (8, 2 * tokens))
        low = mixed.astype(BF16)
        z_to, y_to = place >> 1, place & 1
        for half in range(2):
            part = low[:, half * tokens : (half + 1) * tokens]
            out[half * 8 + y_to * 4 + z_to] = part

    each_run(queries.shape[0], repeat, r_at, one_block)


def attend_back_body(tokens, hd, repeat, coords, cuts, hvec, *refs):
    arrived, queries, keys, keys_t, attended, lse = refs[:6]
    grad_own, grad_other, grad_q, table_out, far_out = refs[6:11]
    bias, grad_keys, table_acc = refs[11:]
    x_at, c_at, z_at, y_at, r_at = (coords[at] for at in range(5))
    block = 4 * tokens
    fill_bias(hvec, bias, c_at, tokens)
    grad_keys[...] = jnp.zeros_like(grad_keys)
    table_acc[...] = jnp.zeros_like(table_acc)
    far_out[...] = jnp.zeros_like(far_out)

    def one_block(place, run):
        z_to, y_to = place >> 1, place & 1
        query_t = queries[place]
        upstream_t = jnp.concatenate(
            [arrived[half * 8 + y_to * 4 + z_to] for half in range(2)], axis=1
        )
        zero = jnp.zeros_like(query_t)
        query_pad = jnp.concatenate([query_t, zero], axis=0)
        upstream_pad = jnp.concatenate([zero, upstream_t], axis=0)
        query_rows = query_pad.T
        upstream_rows = upstream_pad.T
        shift = lse[place][0:1, :]
        delta = jnp.sum(upstream_t.astype(F32) * attended[place], axis=0, keepdims=True)

        def finish(at, values, mask=None):
            rows = chunk(at, block)
            probs = jnp.exp(values - shift)
            if mask is not None:
                probs = jnp.where(mask, probs, 0.0)
            grad_probs = nn(keys[rows, :], upstream_pad)
            grad_scores = probs * (grad_probs - delta)
            grad_low = grad_scores.astype(BF16)
            grad_keys[rows, :] += nn(grad_low, query_rows) + nn(probs.astype(BF16), upstream_rows)
            return grad_low, nn(keys_t[at, :hd, :], grad_low)

        def raw(at):
            return nn(keys[chunk(at, block), :], query_pad)

        def far(at, grad_query):
            grad_low, step = finish(at, raw(at))
            far_out[...] += fold_rows(grad_low.astype(F32), jnp.sum)
            return grad_query + step

        def near(at, grad_query):
            grad_low, step = finish(at, raw(at) + bias[0:block, :])
            table_acc[0:block, :] += grad_low.astype(F32)
            return grad_query + step

        grad_low, grad_query = finish(
            run, raw(run) + bias[block:, :], allowed_mask(cuts, run, c_at, tokens)
        )
        table_acc[block:, :] += grad_low.astype(F32)
        grad_query = sweep(at_least(run - 1, 0), run, near, grad_query)
        grad_query = sweep(0, run - 1, far, grad_query)
        low = grad_query.astype(BF16)
        for half in range(2):
            part = low[:, half * tokens : (half + 1) * tokens]
            grad_q[((x_at ^ half) * 2 + (y_to ^ y_at)) * 4 + (z_to ^ z_at)] = part

    each_run(queries.shape[0], repeat, r_at, one_block)

    for dest in range(4):
        x_from, y_from = x_at ^ (dest >> 1), y_at ^ (dest & 1)
        for at in range(4):
            place = (z_at ^ at) * 2 + y_from
            for rep in range(repeat):
                base = (place * repeat + rep) * block + x_from * 2 * tokens
                start = (dest * repeat + rep) * block + at * tokens
                target = slice(start, start + tokens)
                grad_own[target, :] = grad_keys[
                    pl.ds(pl.multiple_of(base + c_at * tokens, tokens), tokens), :
                ]
                grad_other[target, :] = grad_keys[
                    pl.ds(pl.multiple_of(base + (1 - c_at) * tokens, tokens), tokens), :
                ].astype(BF16)

    def tile_at(rows, half):
        return table_acc[
            rows * tokens : (rows + 1) * tokens, half * tokens : (half + 1) * tokens
        ]

    spots = [(rows, half) for rows in range(8) for half in range(2)]
    flip = (
        lax.broadcasted_iota(jnp.int32, (tokens, tokens), 0)
        + lax.broadcasted_iota(jnp.int32, (tokens, tokens), 1)
        == tokens - 1
    ).astype(F32)
    far_even = jnp.zeros((tokens, tokens), F32)
    far_odd = jnp.zeros((tokens, tokens), F32)
    for rows, half in spots:
        diff = rows - 4 - 2 * half
        if diff <= -2:
            far_even += tile_at(rows, half)
        if diff - 1 <= -2:
            far_odd += tile_at(rows, half)
    extra = fold_rows(jnp.where(c_at == 0, far_even, far_odd), jnp.sum)
    far_out[:, :tokens] += extra
    table_out[...] = jnp.zeros_like(table_out)
    for index, diff in enumerate((-1, 0, 1)):
        even = sum(tile_at(rows, half) for rows, half in spots if rows - 4 - 2 * half == diff)
        odd = sum(tile_at(rows, half) for rows, half in spots if rows - 5 - 2 * half == diff)
        tile = jnp.where(c_at == 0, even, odd)
        turned = jnp.dot(flip, tile, precision=HIGHEST, preferred_element_type=F32)
        wide = jnp.concatenate([turned, jnp.zeros_like(turned)], axis=1)
        wide = pltpu.roll(wide, tokens + 1, 1, stride=1, stride_axis=0)
        table_out[index : index + 1, :] = jnp.sum(wide, axis=0, keepdims=True)


def project_back_body(hd, coords, *refs):
    pieces, (rows_all, weights, gain), out = refs[:4], refs[4:7], refs[7]
    gain_out, pairs_t, queries_t, pairs, queries = refs[8:]
    tokens, width = out.shape[1:]
    z_at = coords[2]
    for dest in range(4):
        lanes = slice(dest * 2 * hd, (dest + 1) * 2 * hd)
        part = pieces[dest][0 : 4 * tokens, :]
        pairs[:, lanes] = part
        pairs_t[lanes, :] = part.T
        for at in range(4):
            queries_t[dest * hd : (dest + 1) * hd, at * tokens : (at + 1) * tokens] = pieces[dest][
                4 * tokens + at * hd : 4 * tokens + (at + 1) * hd, :
            ]
    queries[...] = queries_t[...].T
    grad = nn(pairs[...], weights[0 : 8 * hd, :]) + nn(queries[...], weights[8 * hd :, :])
    unit = rows_all[...].astype(F32) / gain[...]
    gain_out[...] = fold_rows(grad * unit, jnp.sum)
    for at in range(4):
        out[z_at ^ at] = grad[at * tokens : (at + 1) * tokens, :].astype(BF16)


def head_grads_body(hd, coords, pairs_t, queries_t, rows_all, keep, send):
    c_at, y_at = coords[1], coords[3]
    width = rows_all.shape[1]
    half = hd // 2
    normed = rows_all[...]
    pair_rows = nn(pairs_t[...], normed).astype(BF16)
    query_rows = nn(queries_t[...], normed).astype(BF16)
    for dest in range(4):
        other = (y_at ^ (dest & 1)) ^ c_at

        def put(target, dest=dest):
            for part in range(2):
                place = (dest >> 1) * 2 + (y_at ^ part)
                for kind, rows, first in (
                    (0, query_rows, dest * hd),
                    (1, pair_rows, dest * 2 * hd),
                    (2, pair_rows, dest * 2 * hd + hd),
                ):
                    first += part * half
                    target[place, :, kind * width : (kind + 1) * width] = rows[
                        first : first + half, :
                    ]

        pl.when(other == 0)(functools.partial(put, keep))
        pl.when(other == 1)(functools.partial(put, send))


def output_body(hd, coords, *refs):
    arrived, own_in, gain, parts, middle_out, normed_out, weights, features = refs
    x_at, c_at, z_at, y_at = coords[0], coords[1], coords[2], coords[3]
    half, tokens = hd // 2, arrived.shape[1]
    for z_of in range(4):
        for c_of in range(2):
            for dest in range(4):
                head = ((x_at ^ (dest >> 1)) * 2 + c_of) * 4 + z_of
                start = pl.multiple_of(head * hd + (y_at ^ (dest & 1)) * half, half)
                weights[pl.ds(start, half), :] = parts[
                    z_of * 2 + c_of, dest * half : (dest + 1) * half, :
                ]
    for dest in range(4):
        for core in range(2):
            for near in range(4):
                head = ((x_at ^ (dest >> 1)) * 2 + (c_at ^ core)) * 4 + (z_at ^ near)
                start = pl.multiple_of(head * hd + (y_at ^ (dest & 1)) * half, half)
                lanes = slice((core * 4 + near) * tokens, (core * 4 + near + 1) * tokens)
                features[dest, :, lanes] = arrived[pl.ds(start, half), :]
    middle = own_in[...].astype(F32) + nn(arrived[...].T, weights[...])
    middle_out[...] = middle
    normed_out[...] = (middle * norm_scale(middle) * gain[...]).astype(BF16)


def finish_body(*refs):
    parts, own_in, grad_middle, gain, out = refs
    values = own_in[...].astype(F32)
    grad = sum(parts[at].astype(F32) for at in range(4))
    out[...] = (
        grad_middle[...] + norm_back(values, norm_scale(values), gain[...], grad)
    ).astype(BF16)


def gated(gate_act, up_act):
    return jax.nn.gelu(gate_act, approximate=True) * up_act


def body(
    inputs,
    cotangent,
    segment_ids,
    bucket_table,
    gain_attention,
    query_weight,
    key_weight,
    value_weight,
    output_weight,
    bucket_bias,
    gain_feedforward,
    gate_weight,
    up_weight,
    down_weight,
):
    tokens, width = inputs.shape[1:]
    repeat = lax.axis_size("r")
    x_at, c_at, z_at, y_at, r_at = (lax.axis_index(name) for name in EVERY)
    coords = jnp.stack([x_at, c_at, z_at, y_at, r_at]).astype(jnp.int32)
    bucket_count, head_count = bucket_bias.shape
    hd = width // head_count
    block = 4 * tokens
    length = segment_ids.size
    reach = (bucket_table.shape[0] - 1) // 2
    assert reach == tokens and lax.axis_size("x") == lax.axis_size("c") == 2

    hidden_in = inputs[0].astype(F32)
    cot_own = cotangent[0]
    scale_first = norm_scale(hidden_in)
    normed = (hidden_in * scale_first * gain_attention).astype(BF16)
    normed_parts = from_group(normed, "z")

    joined = jnp.concatenate([query_weight, key_weight, value_weight, output_weight], axis=1)
    if repeat > 1:
        joined = lax.all_gather(joined, "r", axis=0, tiled=True)
    head_rows = from_group(joined, SQUARE)
    other_rows = swap(jnp.concatenate([part[:, : 3 * width] for part in head_rows]), "c", 1)
    out_rows = jnp.concatenate([part[:, 3 * width :] for part in head_rows])
    units = jnp.concatenate([gate_weight, up_weight, down_weight], axis=1)
    unit_rows = lax.all_gather(units, UNITS_GROUP, axis=0, tiled=True)
    gate_piece, up_piece, down_piece = (
        unit_rows[:, at * width : (at + 1) * width] for at in range(3)
    )

    windows = segment_ids.reshape(-1, 2 * tokens)
    cuts = jnp.sum((windows < windows[:, -1:]).astype(jnp.int32), axis=1)
    turned = bucket_table[::-1]
    low_half, high_half = turned[reach : 2 * reach], turned[:reach]
    spots = jnp.concatenate(
        [
            jnp.broadcast_to(bucket_table[:1], (reach,)),
            low_half,
            low_half,
            high_half,
            high_half,
            jnp.broadcast_to(bucket_table[2 * reach :], (reach,)),
        ]
    )
    buckets = jnp.arange(bucket_count, dtype=jnp.int32)
    onehot = (spots[:, None] == buckets[None, :]).astype(F32)
    far_onehot = (bucket_table[0] == buckets).astype(F32)
    head_at = (x_at * 2 + y_at) * 4 + z_at
    bias_col = lax.dynamic_slice_in_dim(bucket_bias, head_at, 1, 1)[:, 0]
    diag = jnp.dot(onehot, bias_col, precision=HIGHEST) - jnp.sum(far_onehot * bias_col)
    hvec = jnp.pad(diag.reshape(3, 2 * reach), ((0, 5), (0, 0)))

    normed_parts, hvec, cuts, coords, out_rows = lax.optimization_barrier(
        (normed_parts, hvec, cuts, coords, out_rows)
    )
    made = kernel_call(
        functools.partial(qkv_body, hd),
        [shape((block + 4 * hd, 2 * hd), BF16)] * 4
        + [shape((block, width), BF16), shape((12 * hd, width), BF16)],
        [coords, *normed_parts, *head_rows, other_rows],
    )
    pieces, (normed_all, group_weights) = made[:4], made[4:]
    pieces = to_group(pieces, SQUARE)

    out_all = lax.all_gather(out_rows, ("z", "c"), axis=0, tiled=False)
    own = [piece[:block] for piece in pieces]
    other = swap(jnp.concatenate(own, axis=0), "c", 1)
    other = [other[at * block : (at + 1) * block] for at in range(4)]
    if repeat == 1:
        arrays = [*pieces, *other]
    else:
        own = [lax.all_gather(part, "r", axis=0, tiled=True) for part in own]
        other = [lax.all_gather(part, "r", axis=0, tiled=True) for part in other]
        arrays = [*pieces, *own, *other]
    places = 8
    out_t, lse, attended, keys, keys_t, queries = kernel_call(
        functools.partial(attend_body, tokens, hd, repeat),
        [
            shape((16, hd, tokens), BF16),
            shape((places, 8, 2 * tokens), F32),
            shape((places, hd, 2 * tokens), F32),
            shape((length, 2 * hd), BF16),
            shape((length // block, 2 * hd, block), BF16),
            shape((places, hd, 2 * tokens), BF16),
        ],
        [coords, cuts, hvec, *arrays],
        [
            pltpu.VMEM((length // block, block, 2 * tokens), F32),
            pltpu.VMEM((2 * block, 2 * tokens), F32),
        ],
        scalars=2,
        micros=20,
    )
    cot_sent, _ = lax.optimization_barrier((cot_own, other))
    cot_parts, out_t = lax.optimization_barrier((from_group(cot_sent, SQUARE), out_t))
    cot_all = jnp.concatenate(cot_parts, axis=0)
    arrived = lax.all_to_all(out_t, ("x", "y", "z"), split_axis=0, concat_axis=0, tiled=True)

    middle, normed_mid, out_full, features = kernel_call(
        functools.partial(output_body, hd),
        [
            shape((tokens, width), F32),
            shape((tokens, width), BF16),
            shape((width, width), BF16),
            shape((4, hd // 2, 8 * tokens), BF16),
        ],
        [
            coords,
            arrived.reshape(width, tokens),
            inputs[0],
            gain_feedforward.reshape(1, width),
            out_all,
        ],
    )
    scale_second = norm_scale(middle)
    mid_all = jnp.concatenate(from_group(normed_mid, SQUARE), axis=0)

    gate_act = nt(mid_all, gate_piece)
    up_act = nt(mid_all, up_piece)
    hidden_val, pullback = jax.vjp(gated, gate_act, up_act)
    hidden = hidden_val.astype(BF16)
    grad_gate, grad_up = pullback(nt(cot_all, down_piece))
    gate_low, up_low = grad_gate.astype(BF16), grad_up.astype(BF16)
    grad_norm = (nn(gate_low, gate_piece) + nn(up_low, up_piece)).astype(BF16)
    grad_parts = to_group(
        [grad_norm[at * tokens : (at + 1) * tokens] for at in range(4)], SQUARE
    )
    unit_grads = jnp.concatenate(
        [tn(gate_low, mid_all), tn(up_low, mid_all), tn(hidden, cot_all)], axis=1
    ).astype(BF16)
    feed = nn(hidden, down_piece).astype(BF16)
    grad_parts, unit_grads, feed = lax.optimization_barrier((grad_parts, unit_grads, feed))
    grad_norm_mid = sum(part.astype(F32) for part in grad_parts)

    grad_middle = cot_own.astype(F32) + norm_back(
        middle, scale_second, gain_feedforward, grad_norm_mid
    )
    gain_second_term = jnp.sum(grad_norm_mid * middle * scale_second, axis=0)
    grad_mid_low = grad_middle.astype(BF16)
    grad_attended = nt(out_full, grad_mid_low).astype(BF16)
    grad_arrived = lax.all_to_all(
        grad_attended.reshape(16, hd, tokens),
        ("x", "y", "z"),
        split_axis=0,
        concat_axis=0,
        tiled=True,
    )
    grad_arrived, grad_mid_low, unit_grads = lax.optimization_barrier(
        (grad_arrived, grad_mid_low, unit_grads)
    )
    grad_units = lax.psum_scatter(unit_grads, UNITS_GROUP, scatter_dimension=0, tiled=True)
    mixed = to_group(
        [
            jnp.concatenate(
                [
                    feed[at * tokens : (at + 1) * tokens],
                    grad_mid_low,
                    features[at],
                ]
            )
            for at in range(4)
        ],
        SQUARE,
    )

    grad_own, grad_other, grad_q, table_out, far_out = kernel_call(
        functools.partial(attend_back_body, tokens, hd, repeat),
        [
            shape((4 * repeat * block, 2 * hd), F32),
            shape((4 * repeat * block, 2 * hd), BF16),
            shape((16, hd, tokens), BF16),
            shape((8, 2 * tokens), F32),
            shape((8, 2 * tokens), F32),
        ],
        [coords, cuts, hvec, grad_arrived, queries, keys, keys_t, attended, lse],
        [
            pltpu.VMEM((2 * block, 2 * tokens), F32),
            pltpu.VMEM((length, 2 * hd), F32),
            pltpu.VMEM((2 * block, 2 * tokens), F32),
        ],
        scalars=2,
        micros=20,
    )
    mixed, grad_own = lax.optimization_barrier((mixed, grad_own))
    grad_pairs = (grad_own + swap(grad_other, "c", 1).astype(F32)).astype(BF16)
    grad_pairs = [
        grad_pairs[at * repeat * block : (at + 1) * repeat * block] for at in range(4)
    ]
    if repeat > 1:
        grad_pairs = [
            lax.psum_scatter(part, "r", scatter_dimension=0, tiled=True) for part in grad_pairs
        ]
    grad_pieces = [
        jnp.concatenate([grad_pairs[at], grad_q[4 * at : 4 * at + 4].reshape(4 * hd, tokens)])
        for at in range(4)
    ]
    mixed, grad_pieces = lax.optimization_barrier((mixed, grad_pieces))
    grad_pieces = to_group(grad_pieces, SQUARE)

    made = kernel_call(
        functools.partial(project_back_body, hd),
        [
            shape((4, tokens, width), BF16),
            shape((8, width), F32),
            shape((8 * hd, block), BF16),
            shape((4 * hd, block), BF16),
        ],
        [coords, *grad_pieces, normed_all, group_weights, gain_attention.reshape(1, width)],
        [pltpu.VMEM((block, 8 * hd), BF16), pltpu.VMEM((block, 4 * hd), BF16)],
    )
    normed_grads, gain_first_rows, pairs_t, queries_t = made
    normed_grads = lax.all_to_all(normed_grads, "z", split_axis=0, concat_axis=0, tiled=True)
    keep, send = kernel_call(
        functools.partial(head_grads_body, hd),
        [shape((4, hd // 2, 3 * width), BF16)] * 2,
        [coords, pairs_t, queries_t, normed_all],
    )
    layer_out = (middle + sum(part[:tokens].astype(F32) for part in mixed)).astype(BF16)
    grad_mid_all = jnp.concatenate([part[tokens : 2 * tokens] for part in mixed], axis=0)
    near = jnp.stack([part[2 * tokens :] for part in mixed]).reshape(4, hd // 2, 8, tokens)
    near = near.transpose(2, 1, 0, 3).reshape(4 * hd, block)
    out_grads = nn(near, grad_mid_all).astype(BF16)

    table_out, far_out, keep, send, grad_units, out_grads = lax.optimization_barrier(
        (table_out, far_out, keep, send, grad_units, out_grads)
    )
    out_grads = out_grads.reshape(2, 4, hd // 2, width)
    out_grads = (out_grads[0].astype(F32) + swap(out_grads[1], "c", 1).astype(F32)).astype(BF16)
    head_grads = (keep.astype(F32) + swap(send, "c", 1).astype(F32)).astype(BF16)
    bucket_grad = jnp.dot(table_out[:3].reshape(1, -1), onehot, precision=HIGHEST)[0]
    bucket_grad = bucket_grad + far_onehot * jnp.sum(far_out)
    head_mark = (jnp.arange(head_count) == head_at).astype(F32)
    bias_term = bucket_grad[:, None] * head_mark[None, :]
    sums = jnp.concatenate([jnp.sum(gain_first_rows, axis=0), gain_second_term, bias_term.ravel()])
    sums = sums + swap(sums, "c", 1)
    sums = sum_everywhere(sums, SQUARE)
    head_grads = to_group([head_grads[at] for at in range(4)], SQUARE)
    normed_grads, head_grads, sums, out_grads = lax.optimization_barrier(
        (normed_grads, head_grads, sums, out_grads)
    )
    out_grads, sums = sum_over_z(out_grads, sums)
    head_grads = sum(part.astype(F32) for part in head_grads)
    if repeat > 1:
        sums = lax.psum(sums, "r")
        out_grads = lax.psum_scatter(
            out_grads.astype(BF16), "r", scatter_dimension=0, tiled=True
        ).astype(F32)
        head_grads = lax.psum_scatter(
            head_grads.astype(BF16), "r", scatter_dimension=0, tiled=True
        ).astype(F32)
    gain_first_grad, gain_second_grad = sums[:width], sums[width : 2 * width]
    bias_grad = sums[2 * width :].reshape(bucket_count, head_count)

    grad_inputs = kernel_call(
        finish_body,
        shape((tokens, width), BF16),
        [normed_grads, inputs[0], grad_middle, gain_attention.reshape(1, width)],
        scalars=0,
        micros=100,
    )
    unit_grads = grad_units.astype(F32)
    return (
        layer_out[None],
        grad_inputs[None],
        gain_first_grad,
        head_grads[:, :width],
        head_grads[:, width : 2 * width],
        head_grads[:, 2 * width :],
        out_grads,
        bias_grad,
        gain_second_grad,
        unit_grads[:, :width],
        unit_grads[:, width : 2 * width],
        unit_grads[:, 2 * width :],
    )


def solution(mesh):
    owners, runs = mesh.shape["ulysses"], mesh.shape["blk"]
    fine = Mesh(mesh.devices.reshape(2, owners // 2, 4, 2, runs // 8), EVERY)
    tokens = P(("z", "y", "r"), ("x", "c"), None)
    rows = P(EVERY, None)
    return jax.shard_map(
        body,
        mesh=fine,
        in_specs=(tokens, tokens) + (P(),) * 3 + (rows,) * 4 + (P(),) * 2 + (rows,) * 3,
        out_specs=(tokens, tokens, P()) + (rows,) * 4 + (P(),) * 2 + (rows,) * 3,
        check_vma=False,
    )
```

```python
import functools

import jax
import jax.numpy as jnp
from jax import lax
from jax.experimental import pallas as pl
from jax.experimental.pallas import tpu as pltpu
from jax.sharding import Mesh
from jax.sharding import PartitionSpec as P

EPSILON = 1e-06
NEGATIVE = -1e30
HIGHEST = lax.Precision.HIGHEST
F32 = jnp.float32
BF16 = jnp.bfloat16
VMEM_LIMIT = 60 * 1024 * 1024
SQUARE = ("x", "y")
UNITS_GROUP = ("z", "c", "r")
EVERY = ("x", "c", "z", "y", "r")


def norm_scale(values):
    return lax.rsqrt(jnp.mean(values * values, axis=-1, keepdims=True) + EPSILON)


def norm_back(values, scaling, gain_vec, upstream):
    inner_sum = jnp.mean(values * gain_vec * upstream, axis=-1, keepdims=True)
    return scaling * gain_vec * upstream - values * scaling * scaling * scaling * inner_sum


def nt(left, right):
    return lax.dot_general(left, right, (((1,), (1,)), ((), ())), preferred_element_type=F32)


def nn(left, right):
    return lax.dot_general(left, right, (((1,), (0,)), ((), ())), preferred_element_type=F32)


def tn(left, right):
    return lax.dot_general(left, right, (((0,), (0,)), ((), ())), preferred_element_type=F32)


def swap(value, axis, mask):
    size = lax.axis_size(axis)
    return lax.ppermute(value, axis, [(at, at ^ mask) for at in range(size)])


def from_group(value, axis):
    return [value] + [swap(value, axis, mask) for mask in (1, 2, 3)]


def to_group(values, axis):
    return [values[0]] + [swap(values[mask], axis, mask) for mask in (1, 2, 3)]


def sum_everywhere(value, axis):
    first, second, third, fourth = from_group(value, axis)
    return (first + second) + (third + fourth)


def sum_over_z(rows, values):
    width = rows.shape[-1]
    lines = -(-values.size // width)
    padded = jnp.pad(values, (0, lines * width - values.size)).reshape(lines, width)
    high = lax.reduce_precision(padded, 8, 7)
    extra = jnp.concatenate([high, padded - high]).astype(BF16)
    extra = jnp.pad(extra, ((0, -2 * lines % 8), (0, 0)))
    arrived = to_group([jnp.concatenate([rows[at], extra]) for at in range(4)], "z")
    arrived = [part.astype(F32) for part in arrived]
    count = rows.shape[1]
    tails = [part[count : count + lines] + part[count + lines : count + 2 * lines] for part in arrived]
    total = (tails[0] + tails[1]) + (tails[2] + tails[3])
    return sum(part[:count] for part in arrived), total.ravel()[: values.size]


def kernel_call(body, out_shapes, inputs, scratch=(), scalars=1, micros=4):
    in_specs = [pl.BlockSpec(memory_space=pltpu.SMEM)] * scalars
    in_specs += [pl.BlockSpec(memory_space=pltpu.VMEM)] * (len(inputs) - scalars)
    return pl.pallas_call(
        body,
        out_shape=out_shapes,
        in_specs=in_specs,
        out_specs=jax.tree.map(lambda _: pl.BlockSpec(memory_space=pltpu.VMEM), out_shapes),
        scratch_shapes=list(scratch),
        compiler_params=pltpu.CompilerParams(vmem_limit_bytes=VMEM_LIMIT),
        cost_estimate=pl.CostEstimate(
            flops=int(micros * 1.15e9), bytes_accessed=1 << 20, transcendentals=0
        ),
    )(*inputs)


def shape(dims, dtype):
    return jax.ShapeDtypeStruct(dims, dtype)


def qkv_body(hd, coords, *refs):
    blocks, parts, other_rows, pieces = refs[:4], refs[4:8], refs[8], refs[9:13]
    rows_all, weights = refs[13:15]
    c_at, y_at = coords[1], coords[3]
    tokens, width = blocks[0].shape
    half = hd // 2
    for at in range(4):
        rows_all[at * tokens : (at + 1) * tokens, :] = blocks[at][...]
    for core in range(2):
        for dest in range(4):
            column = y_at ^ c_at ^ core
            place = (dest >> 1) * 2 + column
            shift = pl.multiple_of((y_at ^ (dest & 1)) * half, half)
            source = other_rows.at[dest * half : (dest + 1) * half] if core else parts[dest]
            for kind, first, step in ((0, 8 * hd, hd), (1, 0, 2 * hd), (2, hd, 2 * hd)):
                start = pl.multiple_of(first + place * step + shift, half)
                weights[pl.ds(start, half), :] = source[:, kind * width : (kind + 1) * width]
    normed = rows_all[...]
    pairs = nt(normed, weights[0 : 8 * hd, :]).astype(BF16)
    queries = nt(weights[8 * hd : 12 * hd, :], normed).astype(BF16)
    for dest in range(4):
        pieces[dest][0 : 4 * tokens, :] = pairs[:, dest * 2 * hd : (dest + 1) * 2 * hd]
        for at in range(4):
            pieces[dest][4 * tokens + at * hd : 4 * tokens + (at + 1) * hd, :] = queries[
                dest * hd : (dest + 1) * hd, at * tokens : (at + 1) * tokens
            ]


def bias_tiles(hvec, tokens):
    tiles = {}
    for at, diff in enumerate((-1, 0, 1)):
        spread = jnp.broadcast_to(hvec[at : at + 1, :], (tokens, 2 * tokens))
        tiles[diff] = pltpu.roll(spread, 0, 1, stride=1, stride_axis=0)[:, :tokens]
    return tiles


def fill_bias(hvec_ref, bias, cuts, repeat, c_at, r_at, tokens):
    tiles = bias_tiles(hvec_ref[...], tokens)
    zero = jnp.zeros((tokens, tokens), F32)
    bias[0] = jnp.zeros(bias.shape[1:], F32)
    for rows in range(8):
        for half in range(2):
            diff = rows - 4 - 2 * half
            even, odd = tiles.get(diff, zero), tiles.get(diff - 1, zero)
            row = (rows % 4) * tokens
            bias[1 + rows // 4, row : row + tokens, half * tokens : (half + 1) * tokens] = (
                jnp.where(c_at == 0, even, odd)
            )

    def mask(back, carry):
        place = bias.shape[0] - 3 - back
        allowed = allowed_mask(cuts, place * repeat + r_at, c_at, tokens)
        bias[2 + place] = jnp.where(allowed, bias[2], NEGATIVE)
        return carry

    lax.fori_loop(0, bias.shape[0] - 2, mask, 0)


def bias_slab(bias, place, run, at):
    return bias[jnp.where(at == run, 2 + place, jnp.where(at == run - 1, 1, 0))]


def allowed_mask(cuts, run, c_at, tokens):
    rows, cols = 4 * tokens, 2 * tokens
    key_at = lax.broadcasted_iota(jnp.int32, (rows, cols), 0)
    query_at = lax.broadcasted_iota(jnp.int32, (rows, cols), 1)
    key_window = key_at >= 2 * tokens
    query_window = query_at >= tokens
    key_in = jnp.where(key_window, key_at - 2 * tokens, key_at)
    query_in = jnp.where(query_window, query_at - tokens, query_at) + c_at * tokens
    cut = jnp.where(query_window, cuts[2 * run + 1], cuts[2 * run])
    inside = (key_in < cut) | (query_in >= cut)
    before = jnp.logical_and(jnp.logical_not(key_window), query_window)
    same = key_window == query_window
    return before | (same & inside)


def each_slot(run_low, run_high, repeat, step):
    def one(slot, carry):
        high = (slot > run_low).astype(jnp.int32)
        at = jnp.where(slot > run_low, slot - run_low - 1, slot)
        step(slot, high, at)
        return carry

    count = run_low + run_high + 2
    if repeat == 1:
        for slot in range(9):
            one(jnp.int32(slot), 0)
    else:
        lax.fori_loop(0, count, one, 0)


def chunk(at, block):
    return pl.ds(pl.multiple_of(at * block, block), block)


def fold_rows(values, how):
    rows, cols = values.shape
    return how(values.reshape(rows // 8, 8, cols), axis=0)


def attend_body(tokens, hd, repeat, coords, cuts, hvec, *refs):
    pieces, own, other = refs[:4], refs[4:8], refs[8:12]
    if repeat == 1:
        pieces = refs[:4]
        own, other, refs = refs[:4], refs[4:8], refs[8:]
    else:
        refs = refs[12:]
    out, lse, attended, keys, keys_t, queries, scores, bias, padded, peaks, totals, mixes = refs
    x_at, c_at, z_at, y_at, r_at = (coords[at] for at in range(5))
    block = 4 * tokens
    for dest in range(4):
        x_from, y_from = x_at ^ (dest >> 1), y_at ^ (dest & 1)
        for at in range(4):
            place = (z_at ^ at) * 2 + y_from
            for rep in range(repeat):
                run = place * repeat + rep
                base = run * block + x_from * 2 * tokens
                source = slice(rep * block + at * tokens, rep * block + (at + 1) * tokens)
                keys[pl.ds(pl.multiple_of(base + c_at * tokens, tokens), tokens), :] = own[dest][
                    source, :
                ]
                keys[pl.ds(pl.multiple_of(base + (1 - c_at) * tokens, tokens), tokens), :] = other[
                    dest
                ][source, :]
            start = block + at * hd
            queries[place, :, pl.ds(pl.multiple_of(x_from * tokens, tokens), tokens)] = pieces[
                dest
            ][start : start + hd, :]
    fill_bias(hvec, bias, cuts, repeat, c_at, r_at, tokens)

    def turn(at, carry):
        keys_t[at] = keys[chunk(at, block), :].T
        return carry

    lax.fori_loop(0, keys.shape[0] // block, turn, 0)
    places = queries.shape[0]
    padded[:, 0:hd, :] = queries[...]
    padded[:, hd:, :] = jnp.zeros_like(padded[:, hd:, :])

    def pair(low, carry):
        place_of = (low, places - 1 - low)
        run_of = tuple(place * repeat + r_at for place in place_of)
        peaks[...] = jnp.full_like(peaks, NEGATIVE)
        totals[...] = jnp.zeros_like(totals)
        mixes[...] = jnp.zeros_like(mixes)

        def score(slot, high, at):
            place = jnp.where(high == 1, place_of[1], place_of[0])
            run = place * repeat + r_at
            values = nn(keys[chunk(at, block), :], padded[place])
            values = values + bias_slab(bias, place, run, at)
            scores[slot] = values
            peaks[high] = jnp.maximum(peaks[high], fold_rows(values, jnp.max))

        each_slot(*run_of, repeat, score)
        for high in range(2):
            top = jnp.max(peaks[high], axis=0, keepdims=True)
            peaks[high] = jnp.broadcast_to(top, peaks.shape[1:])

        def mix(slot, high, at):
            weights = jnp.exp(scores[slot] - peaks[high][0:1, :])
            totals[high] += fold_rows(weights, jnp.sum)
            mixes[high] += nn(keys_t[at, hd:, :], weights.astype(BF16))

        each_slot(*run_of, repeat, mix)
        for high, place in enumerate(place_of):
            total = jnp.sum(totals[high], axis=0, keepdims=True)
            mixed = mixes[high] / total
            attended[place] = mixed
            lse[place] = peaks[high] + jnp.log(jnp.broadcast_to(total, peaks.shape[1:]))
            part = mixed.astype(BF16)
            for half in range(2):
                out[half * 8 + (place & 1) * 4 + (place >> 1)] = part[
                    :, half * tokens : (half + 1) * tokens
                ]
        return carry

    lax.fori_loop(0, places // 2, pair, 0)


def attend_back_body(tokens, hd, repeat, coords, cuts, hvec, *refs):
    arrived, queries, keys, keys_t, attended, lse = refs[:6]
    grad_own, grad_other, grad_q, table_out, far_out = refs[6:11]
    bias, grad_keys, table_acc, left, right, shifts, grad_queries = refs[11:]
    x_at, c_at, z_at, y_at, r_at = (coords[at] for at in range(5))
    block = 4 * tokens
    places = queries.shape[0]
    fill_bias(hvec, bias, cuts, repeat, c_at, r_at, tokens)
    grad_keys[...] = jnp.zeros_like(grad_keys)
    table_acc[...] = jnp.zeros_like(table_acc)

    def prepare(place, carry):
        query_t = queries[place]
        upstream_t = jnp.concatenate(
            [arrived[half * 8 + (place & 1) * 4 + (place >> 1)] for half in range(2)], axis=1
        )
        zero = jnp.zeros_like(query_t)
        query_pad = jnp.concatenate([query_t, zero], axis=0)
        upstream_pad = jnp.concatenate([zero, upstream_t], axis=0)
        left[place, :, 0 : 2 * tokens] = query_pad
        left[place, :, 2 * tokens :] = upstream_pad
        right[place, 0 : 2 * tokens, :] = query_pad.T
        right[place, 2 * tokens :, :] = upstream_pad.T
        shifts[place, 0:8, :] = lse[place]
        delta = jnp.sum(upstream_t.astype(F32) * attended[place], axis=0, keepdims=True)
        shifts[place, 8:16, :] = jnp.broadcast_to(delta, (8, 2 * tokens))
        return carry

    lax.fori_loop(0, places, prepare, 0)

    def pair(low, carry):
        place_of = (low, places - 1 - low)
        run_of = tuple(place * repeat + r_at for place in place_of)
        grad_queries[...] = jnp.zeros_like(grad_queries)

        def step(slot, high, at):
            place = jnp.where(high == 1, place_of[1], place_of[0])
            run = place * repeat + r_at
            rows = chunk(at, block)
            both = nn(keys[rows, :], left[place])
            values = both[:, 0 : 2 * tokens] + bias_slab(bias, place, run, at)
            probs = jnp.exp(values - shifts[place, 0:1, :])
            grad_scores = probs * (both[:, 2 * tokens :] - shifts[place, 8:9, :])
            grad_low = grad_scores.astype(BF16)
            grad_keys[rows, :] += nn(
                jnp.concatenate([grad_low, probs.astype(BF16)], axis=1), right[place]
            )
            grad_queries[high] += nn(keys_t[at, :hd, :], grad_low)
            kind = jnp.where(at == run, 2, jnp.where(at == run - 1, 1, 0))
            table_acc[kind] += grad_low.astype(F32)

        each_slot(*run_of, repeat, step)
        for high, place in enumerate(place_of):
            low_part = grad_queries[high].astype(BF16)
            for half in range(2):
                part = low_part[:, half * tokens : (half + 1) * tokens]
                dest = (x_at ^ half) * 2 + ((place & 1) ^ y_at)
                grad_q[dest * 4 + ((place >> 1) ^ z_at)] = part
        return carry

    lax.fori_loop(0, places // 2, pair, 0)

    for dest in range(4):
        x_from, y_from = x_at ^ (dest >> 1), y_at ^ (dest & 1)
        for at in range(4):
            place = (z_at ^ at) * 2 + y_from
            for rep in range(repeat):
                base = (place * repeat + rep) * block + x_from * 2 * tokens
                start = (dest * repeat + rep) * block + at * tokens
                target = slice(start, start + tokens)
                grad_own[target, :] = grad_keys[
                    pl.ds(pl.multiple_of(base + c_at * tokens, tokens), tokens), :
                ]
                grad_other[target, :] = grad_keys[
                    pl.ds(pl.multiple_of(base + (1 - c_at) * tokens, tokens), tokens), :
                ].astype(BF16)

    def tile_at(rows, half):
        row = (rows % 4) * tokens
        return table_acc[
            1 + rows // 4, row : row + tokens, half * tokens : (half + 1) * tokens
        ]

    spots = [(rows, half) for rows in range(8) for half in range(2)]
    flip = (
        lax.broadcasted_iota(jnp.int32, (tokens, tokens), 0)
        + lax.broadcasted_iota(jnp.int32, (tokens, tokens), 1)
        == tokens - 1
    ).astype(F32)
    far_even = jnp.zeros((tokens, tokens), F32)
    far_odd = jnp.zeros((tokens, tokens), F32)
    for rows, half in spots:
        diff = rows - 4 - 2 * half
        if diff <= -2:
            far_even += tile_at(rows, half)
        if diff - 1 <= -2:
            far_odd += tile_at(rows, half)
    extra = fold_rows(jnp.where(c_at == 0, far_even, far_odd), jnp.sum)
    far_out[...] = fold_rows(table_acc[0], jnp.sum)
    far_out[:, :tokens] += extra
    table_out[...] = jnp.zeros_like(table_out)
    for index, diff in enumerate((-1, 0, 1)):
        even = sum(tile_at(rows, half) for rows, half in spots if rows - 4 - 2 * half == diff)
        odd = sum(tile_at(rows, half) for rows, half in spots if rows - 5 - 2 * half == diff)
        tile = jnp.where(c_at == 0, even, odd)
        turned = jnp.dot(flip, tile, precision=HIGHEST, preferred_element_type=F32)
        wide = jnp.concatenate([turned, jnp.zeros_like(turned)], axis=1)
        wide = pltpu.roll(wide, tokens + 1, 1, stride=1, stride_axis=0)
        table_out[index : index + 1, :] = jnp.sum(wide, axis=0, keepdims=True)


def project_back_body(hd, coords, *refs):
    pieces, (rows_all, weights, gain), out = refs[:4], refs[4:7], refs[7]
    gain_out, pairs_t, queries_t, pairs, queries = refs[8:]
    tokens, width = out.shape[1:]
    z_at = coords[2]
    for dest in range(4):
        lanes = slice(dest * 2 * hd, (dest + 1) * 2 * hd)
        part = pieces[dest][0 : 4 * tokens, :]
        pairs[:, lanes] = part
        pairs_t[lanes, :] = part.T
        for at in range(4):
            queries_t[dest * hd : (dest + 1) * hd, at * tokens : (at + 1) * tokens] = pieces[dest][
                4 * tokens + at * hd : 4 * tokens + (at + 1) * hd, :
            ]
    queries[...] = queries_t[...].T
    grad = nn(pairs[...], weights[0 : 8 * hd, :]) + nn(queries[...], weights[8 * hd :, :])
    unit = rows_all[...].astype(F32) / gain[...]
    gain_out[...] = fold_rows(grad * unit, jnp.sum)
    for at in range(4):
        out[z_at ^ at] = grad[at * tokens : (at + 1) * tokens, :].astype(BF16)


def head_grads_body(hd, coords, pairs_t, queries_t, rows_all, keep, send):
    c_at, y_at = coords[1], coords[3]
    width = rows_all.shape[1]
    half = hd // 2
    normed = rows_all[...]
    pair_rows = nn(pairs_t[...], normed).astype(BF16)
    query_rows = nn(queries_t[...], normed).astype(BF16)
    for dest in range(4):
        other = (y_at ^ (dest & 1)) ^ c_at

        def put(target, dest=dest):
            for part in range(2):
                place = (dest >> 1) * 2 + (y_at ^ part)
                for kind, rows, first in (
                    (0, query_rows, dest * hd),
                    (1, pair_rows, dest * 2 * hd),
                    (2, pair_rows, dest * 2 * hd + hd),
                ):
                    first += part * half
                    target[place, :, kind * width : (kind + 1) * width] = rows[
                        first : first + half, :
                    ]

        pl.when(other == 0)(functools.partial(put, keep))
        pl.when(other == 1)(functools.partial(put, send))


def output_body(hd, coords, *refs):
    arrived, own_in, gain, parts, middle_out, normed_out, weights, features = refs
    x_at, c_at, z_at, y_at = coords[0], coords[1], coords[2], coords[3]
    half, tokens = hd // 2, arrived.shape[1]
    for z_of in range(4):
        for c_of in range(2):
            for dest in range(4):
                head = ((x_at ^ (dest >> 1)) * 2 + c_of) * 4 + z_of
                start = pl.multiple_of(head * hd + (y_at ^ (dest & 1)) * half, half)
                weights[pl.ds(start, half), :] = parts[
                    z_of * 2 + c_of, dest * half : (dest + 1) * half, :
                ]
    for dest in range(4):
        for core in range(2):
            for near in range(4):
                head = ((x_at ^ (dest >> 1)) * 2 + (c_at ^ core)) * 4 + (z_at ^ near)
                start = pl.multiple_of(head * hd + (y_at ^ (dest & 1)) * half, half)
                lanes = slice((core * 4 + near) * tokens, (core * 4 + near + 1) * tokens)
                features[dest, :, lanes] = arrived[pl.ds(start, half), :]
    middle = own_in[...].astype(F32) + nn(arrived[...].T, weights[...])
    middle_out[...] = middle
    normed_out[...] = (middle * norm_scale(middle) * gain[...]).astype(BF16)


def finish_body(*refs):
    parts, own_in, grad_middle, gain, out = refs
    values = own_in[...].astype(F32)
    grad = sum(parts[at].astype(F32) for at in range(4))
    out[...] = (
        grad_middle[...] + norm_back(values, norm_scale(values), gain[...], grad)
    ).astype(BF16)


def gated(gate_act, up_act):
    return jax.nn.gelu(gate_act, approximate=True) * up_act


def body(
    inputs,
    cotangent,
    segment_ids,
    bucket_table,
    gain_attention,
    query_weight,
    key_weight,
    value_weight,
    output_weight,
    bucket_bias,
    gain_feedforward,
    gate_weight,
    up_weight,
    down_weight,
):
    tokens, width = inputs.shape[1:]
    repeat = lax.axis_size("r")
    x_at, c_at, z_at, y_at, r_at = (lax.axis_index(name) for name in EVERY)
    coords = jnp.stack([x_at, c_at, z_at, y_at, r_at]).astype(jnp.int32)
    bucket_count, head_count = bucket_bias.shape
    hd = width // head_count
    block = 4 * tokens
    length = segment_ids.size
    reach = (bucket_table.shape[0] - 1) // 2
    assert reach == tokens and lax.axis_size("x") == lax.axis_size("c") == 2

    hidden_in = inputs[0].astype(F32)
    cot_own = cotangent[0]
    scale_first = norm_scale(hidden_in)
    normed = (hidden_in * scale_first * gain_attention).astype(BF16)
    normed_parts = from_group(normed, "z")

    joined = jnp.concatenate([query_weight, key_weight, value_weight, output_weight], axis=1)
    if repeat > 1:
        joined = lax.all_gather(joined, "r", axis=0, tiled=True)
    head_rows = from_group(joined, SQUARE)
    other_rows = swap(jnp.concatenate([part[:, : 3 * width] for part in head_rows]), "c", 1)
    out_rows = jnp.concatenate([part[:, 3 * width :] for part in head_rows])
    units = jnp.concatenate([gate_weight, up_weight, down_weight], axis=1)
    unit_rows = lax.all_gather(units, UNITS_GROUP, axis=0, tiled=True)
    gate_piece, up_piece, down_piece = (
        unit_rows[:, at * width : (at + 1) * width] for at in range(3)
    )

    windows = segment_ids.reshape(-1, 2 * tokens)
    cuts = jnp.sum((windows < windows[:, -1:]).astype(jnp.int32), axis=1)
    turned = bucket_table[::-1]
    low_half, high_half = turned[reach : 2 * reach], turned[:reach]
    spots = jnp.concatenate(
        [
            jnp.broadcast_to(bucket_table[:1], (reach,)),
            low_half,
            low_half,
            high_half,
            high_half,
            jnp.broadcast_to(bucket_table[2 * reach :], (reach,)),
        ]
    )
    buckets = jnp.arange(bucket_count, dtype=jnp.int32)
    onehot = (spots[:, None] == buckets[None, :]).astype(F32)
    far_onehot = (bucket_table[0] == buckets).astype(F32)
    head_at = (x_at * 2 + y_at) * 4 + z_at
    bias_col = lax.dynamic_slice_in_dim(bucket_bias, head_at, 1, 1)[:, 0]
    diag = jnp.dot(onehot, bias_col, precision=HIGHEST) - jnp.sum(far_onehot * bias_col)
    hvec = jnp.pad(diag.reshape(3, 2 * reach), ((0, 5), (0, 0)))

    normed_parts, hvec, cuts, coords, out_rows = lax.optimization_barrier(
        (normed_parts, hvec, cuts, coords, out_rows)
    )
    made = kernel_call(
        functools.partial(qkv_body, hd),
        [shape((block + 4 * hd, 2 * hd), BF16)] * 4
        + [shape((block, width), BF16), shape((12 * hd, width), BF16)],
        [coords, *normed_parts, *head_rows, other_rows],
    )
    pieces, (normed_all, group_weights) = made[:4], made[4:]
    pieces = to_group(pieces, SQUARE)

    out_all = lax.all_gather(out_rows, ("z", "c"), axis=0, tiled=False)
    own = [piece[:block] for piece in pieces]
    other = swap(jnp.concatenate(own, axis=0), "c", 1)
    other = [other[at * block : (at + 1) * block] for at in range(4)]
    if repeat == 1:
        arrays = [*pieces, *other]
    else:
        own = [lax.all_gather(part, "r", axis=0, tiled=True) for part in own]
        other = [lax.all_gather(part, "r", axis=0, tiled=True) for part in other]
        arrays = [*pieces, *own, *other]
    places = 8
    out_t, lse, attended, keys, keys_t, queries = kernel_call(
        functools.partial(attend_body, tokens, hd, repeat),
        [
            shape((16, hd, tokens), BF16),
            shape((places, 8, 2 * tokens), F32),
            shape((places, hd, 2 * tokens), F32),
            shape((length, 2 * hd), BF16),
            shape((length // block, 2 * hd, block), BF16),
            shape((places, hd, 2 * tokens), BF16),
        ],
        [coords, cuts, hvec, *arrays],
        [
            pltpu.VMEM((9 * repeat, block, 2 * tokens), F32),
            pltpu.VMEM((places + 2, block, 2 * tokens), F32),
            pltpu.VMEM((places, 2 * hd, 2 * tokens), BF16),
            pltpu.VMEM((2, 8, 2 * tokens), F32),
            pltpu.VMEM((2, 8, 2 * tokens), F32),
            pltpu.VMEM((2, hd, 2 * tokens), F32),
        ],
        scalars=2,
        micros=20,
    )
    cot_sent, _ = lax.optimization_barrier((cot_own, other))
    cot_parts, out_t = lax.optimization_barrier((from_group(cot_sent, SQUARE), out_t))
    cot_all = jnp.concatenate(cot_parts, axis=0)
    arrived = lax.all_to_all(out_t, ("x", "y", "z"), split_axis=0, concat_axis=0, tiled=True)

    middle, normed_mid, out_full, features = kernel_call(
        functools.partial(output_body, hd),
        [
            shape((tokens, width), F32),
            shape((tokens, width), BF16),
            shape((width, width), BF16),
            shape((4, hd // 2, 8 * tokens), BF16),
        ],
        [
            coords,
            arrived.reshape(width, tokens),
            inputs[0],
            gain_feedforward.reshape(1, width),
            out_all,
        ],
    )
    scale_second = norm_scale(middle)
    mid_all = jnp.concatenate(from_group(normed_mid, SQUARE), axis=0)

    gate_act = nt(mid_all, gate_piece)
    up_act = nt(mid_all, up_piece)
    hidden_val, pullback = jax.vjp(gated, gate_act, up_act)
    hidden = hidden_val.astype(BF16)
    grad_gate, grad_up = pullback(nt(cot_all, down_piece))
    gate_low, up_low = grad_gate.astype(BF16), grad_up.astype(BF16)
    grad_norm = (nn(gate_low, gate_piece) + nn(up_low, up_piece)).astype(BF16)
    grad_parts = to_group(
        [grad_norm[at * tokens : (at + 1) * tokens] for at in range(4)], SQUARE
    )
    unit_grads = jnp.concatenate(
        [tn(gate_low, mid_all), tn(up_low, mid_all), tn(hidden, cot_all)], axis=1
    ).astype(BF16)
    feed = nn(hidden, down_piece).astype(BF16)
    grad_parts, unit_grads, feed = lax.optimization_barrier((grad_parts, unit_grads, feed))
    grad_norm_mid = sum(part.astype(F32) for part in grad_parts)

    grad_middle = cot_own.astype(F32) + norm_back(
        middle, scale_second, gain_feedforward, grad_norm_mid
    )
    gain_second_term = jnp.sum(grad_norm_mid * middle * scale_second, axis=0)
    grad_mid_low = grad_middle.astype(BF16)
    grad_attended = nt(out_full, grad_mid_low).astype(BF16)
    grad_arrived = lax.all_to_all(
        grad_attended.reshape(16, hd, tokens),
        ("x", "y", "z"),
        split_axis=0,
        concat_axis=0,
        tiled=True,
    )
    grad_arrived, grad_mid_low, unit_grads = lax.optimization_barrier(
        (grad_arrived, grad_mid_low, unit_grads)
    )
    grad_units = lax.psum_scatter(unit_grads, UNITS_GROUP, scatter_dimension=0, tiled=True)
    mixed = to_group(
        [
            jnp.concatenate(
                [
                    feed[at * tokens : (at + 1) * tokens],
                    grad_mid_low,
                    features[at],
                ]
            )
            for at in range(4)
        ],
        SQUARE,
    )

    grad_own, grad_other, grad_q, table_out, far_out = kernel_call(
        functools.partial(attend_back_body, tokens, hd, repeat),
        [
            shape((4 * repeat * block, 2 * hd), F32),
            shape((4 * repeat * block, 2 * hd), BF16),
            shape((16, hd, tokens), BF16),
            shape((8, 2 * tokens), F32),
            shape((8, 2 * tokens), F32),
        ],
        [coords, cuts, hvec, grad_arrived, queries, keys, keys_t, attended, lse],
        [
            pltpu.VMEM((places + 2, block, 2 * tokens), F32),
            pltpu.VMEM((length, 2 * hd), F32),
            pltpu.VMEM((3, block, 2 * tokens), F32),
            pltpu.VMEM((places, 2 * hd, 4 * tokens), BF16),
            pltpu.VMEM((places, 4 * tokens, 2 * hd), BF16),
            pltpu.VMEM((places, 16, 2 * tokens), F32),
            pltpu.VMEM((2, hd, 2 * tokens), F32),
        ],
        scalars=2,
        micros=20,
    )
    mixed, grad_own = lax.optimization_barrier((mixed, grad_own))
    grad_pairs = (grad_own + swap(grad_other, "c", 1).astype(F32)).astype(BF16)
    grad_pairs = [
        grad_pairs[at * repeat * block : (at + 1) * repeat * block] for at in range(4)
    ]
    if repeat > 1:
        grad_pairs = [
            lax.psum_scatter(part, "r", scatter_dimension=0, tiled=True) for part in grad_pairs
        ]
    grad_pieces = [
        jnp.concatenate([grad_pairs[at], grad_q[4 * at : 4 * at + 4].reshape(4 * hd, tokens)])
        for at in range(4)
    ]
    mixed, grad_pieces = lax.optimization_barrier((mixed, grad_pieces))
    grad_pieces = to_group(grad_pieces, SQUARE)

    made = kernel_call(
        functools.partial(project_back_body, hd),
        [
            shape((4, tokens, width), BF16),
            shape((8, width), F32),
            shape((8 * hd, block), BF16),
            shape((4 * hd, block), BF16),
        ],
        [coords, *grad_pieces, normed_all, group_weights, gain_attention.reshape(1, width)],
        [pltpu.VMEM((block, 8 * hd), BF16), pltpu.VMEM((block, 4 * hd), BF16)],
    )
    normed_grads, gain_first_rows, pairs_t, queries_t = made
    normed_grads = lax.all_to_all(normed_grads, "z", split_axis=0, concat_axis=0, tiled=True)
    keep, send = kernel_call(
        functools.partial(head_grads_body, hd),
        [shape((4, hd // 2, 3 * width), BF16)] * 2,
        [coords, pairs_t, queries_t, normed_all],
    )
    layer_out = (middle + sum(part[:tokens].astype(F32) for part in mixed)).astype(BF16)
    grad_mid_all = jnp.concatenate([part[tokens : 2 * tokens] for part in mixed], axis=0)
    near = jnp.stack([part[2 * tokens :] for part in mixed]).reshape(4, hd // 2, 8, tokens)
    near = near.transpose(2, 1, 0, 3).reshape(4 * hd, block)
    out_grads = nn(near, grad_mid_all).astype(BF16)

    table_out, far_out, keep, send, grad_units, out_grads = lax.optimization_barrier(
        (table_out, far_out, keep, send, grad_units, out_grads)
    )
    out_grads = out_grads.reshape(2, 4, hd // 2, width)
    out_grads = (out_grads[0].astype(F32) + swap(out_grads[1], "c", 1).astype(F32)).astype(BF16)
    head_grads = (keep.astype(F32) + swap(send, "c", 1).astype(F32)).astype(BF16)
    bucket_grad = jnp.dot(table_out[:3].reshape(1, -1), onehot, precision=HIGHEST)[0]
    bucket_grad = bucket_grad + far_onehot * jnp.sum(far_out)
    head_mark = (jnp.arange(head_count) == head_at).astype(F32)
    bias_term = bucket_grad[:, None] * head_mark[None, :]
    sums = jnp.concatenate([jnp.sum(gain_first_rows, axis=0), gain_second_term, bias_term.ravel()])
    sums = sums + swap(sums, "c", 1)
    sums = sum_everywhere(sums, SQUARE)
    head_grads = to_group([head_grads[at] for at in range(4)], SQUARE)
    normed_grads, head_grads, sums, out_grads = lax.optimization_barrier(
        (normed_grads, head_grads, sums, out_grads)
    )
    out_grads, sums = sum_over_z(out_grads, sums)
    head_grads = sum(part.astype(F32) for part in head_grads)
    if repeat > 1:
        sums = lax.psum(sums, "r")
        out_grads = lax.psum_scatter(
            out_grads.astype(BF16), "r", scatter_dimension=0, tiled=True
        ).astype(F32)
        head_grads = lax.psum_scatter(
            head_grads.astype(BF16), "r", scatter_dimension=0, tiled=True
        ).astype(F32)
    gain_first_grad, gain_second_grad = sums[:width], sums[width : 2 * width]
    bias_grad = sums[2 * width :].reshape(bucket_count, head_count)

    grad_inputs = kernel_call(
        finish_body,
        shape((tokens, width), BF16),
        [normed_grads, inputs[0], grad_middle, gain_attention.reshape(1, width)],
        scalars=0,
        micros=100,
    )
    unit_grads = grad_units.astype(F32)
    return (
        layer_out[None],
        grad_inputs[None],
        gain_first_grad,
        head_grads[:, :width],
        head_grads[:, width : 2 * width],
        head_grads[:, 2 * width :],
        out_grads,
        bias_grad,
        gain_second_grad,
        unit_grads[:, :width],
        unit_grads[:, width : 2 * width],
        unit_grads[:, 2 * width :],
    )


def solution(mesh):
    owners, runs = mesh.shape["ulysses"], mesh.shape["blk"]
    fine = Mesh(mesh.devices.reshape(2, owners // 2, 4, 2, runs // 8), EVERY)
    tokens = P(("z", "y", "r"), ("x", "c"), None)
    rows = P(EVERY, None)
    return jax.shard_map(
        body,
        mesh=fine,
        in_specs=(tokens, tokens) + (P(),) * 3 + (rows,) * 4 + (P(),) * 2 + (rows,) * 3,
        out_specs=(tokens, tokens, P()) + (rows,) * 4 + (P(),) * 2 + (rows,) * 3,
        check_vma=False,
    )
```

```python
import functools

import jax
import jax.numpy as jnp
from jax import lax
from jax.experimental import pallas as pl
from jax.experimental.pallas import tpu as pltpu
from jax.sharding import Mesh
from jax.sharding import PartitionSpec as P

EPSILON = 1e-06
NEGATIVE = -1e30
HIGHEST = lax.Precision.HIGHEST
F32 = jnp.float32
BF16 = jnp.bfloat16
MEBI = 1024 * 1024
SQUARE = ("x", "y")
UNITS_GROUP = ("z", "c", "r")
EVERY = ("x", "c", "z", "y", "r")


def norm_scale(values):
    return lax.rsqrt(jnp.mean(values * values, axis=-1, keepdims=True) + EPSILON)


def norm_back(values, scaling, gain_vec, upstream):
    inner_sum = jnp.mean(values * gain_vec * upstream, axis=-1, keepdims=True)
    return scaling * gain_vec * upstream - values * scaling * scaling * scaling * inner_sum


def nt(left, right):
    return lax.dot_general(left, right, (((1,), (1,)), ((), ())), preferred_element_type=F32)


def nn(left, right):
    return lax.dot_general(left, right, (((1,), (0,)), ((), ())), preferred_element_type=F32)


def tn(left, right):
    return lax.dot_general(left, right, (((0,), (0,)), ((), ())), preferred_element_type=F32)


def swap(value, axis, mask):
    size = lax.axis_size(axis)
    return lax.ppermute(value, axis, [(at, at ^ mask) for at in range(size)])


def from_group(value, axis):
    return [value] + [swap(value, axis, mask) for mask in (1, 2, 3)]


def to_group(values, axis):
    return [values[0]] + [swap(values[mask], axis, mask) for mask in (1, 2, 3)]


def sum_everywhere(value, axis):
    first, second, third, fourth = from_group(value, axis)
    return (first + second) + (third + fourth)


def sum_over_z(rows, values):
    width = rows.shape[-1]
    lines = -(-values.size // width)
    padded = jnp.pad(values, (0, lines * width - values.size)).reshape(lines, width)
    high = lax.reduce_precision(padded, 8, 7)
    extra = jnp.concatenate([high, padded - high]).astype(BF16)
    extra = jnp.pad(extra, ((0, -2 * lines % 8), (0, 0)))
    arrived = to_group([jnp.concatenate([rows[at], extra]) for at in range(4)], "z")
    arrived = [part.astype(F32) for part in arrived]
    count = rows.shape[1]
    tails = [part[count : count + lines] + part[count + lines : count + 2 * lines] for part in arrived]
    total = (tails[0] + tails[1]) + (tails[2] + tails[3])
    return sum(part[:count] for part in arrived), total.ravel()[: values.size]


def kernel_call(body, out_shapes, inputs, scratch=(), scalars=1, micros=4, mebi=60):
    in_specs = [pl.BlockSpec(memory_space=pltpu.SMEM)] * scalars
    in_specs += [pl.BlockSpec(memory_space=pltpu.VMEM)] * (len(inputs) - scalars)
    return pl.pallas_call(
        body,
        out_shape=out_shapes,
        in_specs=in_specs,
        out_specs=jax.tree.map(lambda _: pl.BlockSpec(memory_space=pltpu.VMEM), out_shapes),
        scratch_shapes=list(scratch),
        compiler_params=pltpu.CompilerParams(vmem_limit_bytes=mebi * MEBI),
        cost_estimate=pl.CostEstimate(
            flops=int(micros * 1.15e9), bytes_accessed=1 << 20, transcendentals=0
        ),
    )(*inputs)


def shape(dims, dtype):
    return jax.ShapeDtypeStruct(dims, dtype)


def pack_body(*refs):
    own_in, gain, out_rows = refs[:3]
    heads, units = refs[3:6], refs[6:9]
    message, joined, joined_units = refs[9:]
    tokens, width = own_in.shape
    values = own_in[...].astype(F32)
    message[0:tokens, :] = (values * norm_scale(values) * gain[...]).astype(BF16)
    message[tokens:, :] = out_rows[...]
    for at in range(3):
        joined[:, at * width : (at + 1) * width] = heads[at][...]
        joined_units[:, at * width : (at + 1) * width] = units[at][...]


def anchor_body(*refs):
    refs[-1][...] = jnp.zeros_like(refs[-1])


def anchor(values, micros):
    return pl.pallas_call(
        anchor_body,
        out_shape=shape((8, 128), F32),
        in_specs=[pl.BlockSpec(memory_space=pl.ANY)] * len(values),
        out_specs=pl.BlockSpec(memory_space=pltpu.VMEM),
        cost_estimate=pl.CostEstimate(
            flops=int(micros * 1.15e9), bytes_accessed=1 << 20, transcendentals=0
        ),
    )(*values)


def qkv_body(hd, coords, *refs):
    blocks, parts, other_rows, cot_own, pieces = refs[:4], refs[4:8], refs[8], refs[9], refs[11:15]
    rows_all, weights, onward = refs[15:18]
    c_at, y_at = coords[1], coords[3]
    width, half = rows_all.shape[1], hd // 2
    tokens = rows_all.shape[0] // 4
    for at in range(4):
        rows_all[at * tokens : (at + 1) * tokens, :] = blocks[at][0:tokens, :]
        start = tokens + at * half
        onward[start : start + half, :] = blocks[at][tokens:, :]
    onward[0:tokens, :] = cot_own[...]
    for core in range(2):
        for dest in range(4):
            column = y_at ^ c_at ^ core
            place = (dest >> 1) * 2 + column
            shift = pl.multiple_of((y_at ^ (dest & 1)) * half, half)
            source = other_rows.at[dest * half : (dest + 1) * half] if core else parts[dest]
            for kind, first, step in ((0, 8 * hd, hd), (1, 0, 2 * hd), (2, hd, 2 * hd)):
                start = pl.multiple_of(first + place * step + shift, half)
                weights[pl.ds(start, half), :] = source[:, kind * width : (kind + 1) * width]
    normed = rows_all[...]
    pairs = nt(normed, weights[0 : 8 * hd, :]).astype(BF16)
    queries = nt(weights[8 * hd : 12 * hd, :], normed).astype(BF16)
    for dest in range(4):
        pieces[dest][0 : 4 * tokens, :] = pairs[:, dest * 2 * hd : (dest + 1) * 2 * hd]
        for at in range(4):
            pieces[dest][4 * tokens + at * hd : 4 * tokens + (at + 1) * hd, :] = queries[
                dest * hd : (dest + 1) * hd, at * tokens : (at + 1) * tokens
            ]


def bias_tiles(hvec, tokens):
    tiles = {}
    for at, diff in enumerate((-1, 0, 1)):
        spread = jnp.broadcast_to(hvec[at : at + 1, :], (tokens, 2 * tokens))
        tiles[diff] = pltpu.roll(spread, 0, 1, stride=1, stride_axis=0)[:, :tokens]
    return tiles


def fill_bias(hvec_ref, bias, cuts, repeat, c_at, r_at, tokens):
    tiles = bias_tiles(hvec_ref[...], tokens)
    zero = jnp.zeros((tokens, tokens), F32)
    bias[0] = jnp.zeros(bias.shape[1:], F32)
    for rows in range(8):
        for half in range(2):
            diff = rows - 4 - 2 * half
            even, odd = tiles.get(diff, zero), tiles.get(diff - 1, zero)
            row = (rows % 4) * tokens
            bias[1 + rows // 4, row : row + tokens, half * tokens : (half + 1) * tokens] = (
                jnp.where(c_at == 0, even, odd)
            )

    def mask(back, carry):
        place = bias.shape[0] - 3 - back
        allowed = allowed_mask(cuts, place * repeat + r_at, c_at, tokens)
        bias[2 + place] = jnp.where(allowed, bias[2], NEGATIVE)
        return carry

    lax.fori_loop(0, bias.shape[0] - 2, mask, 0)


def bias_slab(bias, place, run, at):
    return bias[jnp.where(at == run, 2 + place, jnp.where(at == run - 1, 1, 0))]


def allowed_mask(cuts, run, c_at, tokens):
    rows, cols = 4 * tokens, 2 * tokens
    key_at = lax.broadcasted_iota(jnp.int32, (rows, cols), 0)
    query_at = lax.broadcasted_iota(jnp.int32, (rows, cols), 1)
    key_window = key_at >= 2 * tokens
    query_window = query_at >= tokens
    key_in = jnp.where(key_window, key_at - 2 * tokens, key_at)
    query_in = jnp.where(query_window, query_at - tokens, query_at) + c_at * tokens
    cut = jnp.where(query_window, cuts[2 * run + 1], cuts[2 * run])
    inside = (key_in < cut) | (query_in >= cut)
    before = jnp.logical_and(jnp.logical_not(key_window), query_window)
    same = key_window == query_window
    return before | (same & inside)


def each_slot(run_low, run_high, repeat, step):
    def one(slot, carry):
        high = (slot > run_low).astype(jnp.int32)
        at = jnp.where(slot > run_low, slot - run_low - 1, slot)
        step(slot, high, at)
        return carry

    count = run_low + run_high + 2
    if repeat == 1:
        for slot in range(9):
            one(jnp.int32(slot), 0)
    else:
        lax.fori_loop(0, count, one, 0)


def chunk(at, block):
    return pl.ds(pl.multiple_of(at * block, block), block)


def fold_rows(values, how):
    rows, cols = values.shape
    return how(values.reshape(rows // 8, 8, cols), axis=0)


def attend_body(tokens, hd, repeat, coords, cuts, hvec, *refs):
    pieces = refs[:4]
    own, other, refs = (pieces, *refs[4:5], refs[5:]) if repeat == 1 else (refs[4:8], refs[8], refs[9:])
    out, lse, attended, keys, keys_t, queries, scores, bias, padded, peaks, totals, mixes = refs
    x_at, c_at, z_at, y_at, r_at = (coords[at] for at in range(5))
    block = 4 * tokens
    for dest in range(4):
        x_from, y_from = x_at ^ (dest >> 1), y_at ^ (dest & 1)
        for at in range(4):
            place = (z_at ^ at) * 2 + y_from
            for rep in range(repeat):
                run = place * repeat + rep
                base = run * block + x_from * 2 * tokens
                source = slice(rep * block + at * tokens, rep * block + (at + 1) * tokens)
                keys[pl.ds(pl.multiple_of(base + c_at * tokens, tokens), tokens), :] = own[dest][
                    source, :
                ]
                start = (dest * repeat + rep) * block + at * tokens
                keys[pl.ds(pl.multiple_of(base + (1 - c_at) * tokens, tokens), tokens), :] = other[
                    start : start + tokens, :
                ]
            start = block + at * hd
            queries[place, :, pl.ds(pl.multiple_of(x_from * tokens, tokens), tokens)] = pieces[
                dest
            ][start : start + hd, :]
    fill_bias(hvec, bias, cuts, repeat, c_at, r_at, tokens)

    def turn(at, carry):
        keys_t[at] = keys[chunk(at, block), :].T
        return carry

    lax.fori_loop(0, keys.shape[0] // block, turn, 0)
    places = queries.shape[0]
    padded[:, 0:hd, :] = queries[...]
    padded[:, hd:, :] = jnp.zeros_like(padded[:, hd:, :])

    def pair(low, carry):
        place_of = (low, places - 1 - low)
        run_of = tuple(place * repeat + r_at for place in place_of)
        peaks[...] = jnp.full_like(peaks, NEGATIVE)
        totals[...] = jnp.zeros_like(totals)
        mixes[...] = jnp.zeros_like(mixes)

        def score(slot, high, at):
            place = jnp.where(high == 1, place_of[1], place_of[0])
            run = place * repeat + r_at
            values = nn(keys[chunk(at, block), :], padded[place])
            values = values + bias_slab(bias, place, run, at)
            scores[slot] = values
            peaks[high] = jnp.maximum(peaks[high], fold_rows(values, jnp.max))

        each_slot(*run_of, repeat, score)
        for high in range(2):
            top = jnp.max(peaks[high], axis=0, keepdims=True)
            peaks[high] = jnp.broadcast_to(top, peaks.shape[1:])

        def mix(slot, high, at):
            weights = jnp.exp(scores[slot] - peaks[high][0:1, :])
            totals[high] += fold_rows(weights, jnp.sum)
            mixes[high] += nn(keys_t[at, hd:, :], weights.astype(BF16))

        each_slot(*run_of, repeat, mix)
        for high, place in enumerate(place_of):
            total = jnp.sum(totals[high], axis=0, keepdims=True)
            mixed = mixes[high] / total
            attended[place] = mixed
            lse[place] = peaks[high] + jnp.log(jnp.broadcast_to(total, peaks.shape[1:]))
            part = mixed.astype(BF16)
            for half in range(2):
                out[half * 8 + (place & 1) * 4 + (place >> 1)] = part[
                    :, half * tokens : (half + 1) * tokens
                ]
        return carry

    lax.fori_loop(0, places // 2, pair, 0)


def attend_back_body(tokens, hd, repeat, coords, cuts, hvec, *refs):
    arrived, queries, keys, keys_t, attended, lse = refs[:6]
    grad_own, grad_other, grad_q, table_out, far_out = refs[6:11]
    bias, grad_keys, table_acc, left, right, shifts, grad_queries = refs[11:]
    x_at, c_at, z_at, y_at, r_at = (coords[at] for at in range(5))
    block = 4 * tokens
    places = queries.shape[0]
    fill_bias(hvec, bias, cuts, repeat, c_at, r_at, tokens)
    grad_keys[...] = jnp.zeros_like(grad_keys)
    table_acc[...] = jnp.zeros_like(table_acc)

    def prepare(place, carry):
        query_t = queries[place]
        upstream_t = jnp.concatenate(
            [arrived[half * 8 + (place & 1) * 4 + (place >> 1)] for half in range(2)], axis=1
        )
        zero = jnp.zeros_like(query_t)
        query_pad = jnp.concatenate([query_t, zero], axis=0)
        upstream_pad = jnp.concatenate([zero, upstream_t], axis=0)
        left[place, :, 0 : 2 * tokens] = query_pad
        left[place, :, 2 * tokens :] = upstream_pad
        right[place, 0 : 2 * tokens, :] = query_pad.T
        right[place, 2 * tokens :, :] = upstream_pad.T
        shifts[place, 0:8, :] = lse[place]
        delta = jnp.sum(upstream_t.astype(F32) * attended[place], axis=0, keepdims=True)
        shifts[place, 8:16, :] = jnp.broadcast_to(delta, (8, 2 * tokens))
        return carry

    lax.fori_loop(0, places, prepare, 0)

    def pair(low, carry):
        place_of = (low, places - 1 - low)
        run_of = tuple(place * repeat + r_at for place in place_of)
        grad_queries[...] = jnp.zeros_like(grad_queries)

        def step(slot, high, at):
            place = jnp.where(high == 1, place_of[1], place_of[0])
            run = place * repeat + r_at
            rows = chunk(at, block)
            both = nn(keys[rows, :], left[place])
            values = both[:, 0 : 2 * tokens] + bias_slab(bias, place, run, at)
            probs = jnp.exp(values - shifts[place, 0:1, :])
            grad_scores = probs * (both[:, 2 * tokens :] - shifts[place, 8:9, :])
            grad_low = grad_scores.astype(BF16)
            grad_keys[rows, :] += nn(
                jnp.concatenate([grad_low, probs.astype(BF16)], axis=1), right[place]
            )
            grad_queries[high] += nn(keys_t[at, :hd, :], grad_low)
            kind = jnp.where(at == run, 2, jnp.where(at == run - 1, 1, 0))
            table_acc[kind] += grad_low.astype(F32)

        each_slot(*run_of, repeat, step)
        for high, place in enumerate(place_of):
            low_part = grad_queries[high].astype(BF16)
            for half in range(2):
                part = low_part[:, half * tokens : (half + 1) * tokens]
                dest = (x_at ^ half) * 2 + ((place & 1) ^ y_at)
                grad_q[dest * 4 + ((place >> 1) ^ z_at)] = part
        return carry

    lax.fori_loop(0, places // 2, pair, 0)

    for dest in range(4):
        x_from, y_from = x_at ^ (dest >> 1), y_at ^ (dest & 1)
        for at in range(4):
            place = (z_at ^ at) * 2 + y_from
            for rep in range(repeat):
                base = (place * repeat + rep) * block + x_from * 2 * tokens
                start = (dest * repeat + rep) * block + at * tokens
                target = slice(start, start + tokens)
                grad_own[target, :] = grad_keys[
                    pl.ds(pl.multiple_of(base + c_at * tokens, tokens), tokens), :
                ]
                grad_other[target, :] = grad_keys[
                    pl.ds(pl.multiple_of(base + (1 - c_at) * tokens, tokens), tokens), :
                ].astype(BF16)

    def tile_at(rows, half):
        row = (rows % 4) * tokens
        return table_acc[
            1 + rows // 4, row : row + tokens, half * tokens : (half + 1) * tokens
        ]

    spots = [(rows, half) for rows in range(8) for half in range(2)]
    flip = (
        lax.broadcasted_iota(jnp.int32, (tokens, tokens), 0)
        + lax.broadcasted_iota(jnp.int32, (tokens, tokens), 1)
        == tokens - 1
    ).astype(F32)
    far_even = jnp.zeros((tokens, tokens), F32)
    far_odd = jnp.zeros((tokens, tokens), F32)
    for rows, half in spots:
        diff = rows - 4 - 2 * half
        if diff <= -2:
            far_even += tile_at(rows, half)
        if diff - 1 <= -2:
            far_odd += tile_at(rows, half)
    extra = fold_rows(jnp.where(c_at == 0, far_even, far_odd), jnp.sum)
    far_out[...] = fold_rows(table_acc[0], jnp.sum)
    far_out[:, :tokens] += extra
    table_out[...] = jnp.zeros_like(table_out)
    for index, diff in enumerate((-1, 0, 1)):
        even = sum(tile_at(rows, half) for rows, half in spots if rows - 4 - 2 * half == diff)
        odd = sum(tile_at(rows, half) for rows, half in spots if rows - 5 - 2 * half == diff)
        tile = jnp.where(c_at == 0, even, odd)
        turned = jnp.dot(flip, tile, precision=HIGHEST, preferred_element_type=F32)
        wide = jnp.concatenate([turned, jnp.zeros_like(turned)], axis=1)
        wide = pltpu.roll(wide, tokens + 1, 1, stride=1, stride_axis=0)
        table_out[index : index + 1, :] = jnp.sum(wide, axis=0, keepdims=True)


def project_back_body(hd, coords, *refs):
    pieces, (rows_all, weights, gain), out = refs[:4], refs[4:7], refs[7]
    gain_out, pairs_t, queries_t, pairs, queries = refs[8:]
    tokens, width = out.shape[1:]
    z_at = coords[2]
    for dest in range(4):
        lanes = slice(dest * 2 * hd, (dest + 1) * 2 * hd)
        part = pieces[dest][0 : 4 * tokens, :]
        pairs[:, lanes] = part
        pairs_t[lanes, :] = part.T
        for at in range(4):
            queries_t[dest * hd : (dest + 1) * hd, at * tokens : (at + 1) * tokens] = pieces[dest][
                4 * tokens + at * hd : 4 * tokens + (at + 1) * hd, :
            ]
    queries[...] = queries_t[...].T
    grad = nn(pairs[...], weights[0 : 8 * hd, :]) + nn(queries[...], weights[8 * hd :, :])
    unit = rows_all[...].astype(F32) / gain[...]
    gain_out[...] = fold_rows(grad * unit, jnp.sum)
    for at in range(4):
        out[z_at ^ at] = grad[at * tokens : (at + 1) * tokens, :].astype(BF16)


def head_grads_body(hd, coords, pairs_t, queries_t, rows_all, keep, send):
    c_at, y_at = coords[1], coords[3]
    width = rows_all.shape[1]
    half = hd // 2
    normed = rows_all[...]
    pair_rows = nn(pairs_t[...], normed).astype(BF16)
    query_rows = nn(queries_t[...], normed).astype(BF16)
    for dest in range(4):
        other = (y_at ^ (dest & 1)) ^ c_at

        def put(target, dest=dest):
            for part in range(2):
                place = (dest >> 1) * 2 + (y_at ^ part)
                for kind, rows, first in (
                    (0, query_rows, dest * hd),
                    (1, pair_rows, dest * 2 * hd),
                    (2, pair_rows, dest * 2 * hd + hd),
                ):
                    first += part * half
                    target[place, :, kind * width : (kind + 1) * width] = rows[
                        first : first + half, :
                    ]

        pl.when(other == 0)(functools.partial(put, keep))
        pl.when(other == 1)(functools.partial(put, send))


def output_body(hd, coords, *refs):
    arrived, own_in, gain, here, other, middle_out, normed_out, weights, features = refs
    x_at, c_at, z_at, y_at = coords[0], coords[1], coords[2], coords[3]
    half, tokens = hd // 2, arrived.shape[1]
    for core, source in enumerate((here, other)):
        for dest in range(4):
            for near in range(4):
                head = ((x_at ^ (dest >> 1)) * 2 + (c_at ^ core)) * 4 + (z_at ^ near)
                start = pl.multiple_of(head * hd + (y_at ^ (dest & 1)) * half, half)
                first = (dest * 4 + near) * half
                weights[pl.ds(start, half), :] = source[first : first + half, :]
    for dest in range(4):
        for core in range(2):
            for near in range(4):
                head = ((x_at ^ (dest >> 1)) * 2 + (c_at ^ core)) * 4 + (z_at ^ near)
                start = pl.multiple_of(head * hd + (y_at ^ (dest & 1)) * half, half)
                lanes = slice((core * 4 + near) * tokens, (core * 4 + near + 1) * tokens)
                features[dest, :, lanes] = arrived[pl.ds(start, half), :]
    middle = own_in[...].astype(F32) + nn(arrived[...].T, weights[...])
    middle_out[...] = middle
    normed_out[...] = (middle * norm_scale(middle) * gain[...]).astype(BF16)


def finish_body(*refs):
    parts, own_in, grad_middle, gain, out = refs
    values = own_in[...].astype(F32)
    grad = sum(parts[at].astype(F32) for at in range(4))
    out[...] = (
        grad_middle[...] + norm_back(values, norm_scale(values), gain[...], grad)
    ).astype(BF16)


def gated(gate_act, up_act):
    return jax.nn.gelu(gate_act, approximate=True) * up_act


def body(
    inputs,
    cotangent,
    segment_ids,
    bucket_table,
    gain_attention,
    query_weight,
    key_weight,
    value_weight,
    output_weight,
    bucket_bias,
    gain_feedforward,
    gate_weight,
    up_weight,
    down_weight,
):
    tokens, width = inputs.shape[1:]
    repeat = lax.axis_size("r")
    x_at, c_at, z_at, y_at, r_at = (lax.axis_index(name) for name in EVERY)
    coords = jnp.stack([x_at, c_at, z_at, y_at, r_at]).astype(jnp.int32)
    bucket_count, head_count = bucket_bias.shape
    hd = width // head_count
    block = 4 * tokens
    length = segment_ids.size
    reach = (bucket_table.shape[0] - 1) // 2
    assert reach == tokens and lax.axis_size("x") == lax.axis_size("c") == 2

    cot_own = cotangent[0]
    out_rows = output_weight
    if repeat > 1:
        out_rows = lax.all_gather(out_rows, "r", axis=0, tiled=True)
    message, joined, units = kernel_call(
        pack_body,
        [
            shape((tokens + hd // 2, width), BF16),
            shape((query_weight.shape[0], 3 * width), BF16),
            shape((gate_weight.shape[0], 3 * width), BF16),
        ],
        [
            inputs[0],
            gain_attention.reshape(1, width),
            out_rows,
            query_weight,
            key_weight,
            value_weight,
            gate_weight,
            up_weight,
            down_weight,
        ],
        scalars=0,
        micros=2,
    )
    messages = from_group(message, "z")
    if repeat > 1:
        joined = lax.all_gather(joined, "r", axis=0, tiled=True)
    head_rows = from_group(joined, SQUARE)
    other_rows = swap(jnp.concatenate(head_rows, axis=0), "c", 1)

    windows = segment_ids.reshape(-1, 2 * tokens)
    cuts = jnp.sum((windows < windows[:, -1:]).astype(jnp.int32), axis=1)
    turned = bucket_table[::-1]
    low_half, high_half = turned[reach : 2 * reach], turned[:reach]
    spots = jnp.concatenate(
        [
            jnp.broadcast_to(bucket_table[:1], (reach,)),
            low_half,
            low_half,
            high_half,
            high_half,
            jnp.broadcast_to(bucket_table[2 * reach :], (reach,)),
        ]
    )
    buckets = jnp.arange(bucket_count, dtype=jnp.int32)
    onehot = (spots[:, None] == buckets[None, :]).astype(F32)
    far_onehot = (bucket_table[0] == buckets).astype(F32)
    head_at = (x_at * 2 + y_at) * 4 + z_at
    bias_col = lax.dynamic_slice_in_dim(bucket_bias, head_at, 1, 1)[:, 0]
    diag = jnp.dot(onehot, bias_col, precision=HIGHEST) - jnp.sum(far_onehot * bias_col)
    hvec = jnp.pad(diag.reshape(3, 2 * reach), ((0, 5), (0, 0)))

    messages, hvec, cuts, coords, units = lax.optimization_barrier(
        (messages, hvec, cuts, coords, units)
    )
    unit_rows = lax.all_gather(units, UNITS_GROUP, axis=0, tiled=True)
    gate_piece, up_piece, down_piece = (
        unit_rows[:, at * width : (at + 1) * width] for at in range(3)
    )

    made = kernel_call(
        functools.partial(qkv_body, hd),
        [shape((block + 4 * hd, 2 * hd), BF16)] * 4
        + [
            shape((block, width), BF16),
            shape((12 * hd, width), BF16),
            shape((tokens + 2 * hd, width), BF16),
        ],
        [coords, *messages, *head_rows, other_rows, cot_own, anchor(messages, 30)],
    )
    pieces, (normed_all, group_weights, sent) = made[:4], made[4:]
    pieces = to_group(pieces, SQUARE)

    own = [piece[:block] for piece in pieces]
    other = swap(jnp.concatenate(own, axis=0), "c", 1)
    if repeat == 1:
        arrays = [*pieces, other]
    else:
        own = [lax.all_gather(part, "r", axis=0, tiled=True) for part in own]
        other = other.reshape(4, block, 2 * hd)
        other = [lax.all_gather(other[at], "r", axis=0, tiled=True) for at in range(4)]
        arrays = [*pieces, *own, jnp.concatenate(other, axis=0)]
    places = 8
    out_t, lse, attended, keys, keys_t, queries = kernel_call(
        functools.partial(attend_body, tokens, hd, repeat),
        [
            shape((16, hd, tokens), BF16),
            shape((places, 8, 2 * tokens), F32),
            shape((places, hd, 2 * tokens), F32),
            shape((length, 2 * hd), BF16),
            shape((length // block, 2 * hd, block), BF16),
            shape((places, hd, 2 * tokens), BF16),
        ],
        [coords, cuts, hvec, *arrays],
        [
            pltpu.VMEM((9 * repeat, block, 2 * tokens), F32),
            pltpu.VMEM((places + 2, block, 2 * tokens), F32),
            pltpu.VMEM((places, 2 * hd, 2 * tokens), BF16),
            pltpu.VMEM((2, 8, 2 * tokens), F32),
            pltpu.VMEM((2, 8, 2 * tokens), F32),
            pltpu.VMEM((2, hd, 2 * tokens), F32),
        ],
        scalars=2,
        micros=20,
    )
    sent, _ = lax.optimization_barrier((sent, pieces))
    parts = from_group(sent, SQUARE)
    arrived = lax.all_to_all(out_t, ("x", "y", "z"), split_axis=0, concat_axis=0, tiled=True)
    parts, arrived = lax.optimization_barrier((parts, arrived))
    cot_all = jnp.concatenate([part[:tokens] for part in parts], axis=0)
    out_here = jnp.concatenate([part[tokens:] for part in parts], axis=0)
    out_other = swap(out_here, "c", 1)

    middle, normed_mid, out_full, features = kernel_call(
        functools.partial(output_body, hd),
        [
            shape((tokens, width), F32),
            shape((tokens, width), BF16),
            shape((width, width), BF16),
            shape((4, hd // 2, 8 * tokens), BF16),
        ],
        [
            coords,
            arrived.reshape(width, tokens),
            inputs[0],
            gain_feedforward.reshape(1, width),
            out_here,
            out_other,
        ],
    )
    scale_second = norm_scale(middle)
    mid_all = jnp.concatenate(from_group(normed_mid, SQUARE), axis=0)

    gate_act = nt(mid_all, gate_piece)
    up_act = nt(mid_all, up_piece)
    hidden_val, pullback = jax.vjp(gated, gate_act, up_act)
    hidden = hidden_val.astype(BF16)
    grad_gate, grad_up = pullback(nt(cot_all, down_piece))
    gate_low, up_low = grad_gate.astype(BF16), grad_up.astype(BF16)
    grad_norm = (nn(gate_low, gate_piece) + nn(up_low, up_piece)).astype(BF16)
    grad_parts = to_group(
        [grad_norm[at * tokens : (at + 1) * tokens] for at in range(4)], SQUARE
    )
    unit_grads = jnp.concatenate(
        [tn(gate_low, mid_all), tn(up_low, mid_all), tn(hidden, cot_all)], axis=1
    ).astype(BF16)
    feed = nn(hidden, down_piece).astype(BF16)
    grad_parts, unit_grads, feed = lax.optimization_barrier((grad_parts, unit_grads, feed))
    grad_norm_mid = sum(part.astype(F32) for part in grad_parts)

    grad_middle = cot_own.astype(F32) + norm_back(
        middle, scale_second, gain_feedforward, grad_norm_mid
    )
    gain_second_term = jnp.sum(grad_norm_mid * middle * scale_second, axis=0)
    grad_mid_low = grad_middle.astype(BF16)
    grad_attended = nt(out_full, grad_mid_low).astype(BF16)
    grad_arrived = lax.all_to_all(
        grad_attended.reshape(16, hd, tokens),
        ("x", "y", "z"),
        split_axis=0,
        concat_axis=0,
        tiled=True,
    )
    grad_arrived, grad_mid_low, unit_grads = lax.optimization_barrier(
        (grad_arrived, grad_mid_low, unit_grads)
    )
    grad_units = lax.psum_scatter(unit_grads, UNITS_GROUP, scatter_dimension=0, tiled=True)
    mixed = to_group(
        [
            jnp.concatenate(
                [
                    feed[at * tokens : (at + 1) * tokens],
                    grad_mid_low,
                    features[at],
                ]
            )
            for at in range(4)
        ],
        SQUARE,
    )

    grad_own, grad_other, grad_q, table_out, far_out = kernel_call(
        functools.partial(attend_back_body, tokens, hd, repeat),
        [
            shape((4 * repeat * block, 2 * hd), F32),
            shape((4 * repeat * block, 2 * hd), BF16),
            shape((16, hd, tokens), BF16),
            shape((8, 2 * tokens), F32),
            shape((8, 2 * tokens), F32),
        ],
        [coords, cuts, hvec, grad_arrived, queries, keys, keys_t, attended, lse],
        [
            pltpu.VMEM((places + 2, block, 2 * tokens), F32),
            pltpu.VMEM((length, 2 * hd), F32),
            pltpu.VMEM((3, block, 2 * tokens), F32),
            pltpu.VMEM((places, 2 * hd, 4 * tokens), BF16),
            pltpu.VMEM((places, 4 * tokens, 2 * hd), BF16),
            pltpu.VMEM((places, 16, 2 * tokens), F32),
            pltpu.VMEM((2, hd, 2 * tokens), F32),
        ],
        scalars=2,
        micros=20,
    )
    mixed, grad_own = lax.optimization_barrier((mixed, grad_own))
    grad_pairs = (grad_own + swap(grad_other, "c", 1).astype(F32)).astype(BF16)
    grad_pairs = [
        grad_pairs[at * repeat * block : (at + 1) * repeat * block] for at in range(4)
    ]
    if repeat > 1:
        grad_pairs = [
            lax.psum_scatter(part, "r", scatter_dimension=0, tiled=True) for part in grad_pairs
        ]
    grad_pieces = [
        jnp.concatenate([grad_pairs[at], grad_q[4 * at : 4 * at + 4].reshape(4 * hd, tokens)])
        for at in range(4)
    ]
    mixed, grad_pieces = lax.optimization_barrier((mixed, grad_pieces))
    grad_pieces = to_group(grad_pieces, SQUARE)

    made = kernel_call(
        functools.partial(project_back_body, hd),
        [
            shape((4, tokens, width), BF16),
            shape((8, width), F32),
            shape((8 * hd, block), BF16),
            shape((4 * hd, block), BF16),
        ],
        [coords, *grad_pieces, normed_all, group_weights, gain_attention.reshape(1, width)],
        [pltpu.VMEM((block, 8 * hd), BF16), pltpu.VMEM((block, 4 * hd), BF16)],
        mebi=16,
    )
    normed_grads, gain_first_rows, pairs_t, queries_t = made
    normed_grads = lax.all_to_all(normed_grads, "z", split_axis=0, concat_axis=0, tiled=True)
    keep, send = kernel_call(
        functools.partial(head_grads_body, hd),
        [shape((4, hd // 2, 3 * width), BF16)] * 2,
        [coords, pairs_t, queries_t, normed_all],
    )
    layer_out = (middle + sum(part[:tokens].astype(F32) for part in mixed)).astype(BF16)
    grad_mid_all = jnp.concatenate([part[tokens : 2 * tokens] for part in mixed], axis=0)
    near = jnp.stack([part[2 * tokens :] for part in mixed]).reshape(4, hd // 2, 8, tokens)
    near = near.transpose(2, 1, 0, 3).reshape(4 * hd, block)
    out_grads = nn(near, grad_mid_all).astype(BF16)

    table_out, far_out, keep, send, grad_units, out_grads = lax.optimization_barrier(
        (table_out, far_out, keep, send, grad_units, out_grads)
    )
    out_grads = out_grads.reshape(2, 4, hd // 2, width)
    out_grads = (out_grads[0].astype(F32) + swap(out_grads[1], "c", 1).astype(F32)).astype(BF16)
    head_grads = (keep.astype(F32) + swap(send, "c", 1).astype(F32)).astype(BF16)
    bucket_grad = jnp.dot(table_out[:3].reshape(1, -1), onehot, precision=HIGHEST)[0]
    bucket_grad = bucket_grad + far_onehot * jnp.sum(far_out)
    head_mark = (jnp.arange(head_count) == head_at).astype(F32)
    bias_term = bucket_grad[:, None] * head_mark[None, :]
    sums = jnp.concatenate([jnp.sum(gain_first_rows, axis=0), gain_second_term, bias_term.ravel()])
    sums = sums + swap(sums, "c", 1)
    sums = sum_everywhere(sums, SQUARE)
    head_grads = to_group([head_grads[at] for at in range(4)], SQUARE)
    normed_grads, head_grads, sums, out_grads = lax.optimization_barrier(
        (normed_grads, head_grads, sums, out_grads)
    )
    out_grads, sums = sum_over_z(out_grads, sums)
    head_grads = sum(part.astype(F32) for part in head_grads)
    if repeat > 1:
        sums = lax.psum(sums, "r")
        out_grads = lax.psum_scatter(
            out_grads.astype(BF16), "r", scatter_dimension=0, tiled=True
        ).astype(F32)
        head_grads = lax.psum_scatter(
            head_grads.astype(BF16), "r", scatter_dimension=0, tiled=True
        ).astype(F32)
    gain_first_grad, gain_second_grad = sums[:width], sums[width : 2 * width]
    bias_grad = sums[2 * width :].reshape(bucket_count, head_count)

    grad_inputs = kernel_call(
        finish_body,
        shape((tokens, width), BF16),
        [normed_grads, inputs[0], grad_middle, gain_attention.reshape(1, width)],
        scalars=0,
        micros=100,
        mebi=16,
    )
    unit_grads = grad_units.astype(F32)
    return (
        layer_out[None],
        grad_inputs[None],
        gain_first_grad,
        head_grads[:, :width],
        head_grads[:, width : 2 * width],
        head_grads[:, 2 * width :],
        out_grads,
        bias_grad,
        gain_second_grad,
        unit_grads[:, :width],
        unit_grads[:, width : 2 * width],
        unit_grads[:, 2 * width :],
    )


def solution(mesh):
    owners, runs = mesh.shape["ulysses"], mesh.shape["blk"]
    fine = Mesh(mesh.devices.reshape(2, owners // 2, 4, 2, runs // 8), EVERY)
    tokens = P(("z", "y", "r"), ("x", "c"), None)
    rows = P(EVERY, None)
    return jax.shard_map(
        body,
        mesh=fine,
        in_specs=(tokens, tokens) + (P(),) * 3 + (rows,) * 4 + (P(),) * 2 + (rows,) * 3,
        out_specs=(tokens, tokens, P()) + (rows,) * 4 + (P(),) * 2 + (rows,) * 3,
        check_vma=False,
    )
```

```python
import functools
import math

import jax
import jax.numpy as jnp
from jax import lax
from jax.experimental import pallas as pl
from jax.experimental.pallas import tpu as pltpu
from jax.sharding import Mesh
from jax.sharding import PartitionSpec as P

EPSILON = 1e-06
NEGATIVE = -1e30
HIGHEST = lax.Precision.HIGHEST
F32 = jnp.float32
BF16 = jnp.bfloat16
MEBI = 1024 * 1024
FEED_MEBI = 24
GELU_SCALE = math.sqrt(2.0 / math.pi)
GELU_CUBE = 0.044715
SQUARE = ("x", "y")
UNITS_GROUP = ("z", "c", "r")
EVERY = ("x", "c", "z", "y", "r")


def norm_scale(values):
    return lax.rsqrt(jnp.mean(values * values, axis=-1, keepdims=True) + EPSILON)


def norm_back(values, scaling, gain_vec, upstream):
    inner_sum = jnp.mean(values * gain_vec * upstream, axis=-1, keepdims=True)
    return scaling * gain_vec * upstream - values * scaling * scaling * scaling * inner_sum


def nt(left, right):
    return lax.dot_general(left, right, (((1,), (1,)), ((), ())), preferred_element_type=F32)


def nn(left, right):
    return lax.dot_general(left, right, (((1,), (0,)), ((), ())), preferred_element_type=F32)


def tn(left, right):
    return lax.dot_general(left, right, (((0,), (0,)), ((), ())), preferred_element_type=F32)


def swap(value, axis, mask):
    size = lax.axis_size(axis)
    return lax.ppermute(value, axis, [(at, at ^ mask) for at in range(size)])


def from_group(value, axis):
    return [value] + [swap(value, axis, mask) for mask in (1, 2, 3)]


def to_group(values, axis):
    return [values[0]] + [swap(values[mask], axis, mask) for mask in (1, 2, 3)]


def sum_everywhere(value, axis):
    first, second, third, fourth = from_group(value, axis)
    return (first + second) + (third + fourth)


def sum_over_z(rows, values):
    width = rows.shape[-1]
    lines = -(-values.size // width)
    padded = jnp.pad(values, (0, lines * width - values.size)).reshape(lines, width)
    high = lax.reduce_precision(padded, 8, 7)
    extra = jnp.concatenate([high, padded - high]).astype(BF16)
    extra = jnp.pad(extra, ((0, -2 * lines % 8), (0, 0)))
    arrived = to_group([jnp.concatenate([rows[at], extra]) for at in range(4)], "z")
    arrived = [part.astype(F32) for part in arrived]
    count = rows.shape[1]
    tails = [part[count : count + lines] + part[count + lines : count + 2 * lines] for part in arrived]
    total = (tails[0] + tails[1]) + (tails[2] + tails[3])
    return sum(part[:count] for part in arrived), total.ravel()[: values.size]


def kernel_call(body, out_shapes, inputs, scratch=(), scalars=1, micros=4, mebi=60):
    in_specs = [pl.BlockSpec(memory_space=pltpu.SMEM)] * scalars
    in_specs += [pl.BlockSpec(memory_space=pltpu.VMEM)] * (len(inputs) - scalars)
    return pl.pallas_call(
        body,
        out_shape=out_shapes,
        in_specs=in_specs,
        out_specs=jax.tree.map(lambda _: pl.BlockSpec(memory_space=pltpu.VMEM), out_shapes),
        scratch_shapes=list(scratch),
        compiler_params=pltpu.CompilerParams(vmem_limit_bytes=mebi * MEBI),
        cost_estimate=pl.CostEstimate(
            flops=int(micros * 1.15e9), bytes_accessed=1 << 20, transcendentals=0
        ),
    )(*inputs)


def shape(dims, dtype):
    return jax.ShapeDtypeStruct(dims, dtype)


def pack_body(*refs):
    own_in, gain, out_rows = refs[:3]
    heads, units = refs[3:6], refs[6:9]
    message, joined, joined_units = refs[9:]
    tokens, width = own_in.shape
    values = own_in[...].astype(F32)
    message[0:tokens, :] = (values * norm_scale(values) * gain[...]).astype(BF16)
    message[tokens:, :] = out_rows[...]
    for at in range(3):
        joined[:, at * width : (at + 1) * width] = heads[at][...]
        joined_units[:, at * width : (at + 1) * width] = units[at][...]


def anchor_body(*refs):
    refs[-1][...] = jnp.zeros_like(refs[-1])


def anchor(values, micros):
    return pl.pallas_call(
        anchor_body,
        out_shape=shape((8, 128), F32),
        in_specs=[pl.BlockSpec(memory_space=pl.ANY)] * len(values),
        out_specs=pl.BlockSpec(memory_space=pltpu.VMEM),
        cost_estimate=pl.CostEstimate(
            flops=int(micros * 1.15e9), bytes_accessed=1 << 20, transcendentals=0
        ),
    )(*values)


def qkv_body(hd, coords, *refs):
    blocks, parts, other_rows, cot_own, pieces = refs[:4], refs[4:8], refs[8], refs[9], refs[11:15]
    rows_all, weights, onward = refs[15:18]
    c_at, y_at = coords[1], coords[3]
    width, half = rows_all.shape[1], hd // 2
    tokens = rows_all.shape[0] // 4
    for at in range(4):
        rows_all[at * tokens : (at + 1) * tokens, :] = blocks[at][0:tokens, :]
        start = tokens + at * half
        onward[start : start + half, :] = blocks[at][tokens:, :]
    onward[0:tokens, :] = cot_own[...]
    for core in range(2):
        for dest in range(4):
            column = y_at ^ c_at ^ core
            place = (dest >> 1) * 2 + column
            shift = pl.multiple_of((y_at ^ (dest & 1)) * half, half)
            source = other_rows.at[dest * half : (dest + 1) * half] if core else parts[dest]
            for kind, first, step in ((0, 8 * hd, hd), (1, 0, 2 * hd), (2, hd, 2 * hd)):
                start = pl.multiple_of(first + place * step + shift, half)
                weights[pl.ds(start, half), :] = source[:, kind * width : (kind + 1) * width]
    normed = rows_all[...]
    pairs = nt(normed, weights[0 : 8 * hd, :]).astype(BF16)
    queries = nt(weights[8 * hd : 12 * hd, :], normed).astype(BF16)
    for dest in range(4):
        pieces[dest][0 : 4 * tokens, :] = pairs[:, dest * 2 * hd : (dest + 1) * 2 * hd]
        for at in range(4):
            pieces[dest][4 * tokens + at * hd : 4 * tokens + (at + 1) * hd, :] = queries[
                dest * hd : (dest + 1) * hd, at * tokens : (at + 1) * tokens
            ]


def bias_tiles(hvec, tokens):
    tiles = {}
    for at, diff in enumerate((-1, 0, 1)):
        spread = jnp.broadcast_to(hvec[at : at + 1, :], (tokens, 2 * tokens))
        tiles[diff] = pltpu.roll(spread, 0, 1, stride=1, stride_axis=0)[:, :tokens]
    return tiles


def fill_bias(hvec_ref, bias, cuts, repeat, c_at, r_at, tokens):
    tiles = bias_tiles(hvec_ref[...], tokens)
    zero = jnp.zeros((tokens, tokens), F32)
    bias[0] = jnp.zeros(bias.shape[1:], F32)
    for rows in range(8):
        for half in range(2):
            diff = rows - 4 - 2 * half
            even, odd = tiles.get(diff, zero), tiles.get(diff - 1, zero)
            row = (rows % 4) * tokens
            bias[1 + rows // 4, row : row + tokens, half * tokens : (half + 1) * tokens] = (
                jnp.where(c_at == 0, even, odd)
            )

    def mask(back, carry):
        place = bias.shape[0] - 3 - back
        allowed = allowed_mask(cuts, place * repeat + r_at, c_at, tokens)
        bias[2 + place] = jnp.where(allowed, bias[2], NEGATIVE)
        return carry

    lax.fori_loop(0, bias.shape[0] - 2, mask, 0)


def bias_slab(bias, place, run, at):
    return bias[jnp.where(at == run, 2 + place, jnp.where(at == run - 1, 1, 0))]


def allowed_mask(cuts, run, c_at, tokens):
    rows, cols = 4 * tokens, 2 * tokens
    key_at = lax.broadcasted_iota(jnp.int32, (rows, cols), 0)
    query_at = lax.broadcasted_iota(jnp.int32, (rows, cols), 1)
    key_window = key_at >= 2 * tokens
    query_window = query_at >= tokens
    key_in = jnp.where(key_window, key_at - 2 * tokens, key_at)
    query_in = jnp.where(query_window, query_at - tokens, query_at) + c_at * tokens
    cut = jnp.where(query_window, cuts[2 * run + 1], cuts[2 * run])
    inside = (key_in < cut) | (query_in >= cut)
    before = jnp.logical_and(jnp.logical_not(key_window), query_window)
    same = key_window == query_window
    return before | (same & inside)


def each_slot(run_low, run_high, repeat, step):
    def one(slot, carry):
        high = (slot > run_low).astype(jnp.int32)
        at = jnp.where(slot > run_low, slot - run_low - 1, slot)
        step(slot, high, at)
        return carry

    count = run_low + run_high + 2
    if repeat == 1:
        for slot in range(9):
            one(jnp.int32(slot), 0)
    else:
        lax.fori_loop(0, count, one, 0)


def chunk(at, block):
    return pl.ds(pl.multiple_of(at * block, block), block)


def fold_rows(values, how):
    rows, cols = values.shape
    return how(values.reshape(rows // 8, 8, cols), axis=0)


def attend_body(tokens, hd, repeat, coords, cuts, hvec, *refs):
    pieces = refs[:4]
    own, other, refs = (pieces, *refs[4:5], refs[5:]) if repeat == 1 else (refs[4:8], refs[8], refs[9:])
    out, lse, attended, keys, keys_t, queries, scores, bias, padded, peaks, totals, mixes = refs
    x_at, c_at, z_at, y_at, r_at = (coords[at] for at in range(5))
    block = 4 * tokens
    for dest in range(4):
        x_from, y_from = x_at ^ (dest >> 1), y_at ^ (dest & 1)
        for at in range(4):
            place = (z_at ^ at) * 2 + y_from
            for rep in range(repeat):
                run = place * repeat + rep
                base = run * block + x_from * 2 * tokens
                source = slice(rep * block + at * tokens, rep * block + (at + 1) * tokens)
                keys[pl.ds(pl.multiple_of(base + c_at * tokens, tokens), tokens), :] = own[dest][
                    source, :
                ]
                start = (dest * repeat + rep) * block + at * tokens
                keys[pl.ds(pl.multiple_of(base + (1 - c_at) * tokens, tokens), tokens), :] = other[
                    start : start + tokens, :
                ]
            start = block + at * hd
            queries[place, :, pl.ds(pl.multiple_of(x_from * tokens, tokens), tokens)] = pieces[
                dest
            ][start : start + hd, :]
    fill_bias(hvec, bias, cuts, repeat, c_at, r_at, tokens)

    def turn(at, carry):
        keys_t[at] = keys[chunk(at, block), :].T
        return carry

    lax.fori_loop(0, keys.shape[0] // block, turn, 0)
    places = queries.shape[0]
    padded[:, 0:hd, :] = queries[...]
    padded[:, hd:, :] = jnp.zeros_like(padded[:, hd:, :])

    def pair(low, carry):
        place_of = (low, places - 1 - low)
        run_of = tuple(place * repeat + r_at for place in place_of)
        peaks[...] = jnp.full_like(peaks, NEGATIVE)
        totals[...] = jnp.zeros_like(totals)
        mixes[...] = jnp.zeros_like(mixes)

        def score(slot, high, at):
            place = jnp.where(high == 1, place_of[1], place_of[0])
            run = place * repeat + r_at
            values = nn(keys[chunk(at, block), :], padded[place])
            values = values + bias_slab(bias, place, run, at)
            scores[slot] = values
            peaks[high] = jnp.maximum(peaks[high], fold_rows(values, jnp.max))

        each_slot(*run_of, repeat, score)
        for high in range(2):
            top = jnp.max(peaks[high], axis=0, keepdims=True)
            peaks[high] = jnp.broadcast_to(top, peaks.shape[1:])

        def mix(slot, high, at):
            weights = jnp.exp(scores[slot] - peaks[high][0:1, :])
            totals[high] += fold_rows(weights, jnp.sum)
            mixes[high] += nn(keys_t[at, hd:, :], weights.astype(BF16))

        each_slot(*run_of, repeat, mix)
        for high, place in enumerate(place_of):
            total = jnp.sum(totals[high], axis=0, keepdims=True)
            mixed = mixes[high] / total
            attended[place] = mixed
            lse[place] = peaks[high] + jnp.log(jnp.broadcast_to(total, peaks.shape[1:]))
            part = mixed.astype(BF16)
            for half in range(2):
                out[half * 8 + (place & 1) * 4 + (place >> 1)] = part[
                    :, half * tokens : (half + 1) * tokens
                ]
        return carry

    lax.fori_loop(0, places // 2, pair, 0)


def attend_back_body(tokens, hd, repeat, coords, cuts, hvec, *refs):
    arrived, queries, keys, keys_t, attended, lse = refs[:6]
    grad_own, grad_other, grad_q, table_out, far_out = refs[6:11]
    bias, grad_keys, table_acc, left, right, shifts, grad_queries = refs[11:]
    x_at, c_at, z_at, y_at, r_at = (coords[at] for at in range(5))
    block = 4 * tokens
    places = queries.shape[0]
    fill_bias(hvec, bias, cuts, repeat, c_at, r_at, tokens)
    grad_keys[...] = jnp.zeros_like(grad_keys)
    table_acc[...] = jnp.zeros_like(table_acc)

    def prepare(place, carry):
        query_t = queries[place]
        upstream_t = jnp.concatenate(
            [arrived[half * 8 + (place & 1) * 4 + (place >> 1)] for half in range(2)], axis=1
        )
        zero = jnp.zeros_like(query_t)
        query_pad = jnp.concatenate([query_t, zero], axis=0)
        upstream_pad = jnp.concatenate([zero, upstream_t], axis=0)
        left[place, :, 0 : 2 * tokens] = query_pad
        left[place, :, 2 * tokens :] = upstream_pad
        right[place, 0 : 2 * tokens, :] = query_pad.T
        right[place, 2 * tokens :, :] = upstream_pad.T
        shifts[place, 0:8, :] = lse[place]
        delta = jnp.sum(upstream_t.astype(F32) * attended[place], axis=0, keepdims=True)
        shifts[place, 8:16, :] = jnp.broadcast_to(delta, (8, 2 * tokens))
        return carry

    lax.fori_loop(0, places, prepare, 0)

    def pair(low, carry):
        place_of = (low, places - 1 - low)
        run_of = tuple(place * repeat + r_at for place in place_of)
        grad_queries[...] = jnp.zeros_like(grad_queries)

        def step(slot, high, at):
            place = jnp.where(high == 1, place_of[1], place_of[0])
            run = place * repeat + r_at
            rows = chunk(at, block)
            both = nn(keys[rows, :], left[place])
            values = both[:, 0 : 2 * tokens] + bias_slab(bias, place, run, at)
            probs = jnp.exp(values - shifts[place, 0:1, :])
            grad_scores = probs * (both[:, 2 * tokens :] - shifts[place, 8:9, :])
            grad_low = grad_scores.astype(BF16)
            grad_keys[rows, :] += nn(
                jnp.concatenate([grad_low, probs.astype(BF16)], axis=1), right[place]
            )
            grad_queries[high] += nn(keys_t[at, :hd, :], grad_low)
            kind = jnp.where(at == run, 2, jnp.where(at == run - 1, 1, 0))
            table_acc[kind] += grad_low.astype(F32)

        each_slot(*run_of, repeat, step)
        for high, place in enumerate(place_of):
            low_part = grad_queries[high].astype(BF16)
            for half in range(2):
                part = low_part[:, half * tokens : (half + 1) * tokens]
                dest = (x_at ^ half) * 2 + ((place & 1) ^ y_at)
                grad_q[dest * 4 + ((place >> 1) ^ z_at)] = part
        return carry

    lax.fori_loop(0, places // 2, pair, 0)

    for dest in range(4):
        x_from, y_from = x_at ^ (dest >> 1), y_at ^ (dest & 1)
        for at in range(4):
            place = (z_at ^ at) * 2 + y_from
            for rep in range(repeat):
                base = (place * repeat + rep) * block + x_from * 2 * tokens
                start = (dest * repeat + rep) * block + at * tokens
                target = slice(start, start + tokens)
                grad_own[target, :] = grad_keys[
                    pl.ds(pl.multiple_of(base + c_at * tokens, tokens), tokens), :
                ]
                grad_other[target, :] = grad_keys[
                    pl.ds(pl.multiple_of(base + (1 - c_at) * tokens, tokens), tokens), :
                ].astype(BF16)

    def tile_at(rows, half):
        row = (rows % 4) * tokens
        return table_acc[
            1 + rows // 4, row : row + tokens, half * tokens : (half + 1) * tokens
        ]

    spots = [(rows, half) for rows in range(8) for half in range(2)]
    flip = (
        lax.broadcasted_iota(jnp.int32, (tokens, tokens), 0)
        + lax.broadcasted_iota(jnp.int32, (tokens, tokens), 1)
        == tokens - 1
    ).astype(F32)
    far_even = jnp.zeros((tokens, tokens), F32)
    far_odd = jnp.zeros((tokens, tokens), F32)
    for rows, half in spots:
        diff = rows - 4 - 2 * half
        if diff <= -2:
            far_even += tile_at(rows, half)
        if diff - 1 <= -2:
            far_odd += tile_at(rows, half)
    extra = fold_rows(jnp.where(c_at == 0, far_even, far_odd), jnp.sum)
    far_out[...] = fold_rows(table_acc[0], jnp.sum)
    far_out[:, :tokens] += extra
    table_out[...] = jnp.zeros_like(table_out)
    for index, diff in enumerate((-1, 0, 1)):
        even = sum(tile_at(rows, half) for rows, half in spots if rows - 4 - 2 * half == diff)
        odd = sum(tile_at(rows, half) for rows, half in spots if rows - 5 - 2 * half == diff)
        tile = jnp.where(c_at == 0, even, odd)
        turned = jnp.dot(flip, tile, precision=HIGHEST, preferred_element_type=F32)
        wide = jnp.concatenate([turned, jnp.zeros_like(turned)], axis=1)
        wide = pltpu.roll(wide, tokens + 1, 1, stride=1, stride_axis=0)
        table_out[index : index + 1, :] = jnp.sum(wide, axis=0, keepdims=True)


def project_back_body(hd, coords, *refs):
    pieces, (rows_all, weights, gain), out = refs[:4], refs[4:7], refs[7]
    gain_out, pairs_t, queries_t, pairs, queries = refs[8:]
    tokens, width = out.shape[1:]
    z_at = coords[2]
    for dest in range(4):
        lanes = slice(dest * 2 * hd, (dest + 1) * 2 * hd)
        part = pieces[dest][0 : 4 * tokens, :]
        pairs[:, lanes] = part
        pairs_t[lanes, :] = part.T
        for at in range(4):
            queries_t[dest * hd : (dest + 1) * hd, at * tokens : (at + 1) * tokens] = pieces[dest][
                4 * tokens + at * hd : 4 * tokens + (at + 1) * hd, :
            ]
    queries[...] = queries_t[...].T
    grad = nn(pairs[...], weights[0 : 8 * hd, :]) + nn(queries[...], weights[8 * hd :, :])
    unit = rows_all[...].astype(F32) / gain[...]
    gain_out[...] = fold_rows(grad * unit, jnp.sum)
    for at in range(4):
        out[z_at ^ at] = grad[at * tokens : (at + 1) * tokens, :].astype(BF16)


def head_grads_body(hd, coords, pairs_t, queries_t, rows_all, keep, send):
    c_at, y_at = coords[1], coords[3]
    width = rows_all.shape[1]
    half = hd // 2
    normed = rows_all[...]
    pair_rows = nn(pairs_t[...], normed).astype(BF16)
    query_rows = nn(queries_t[...], normed).astype(BF16)
    for dest in range(4):
        other = (y_at ^ (dest & 1)) ^ c_at

        def put(target, dest=dest):
            for part in range(2):
                place = (dest >> 1) * 2 + (y_at ^ part)
                for kind, rows, first in (
                    (0, query_rows, dest * hd),
                    (1, pair_rows, dest * 2 * hd),
                    (2, pair_rows, dest * 2 * hd + hd),
                ):
                    first += part * half
                    target[place, :, kind * width : (kind + 1) * width] = rows[
                        first : first + half, :
                    ]

        pl.when(other == 0)(functools.partial(put, keep))
        pl.when(other == 1)(functools.partial(put, send))


def output_body(hd, coords, *refs):
    arrived, own_in, gain, here, other, middle_out, normed_out, weights, features = refs
    x_at, c_at, z_at, y_at = coords[0], coords[1], coords[2], coords[3]
    half, tokens = hd // 2, arrived.shape[1]
    for core, source in enumerate((here, other)):
        for dest in range(4):
            for near in range(4):
                head = ((x_at ^ (dest >> 1)) * 2 + (c_at ^ core)) * 4 + (z_at ^ near)
                start = pl.multiple_of(head * hd + (y_at ^ (dest & 1)) * half, half)
                first = (dest * 4 + near) * half
                weights[pl.ds(start, half), :] = source[first : first + half, :]
    for dest in range(4):
        for core in range(2):
            for near in range(4):
                head = ((x_at ^ (dest >> 1)) * 2 + (c_at ^ core)) * 4 + (z_at ^ near)
                start = pl.multiple_of(head * hd + (y_at ^ (dest & 1)) * half, half)
                lanes = slice((core * 4 + near) * tokens, (core * 4 + near + 1) * tokens)
                features[dest, :, lanes] = arrived[pl.ds(start, half), :]
    middle = own_in[...].astype(F32) + nn(arrived[...].T, weights[...])
    middle_out[...] = middle
    normed_out[...] = (middle * norm_scale(middle) * gain[...]).astype(BF16)


def finish_body(*refs):
    parts, own_in, grad_middle, gain, out = refs
    values = own_in[...].astype(F32)
    grad = sum(parts[at].astype(F32) for at in range(4))
    out[...] = (
        grad_middle[...] + norm_back(values, norm_scale(values), gain[...], grad)
    ).astype(BF16)


def feed_body(count, *refs):
    blocks, cot, rows = refs[:count], refs[count], refs[count + 1]
    outs = refs[-5 - count : -5]
    mid_out, gate_out, up_out, hidden_out, acc = refs[-5:]
    tokens, width = blocks[0].shape
    for at in range(count):
        mid_out[at * tokens : (at + 1) * tokens, :] = blocks[at][...]
    units = rows.shape[0]
    for start in range(0, units, 256):
        part = slice(start, min(start + 256, units))
        gate_rows = rows[part, 0:width]
        up_rows = rows[part, width : 2 * width]
        gate_act = nt(mid_out[...], gate_rows)
        up_act = nt(mid_out[...], up_rows)
        upstream = nt(cot[...], rows[part, 2 * width :])
        square = gate_act * gate_act
        curve = jnp.tanh(GELU_SCALE * gate_act * (1.0 + GELU_CUBE * square))
        half = 0.5 + 0.5 * curve
        gelu = gate_act * half
        slope = half + (0.5 * GELU_SCALE) * gate_act * (1.0 - curve * curve) * (
            1.0 + 3.0 * GELU_CUBE * square
        )
        hidden_out[:, part] = (gelu * up_act).astype(BF16)
        gate_low = (upstream * up_act * slope).astype(BF16)
        up_low = (upstream * gelu).astype(BF16)
        gate_out[:, part] = gate_low
        up_out[:, part] = up_low
        step = nn(gate_low, gate_rows) + nn(up_low, up_rows)
        if start == 0:
            acc[...] = step
        else:
            acc[...] += step
    for at in range(count):
        outs[at][...] = acc[at * tokens : (at + 1) * tokens, :].astype(BF16)


def feed_call(blocks, place, cot_all, unit_rows, kept):
    count, (tokens, width) = len(blocks), blocks[0].shape
    total, units = cot_all.shape[0], unit_rows.shape[0]
    size = count * tokens
    once = pl.Buffered(1)

    def whole(dims):
        return pl.BlockSpec(dims, lambda i: (0, 0), pipeline_mode=once)

    def mine(columns):
        return pl.BlockSpec((size, columns), lambda i: (place, 0), pipeline_mode=once)

    made = pl.pallas_call(
        functools.partial(feed_body, count),
        grid=(1,),
        in_specs=[whole((tokens, width))] * count
        + [mine(width), whole(unit_rows.shape)]
        + [pl.BlockSpec(memory_space=pl.ANY)] * len(kept),
        out_specs=[whole((tokens, width))] * count + [mine(width)] + [mine(units)] * 3,
        out_shape=[shape((tokens, width), BF16)] * count
        + [shape((total, width), BF16)]
        + [shape((total, units), BF16)] * 3,
        scratch_shapes=[pltpu.VMEM((size, width), F32)],
        input_output_aliases={count + 2 + at: count + at for at in range(len(kept))},
        compiler_params=pltpu.CompilerParams(vmem_limit_bytes=MEBI * FEED_MEBI),
        cost_estimate=pl.CostEstimate(
            flops=int(2.5e9 * count), bytes_accessed=1 << 20, transcendentals=0
        ),
    )(*blocks, cot_all, unit_rows, *kept)
    return made[:count], made[count:]


def body(
    inputs,
    cotangent,
    segment_ids,
    bucket_table,
    gain_attention,
    query_weight,
    key_weight,
    value_weight,
    output_weight,
    bucket_bias,
    gain_feedforward,
    gate_weight,
    up_weight,
    down_weight,
):
    tokens, width = inputs.shape[1:]
    repeat = lax.axis_size("r")
    x_at, c_at, z_at, y_at, r_at = (lax.axis_index(name) for name in EVERY)
    coords = jnp.stack([x_at, c_at, z_at, y_at, r_at]).astype(jnp.int32)
    bucket_count, head_count = bucket_bias.shape
    hd = width // head_count
    block = 4 * tokens
    length = segment_ids.size
    reach = (bucket_table.shape[0] - 1) // 2
    assert reach == tokens and lax.axis_size("x") == lax.axis_size("c") == 2

    cot_own = cotangent[0]
    out_rows = output_weight
    if repeat > 1:
        out_rows = lax.all_gather(out_rows, "r", axis=0, tiled=True)
    message, joined, units = kernel_call(
        pack_body,
        [
            shape((tokens + hd // 2, width), BF16),
            shape((query_weight.shape[0], 3 * width), BF16),
            shape((gate_weight.shape[0], 3 * width), BF16),
        ],
        [
            inputs[0],
            gain_attention.reshape(1, width),
            out_rows,
            query_weight,
            key_weight,
            value_weight,
            gate_weight,
            up_weight,
            down_weight,
        ],
        scalars=0,
        micros=2,
    )
    messages = from_group(message, "z")
    if repeat > 1:
        joined = lax.all_gather(joined, "r", axis=0, tiled=True)
    head_rows = from_group(joined, SQUARE)
    other_rows = swap(jnp.concatenate(head_rows, axis=0), "c", 1)

    windows = segment_ids.reshape(-1, 2 * tokens)
    cuts = jnp.sum((windows < windows[:, -1:]).astype(jnp.int32), axis=1)
    turned = bucket_table[::-1]
    low_half, high_half = turned[reach : 2 * reach], turned[:reach]
    spots = jnp.concatenate(
        [
            jnp.broadcast_to(bucket_table[:1], (reach,)),
            low_half,
            low_half,
            high_half,
            high_half,
            jnp.broadcast_to(bucket_table[2 * reach :], (reach,)),
        ]
    )
    buckets = jnp.arange(bucket_count, dtype=jnp.int32)
    onehot = (spots[:, None] == buckets[None, :]).astype(F32)
    far_onehot = (bucket_table[0] == buckets).astype(F32)
    head_at = (x_at * 2 + y_at) * 4 + z_at
    bias_col = lax.dynamic_slice_in_dim(bucket_bias, head_at, 1, 1)[:, 0]
    diag = jnp.dot(onehot, bias_col, precision=HIGHEST) - jnp.sum(far_onehot * bias_col)
    hvec = jnp.pad(diag.reshape(3, 2 * reach), ((0, 5), (0, 0)))

    messages, hvec, cuts, coords, units = lax.optimization_barrier(
        (messages, hvec, cuts, coords, units)
    )
    unit_rows = lax.all_gather(units, UNITS_GROUP, axis=0, tiled=True)
    down_piece = unit_rows[:, 2 * width :]

    made = kernel_call(
        functools.partial(qkv_body, hd),
        [shape((block + 4 * hd, 2 * hd), BF16)] * 4
        + [
            shape((block, width), BF16),
            shape((12 * hd, width), BF16),
            shape((tokens + 2 * hd, width), BF16),
        ],
        [coords, *messages, *head_rows, other_rows, cot_own, anchor(messages, 30)],
    )
    pieces, (normed_all, group_weights, sent) = made[:4], made[4:]
    pieces = to_group(pieces, SQUARE)

    own = [piece[:block] for piece in pieces]
    other = swap(jnp.concatenate(own, axis=0), "c", 1)
    if repeat == 1:
        arrays = [*pieces, other]
    else:
        own = [lax.all_gather(part, "r", axis=0, tiled=True) for part in own]
        other = other.reshape(4, block, 2 * hd)
        other = [lax.all_gather(other[at], "r", axis=0, tiled=True) for at in range(4)]
        arrays = [*pieces, *own, jnp.concatenate(other, axis=0)]
    places = 8
    out_t, lse, attended, keys, keys_t, queries = kernel_call(
        functools.partial(attend_body, tokens, hd, repeat),
        [
            shape((16, hd, tokens), BF16),
            shape((places, 8, 2 * tokens), F32),
            shape((places, hd, 2 * tokens), F32),
            shape((length, 2 * hd), BF16),
            shape((length // block, 2 * hd, block), BF16),
            shape((places, hd, 2 * tokens), BF16),
        ],
        [coords, cuts, hvec, *arrays],
        [
            pltpu.VMEM((9 * repeat, block, 2 * tokens), F32),
            pltpu.VMEM((places + 2, block, 2 * tokens), F32),
            pltpu.VMEM((places, 2 * hd, 2 * tokens), BF16),
            pltpu.VMEM((2, 8, 2 * tokens), F32),
            pltpu.VMEM((2, 8, 2 * tokens), F32),
            pltpu.VMEM((2, hd, 2 * tokens), F32),
        ],
        scalars=2,
        micros=20,
    )
    sent, _ = lax.optimization_barrier((sent, pieces))
    parts = from_group(sent, SQUARE)
    arrived = lax.all_to_all(out_t, ("x", "y", "z"), split_axis=0, concat_axis=0, tiled=True)
    parts, arrived = lax.optimization_barrier((parts, arrived))
    cot_all = jnp.concatenate([parts[at][:tokens] for at in (1, 2, 0, 3)], axis=0)
    out_here = jnp.concatenate([part[tokens:] for part in parts], axis=0)
    out_other = swap(out_here, "c", 1)

    middle, normed_mid, out_full, features = kernel_call(
        functools.partial(output_body, hd),
        [
            shape((tokens, width), F32),
            shape((tokens, width), BF16),
            shape((width, width), BF16),
            shape((4, hd // 2, 8 * tokens), BF16),
        ],
        [
            coords,
            arrived.reshape(width, tokens),
            inputs[0],
            gain_feedforward.reshape(1, width),
            out_here,
            out_other,
        ],
    )
    scale_second = norm_scale(middle)
    own, second, third, fourth = from_group(normed_mid, SQUARE)

    (grad_own_part,), kept = feed_call([own], 2, cot_all, unit_rows, [])
    grad_near, kept = feed_call([second, third], 0, cot_all, unit_rows, kept)
    (grad_last,), kept = feed_call([fourth], 3, cot_all, unit_rows, kept)
    mid_all, gate_low, up_low, hidden = kept
    grad_parts = to_group([grad_own_part, *grad_near, grad_last], SQUARE)
    unit_grads = jnp.concatenate(
        [tn(gate_low, mid_all), tn(up_low, mid_all), tn(hidden, cot_all)], axis=1
    ).astype(BF16)
    feed = nn(hidden, down_piece).astype(BF16)
    grad_parts, unit_grads, feed = lax.optimization_barrier((grad_parts, unit_grads, feed))
    grad_norm_mid = sum(part.astype(F32) for part in grad_parts)
    feed, grad_norm_mid = lax.optimization_barrier((feed, grad_norm_mid))

    grad_middle = cot_own.astype(F32) + norm_back(
        middle, scale_second, gain_feedforward, grad_norm_mid
    )
    gain_second_term = jnp.sum(grad_norm_mid * middle * scale_second, axis=0)
    grad_mid_low = grad_middle.astype(BF16)
    grad_attended = nt(out_full, grad_mid_low).astype(BF16)
    grad_arrived = lax.all_to_all(
        grad_attended.reshape(16, hd, tokens),
        ("x", "y", "z"),
        split_axis=0,
        concat_axis=0,
        tiled=True,
    )
    grad_arrived, grad_mid_low, unit_grads = lax.optimization_barrier(
        (grad_arrived, grad_mid_low, unit_grads)
    )
    grad_units = lax.psum_scatter(unit_grads, UNITS_GROUP, scatter_dimension=0, tiled=True)
    mixed = to_group(
        [
            jnp.concatenate(
                [
                    feed[order * tokens : (order + 1) * tokens],
                    grad_mid_low,
                    features[at],
                ]
            )
            for at, order in enumerate((2, 0, 1, 3))
        ],
        SQUARE,
    )

    grad_own, grad_other, grad_q, table_out, far_out = kernel_call(
        functools.partial(attend_back_body, tokens, hd, repeat),
        [
            shape((4 * repeat * block, 2 * hd), F32),
            shape((4 * repeat * block, 2 * hd), BF16),
            shape((16, hd, tokens), BF16),
            shape((8, 2 * tokens), F32),
            shape((8, 2 * tokens), F32),
        ],
        [coords, cuts, hvec, grad_arrived, queries, keys, keys_t, attended, lse],
        [
            pltpu.VMEM((places + 2, block, 2 * tokens), F32),
            pltpu.VMEM((length, 2 * hd), F32),
            pltpu.VMEM((3, block, 2 * tokens), F32),
            pltpu.VMEM((places, 2 * hd, 4 * tokens), BF16),
            pltpu.VMEM((places, 4 * tokens, 2 * hd), BF16),
            pltpu.VMEM((places, 16, 2 * tokens), F32),
            pltpu.VMEM((2, hd, 2 * tokens), F32),
        ],
        scalars=2,
        micros=20,
    )
    mixed, grad_own = lax.optimization_barrier((mixed, grad_own))
    grad_pairs = (grad_own + swap(grad_other, "c", 1).astype(F32)).astype(BF16)
    grad_pairs = [
        grad_pairs[at * repeat * block : (at + 1) * repeat * block] for at in range(4)
    ]
    if repeat > 1:
        grad_pairs = [
            lax.psum_scatter(part, "r", scatter_dimension=0, tiled=True) for part in grad_pairs
        ]
    grad_pieces = [
        jnp.concatenate([grad_pairs[at], grad_q[4 * at : 4 * at + 4].reshape(4 * hd, tokens)])
        for at in range(4)
    ]
    mixed, grad_pieces = lax.optimization_barrier((mixed, grad_pieces))
    grad_pieces = to_group(grad_pieces, SQUARE)

    made = kernel_call(
        functools.partial(project_back_body, hd),
        [
            shape((4, tokens, width), BF16),
            shape((8, width), F32),
            shape((8 * hd, block), BF16),
            shape((4 * hd, block), BF16),
        ],
        [coords, *grad_pieces, normed_all, group_weights, gain_attention.reshape(1, width)],
        [pltpu.VMEM((block, 8 * hd), BF16), pltpu.VMEM((block, 4 * hd), BF16)],
        mebi=16,
    )
    normed_grads, gain_first_rows, pairs_t, queries_t = made
    normed_grads = lax.all_to_all(normed_grads, "z", split_axis=0, concat_axis=0, tiled=True)
    keep, send = kernel_call(
        functools.partial(head_grads_body, hd),
        [shape((4, hd // 2, 3 * width), BF16)] * 2,
        [coords, pairs_t, queries_t, normed_all],
    )
    layer_out = (middle + sum(part[:tokens].astype(F32) for part in mixed)).astype(BF16)
    grad_mid_all = jnp.concatenate([part[tokens : 2 * tokens] for part in mixed], axis=0)
    near = jnp.stack([part[2 * tokens :] for part in mixed]).reshape(4, hd // 2, 8, tokens)
    near = near.transpose(2, 1, 0, 3).reshape(4 * hd, block)
    out_grads = nn(near, grad_mid_all).astype(BF16)

    table_out, far_out, keep, send, grad_units, out_grads = lax.optimization_barrier(
        (table_out, far_out, keep, send, grad_units, out_grads)
    )
    out_grads = out_grads.reshape(2, 4, hd // 2, width)
    out_grads = (out_grads[0].astype(F32) + swap(out_grads[1], "c", 1).astype(F32)).astype(BF16)
    head_grads = (keep.astype(F32) + swap(send, "c", 1).astype(F32)).astype(BF16)
    bucket_grad = jnp.dot(table_out[:3].reshape(1, -1), onehot, precision=HIGHEST)[0]
    bucket_grad = bucket_grad + far_onehot * jnp.sum(far_out)
    head_mark = (jnp.arange(head_count) == head_at).astype(F32)
    bias_term = bucket_grad[:, None] * head_mark[None, :]
    sums = jnp.concatenate([jnp.sum(gain_first_rows, axis=0), gain_second_term, bias_term.ravel()])
    sums = sums + swap(sums, "c", 1)
    sums = sum_everywhere(sums, SQUARE)
    head_grads = to_group([head_grads[at] for at in range(4)], SQUARE)
    normed_grads, head_grads, sums, out_grads = lax.optimization_barrier(
        (normed_grads, head_grads, sums, out_grads)
    )
    out_grads, sums = sum_over_z(out_grads, sums)
    head_grads = sum(part.astype(F32) for part in head_grads)
    if repeat > 1:
        sums = lax.psum(sums, "r")
        out_grads = lax.psum_scatter(
            out_grads.astype(BF16), "r", scatter_dimension=0, tiled=True
        ).astype(F32)
        head_grads = lax.psum_scatter(
            head_grads.astype(BF16), "r", scatter_dimension=0, tiled=True
        ).astype(F32)
    gain_first_grad, gain_second_grad = sums[:width], sums[width : 2 * width]
    bias_grad = sums[2 * width :].reshape(bucket_count, head_count)

    grad_inputs = kernel_call(
        finish_body,
        shape((tokens, width), BF16),
        [normed_grads, inputs[0], grad_middle, gain_attention.reshape(1, width)],
        scalars=0,
        micros=100,
        mebi=16,
    )
    unit_grads = grad_units.astype(F32)
    return (
        layer_out[None],
        grad_inputs[None],
        gain_first_grad,
        head_grads[:, :width],
        head_grads[:, width : 2 * width],
        head_grads[:, 2 * width :],
        out_grads,
        bias_grad,
        gain_second_grad,
        unit_grads[:, :width],
        unit_grads[:, width : 2 * width],
        unit_grads[:, 2 * width :],
    )


def solution(mesh):
    owners, runs = mesh.shape["ulysses"], mesh.shape["blk"]
    fine = Mesh(mesh.devices.reshape(2, owners // 2, 4, 2, runs // 8), EVERY)
    tokens = P(("z", "y", "r"), ("x", "c"), None)
    rows = P(EVERY, None)
    return jax.shard_map(
        body,
        mesh=fine,
        in_specs=(tokens, tokens) + (P(),) * 3 + (rows,) * 4 + (P(),) * 2 + (rows,) * 3,
        out_specs=(tokens, tokens, P()) + (rows,) * 4 + (P(),) * 2 + (rows,) * 3,
        check_vma=False,
    )
```

```python
import functools
import math

import jax
import jax.numpy as jnp
from jax import lax
from jax.experimental import pallas as pl
from jax.experimental.pallas import tpu as pltpu
from jax.sharding import Mesh
from jax.sharding import PartitionSpec as P

EPSILON = 1e-06
NEGATIVE = -1e30
HIGHEST = lax.Precision.HIGHEST
F32 = jnp.float32
BF16 = jnp.bfloat16
MEBI = 1024 * 1024
FEED_MEBI = 24
GELU_SCALE = math.sqrt(2.0 / math.pi)
GELU_CUBE = 0.044715
SQUARE = ("x", "y")
UNITS_GROUP = ("z", "c", "r")
EVERY = ("x", "c", "z", "y", "r")


def norm_scale(values):
    return lax.rsqrt(jnp.mean(values * values, axis=-1, keepdims=True) + EPSILON)


def norm_back(values, scaling, gain_vec, upstream):
    inner_sum = jnp.mean(values * gain_vec * upstream, axis=-1, keepdims=True)
    return scaling * gain_vec * upstream - values * scaling * scaling * scaling * inner_sum


def nt(left, right):
    return lax.dot_general(left, right, (((1,), (1,)), ((), ())), preferred_element_type=F32)


def nn(left, right):
    return lax.dot_general(left, right, (((1,), (0,)), ((), ())), preferred_element_type=F32)


def tn(left, right):
    return lax.dot_general(left, right, (((0,), (0,)), ((), ())), preferred_element_type=F32)


def swap(value, axis, mask):
    size = lax.axis_size(axis)
    return lax.ppermute(value, axis, [(at, at ^ mask) for at in range(size)])


def from_group(value, axis):
    return [value] + [swap(value, axis, mask) for mask in (1, 2, 3)]


def to_group(values, axis):
    return [values[0]] + [swap(values[mask], axis, mask) for mask in (1, 2, 3)]


def sum_everywhere(value, axis):
    first, second, third, fourth = from_group(value, axis)
    return (first + second) + (third + fourth)


def sum_over_z(rows, values):
    width = rows.shape[-1]
    lines = -(-values.size // width)
    padded = jnp.pad(values, (0, lines * width - values.size)).reshape(lines, width)
    high = lax.reduce_precision(padded, 8, 7)
    extra = jnp.concatenate([high, padded - high]).astype(BF16)
    extra = jnp.pad(extra, ((0, -2 * lines % 8), (0, 0)))
    arrived = to_group([jnp.concatenate([rows[at], extra]) for at in range(4)], "z")
    arrived = [part.astype(F32) for part in arrived]
    count = rows.shape[1]
    tails = [part[count : count + lines] + part[count + lines : count + 2 * lines] for part in arrived]
    total = (tails[0] + tails[1]) + (tails[2] + tails[3])
    return sum(part[:count] for part in arrived), total.ravel()[: values.size]


def kernel_call(body, out_shapes, inputs, scratch=(), scalars=1, micros=4, mebi=60):
    in_specs = [pl.BlockSpec(memory_space=pltpu.SMEM)] * scalars
    in_specs += [pl.BlockSpec(memory_space=pltpu.VMEM)] * (len(inputs) - scalars)
    return pl.pallas_call(
        body,
        out_shape=out_shapes,
        in_specs=in_specs,
        out_specs=jax.tree.map(lambda _: pl.BlockSpec(memory_space=pltpu.VMEM), out_shapes),
        scratch_shapes=list(scratch),
        compiler_params=pltpu.CompilerParams(vmem_limit_bytes=mebi * MEBI),
        cost_estimate=pl.CostEstimate(
            flops=int(micros * 1.15e9), bytes_accessed=1 << 20, transcendentals=0
        ),
    )(*inputs)


def shape(dims, dtype):
    return jax.ShapeDtypeStruct(dims, dtype)


def pack_body(*refs):
    own_in, gain, out_rows = refs[:3]
    heads, units = refs[3:6], refs[6:9]
    message, joined, joined_units = refs[9:]
    tokens, width = own_in.shape
    values = own_in[...].astype(F32)
    message[0:tokens, :] = (values * norm_scale(values) * gain[...]).astype(BF16)
    message[tokens:, :] = out_rows[...]
    for at in range(3):
        joined[:, at * width : (at + 1) * width] = heads[at][...]
        joined_units[:, at * width : (at + 1) * width] = units[at][...]


def anchor_body(*refs):
    refs[-1][...] = jnp.zeros_like(refs[-1])


def anchor(values, micros):
    return pl.pallas_call(
        anchor_body,
        out_shape=shape((8, 128), F32),
        in_specs=[pl.BlockSpec(memory_space=pl.ANY)] * len(values),
        out_specs=pl.BlockSpec(memory_space=pltpu.VMEM),
        cost_estimate=pl.CostEstimate(
            flops=int(micros * 1.15e9), bytes_accessed=1 << 20, transcendentals=0
        ),
    )(*values)


def qkv_body(hd, coords, *refs):
    blocks, parts, other_rows, cot_own, pieces = refs[:4], refs[4:8], refs[8], refs[9], refs[11:15]
    rows_all, weights, onward = refs[15:18]
    c_at, y_at = coords[1], coords[3]
    width, half = rows_all.shape[1], hd // 2
    tokens = rows_all.shape[0] // 4
    for at in range(4):
        rows_all[at * tokens : (at + 1) * tokens, :] = blocks[at][0:tokens, :]
        start = tokens + at * half
        onward[start : start + half, :] = blocks[at][tokens:, :]
    onward[0:tokens, :] = cot_own[...]
    for core in range(2):
        for dest in range(4):
            column = y_at ^ c_at ^ core
            place = (dest >> 1) * 2 + column
            shift = pl.multiple_of((y_at ^ (dest & 1)) * half, half)
            source = other_rows.at[dest * half : (dest + 1) * half] if core else parts[dest]
            for kind, first, step in ((0, 8 * hd, hd), (1, 0, 2 * hd), (2, hd, 2 * hd)):
                start = pl.multiple_of(first + place * step + shift, half)
                weights[pl.ds(start, half), :] = source[:, kind * width : (kind + 1) * width]
    normed = rows_all[...]
    pairs = nt(normed, weights[0 : 8 * hd, :]).astype(BF16)
    queries = nt(weights[8 * hd : 12 * hd, :], normed).astype(BF16)
    for dest in range(4):
        pieces[dest][0 : 4 * tokens, :] = pairs[:, dest * 2 * hd : (dest + 1) * 2 * hd]
        for at in range(4):
            pieces[dest][4 * tokens + at * hd : 4 * tokens + (at + 1) * hd, :] = queries[
                dest * hd : (dest + 1) * hd, at * tokens : (at + 1) * tokens
            ]


def bias_tiles(hvec, tokens):
    tiles = {}
    for at, diff in enumerate((-1, 0, 1)):
        spread = jnp.broadcast_to(hvec[at : at + 1, :], (tokens, 2 * tokens))
        tiles[diff] = pltpu.roll(spread, 0, 1, stride=1, stride_axis=0)[:, :tokens]
    return tiles


def fill_bias(hvec_ref, bias, cuts, repeat, c_at, r_at, tokens):
    tiles = bias_tiles(hvec_ref[...], tokens)
    zero = jnp.zeros((tokens, tokens), F32)
    bias[0] = jnp.zeros(bias.shape[1:], F32)
    for rows in range(8):
        for half in range(2):
            diff = rows - 4 - 2 * half
            even, odd = tiles.get(diff, zero), tiles.get(diff - 1, zero)
            row = (rows % 4) * tokens
            bias[1 + rows // 4, row : row + tokens, half * tokens : (half + 1) * tokens] = (
                jnp.where(c_at == 0, even, odd)
            )

    def mask(back, carry):
        place = bias.shape[0] - 3 - back
        allowed = allowed_mask(cuts, place * repeat + r_at, c_at, tokens)
        bias[2 + place] = jnp.where(allowed, bias[2], NEGATIVE)
        return carry

    lax.fori_loop(0, bias.shape[0] - 2, mask, 0)


def bias_slab(bias, place, run, at):
    return bias[jnp.where(at == run, 2 + place, jnp.where(at == run - 1, 1, 0))]


def allowed_mask(cuts, run, c_at, tokens):
    rows, cols = 4 * tokens, 2 * tokens
    key_at = lax.broadcasted_iota(jnp.int32, (rows, cols), 0)
    query_at = lax.broadcasted_iota(jnp.int32, (rows, cols), 1)
    key_window = key_at >= 2 * tokens
    query_window = query_at >= tokens
    key_in = jnp.where(key_window, key_at - 2 * tokens, key_at)
    query_in = jnp.where(query_window, query_at - tokens, query_at) + c_at * tokens
    cut = jnp.where(query_window, cuts[2 * run + 1], cuts[2 * run])
    inside = (key_in < cut) | (query_in >= cut)
    before = jnp.logical_and(jnp.logical_not(key_window), query_window)
    same = key_window == query_window
    return before | (same & inside)


def each_slot(run_low, run_high, repeat, step):
    def one(slot, carry):
        high = (slot > run_low).astype(jnp.int32)
        at = jnp.where(slot > run_low, slot - run_low - 1, slot)
        step(slot, high, at)
        return carry

    count = run_low + run_high + 2
    if repeat == 1:
        for slot in range(9):
            one(jnp.int32(slot), 0)
    else:
        lax.fori_loop(0, count, one, 0)


def chunk(at, block):
    return pl.ds(pl.multiple_of(at * block, block), block)


def fold_rows(values, how):
    rows, cols = values.shape
    return how(values.reshape(rows // 8, 8, cols), axis=0)


def attend_body(tokens, hd, repeat, coords, cuts, hvec, *refs):
    pieces = refs[:4]
    own, other, refs = (pieces, *refs[4:5], refs[5:]) if repeat == 1 else (refs[4:8], refs[8], refs[9:])
    out, lse, attended, keys, keys_t, queries, scores, bias, padded, peaks, totals, mixes = refs
    x_at, c_at, z_at, y_at, r_at = (coords[at] for at in range(5))
    block = 4 * tokens
    for dest in range(4):
        x_from, y_from = x_at ^ (dest >> 1), y_at ^ (dest & 1)
        for at in range(4):
            place = (z_at ^ at) * 2 + y_from
            for rep in range(repeat):
                run = place * repeat + rep
                base = run * block + x_from * 2 * tokens
                source = slice(rep * block + at * tokens, rep * block + (at + 1) * tokens)
                keys[pl.ds(pl.multiple_of(base + c_at * tokens, tokens), tokens), :] = own[dest][
                    source, :
                ]
                start = (dest * repeat + rep) * block + at * tokens
                keys[pl.ds(pl.multiple_of(base + (1 - c_at) * tokens, tokens), tokens), :] = other[
                    start : start + tokens, :
                ]
            start = block + at * hd
            queries[place, :, pl.ds(pl.multiple_of(x_from * tokens, tokens), tokens)] = pieces[
                dest
            ][start : start + hd, :]
    fill_bias(hvec, bias, cuts, repeat, c_at, r_at, tokens)

    def turn(at, carry):
        keys_t[at] = keys[chunk(at, block), :].T
        return carry

    lax.fori_loop(0, keys.shape[0] // block, turn, 0)
    places = queries.shape[0]
    padded[:, 0:hd, :] = queries[...]
    padded[:, hd:, :] = jnp.zeros_like(padded[:, hd:, :])

    def pair(low, carry):
        place_of = (low, places - 1 - low)
        run_of = tuple(place * repeat + r_at for place in place_of)
        peaks[...] = jnp.full_like(peaks, NEGATIVE)
        totals[...] = jnp.zeros_like(totals)
        mixes[...] = jnp.zeros_like(mixes)

        def score(slot, high, at):
            place = jnp.where(high == 1, place_of[1], place_of[0])
            run = place * repeat + r_at
            values = nn(keys[chunk(at, block), :], padded[place])
            values = values + bias_slab(bias, place, run, at)
            scores[slot] = values
            peaks[high] = jnp.maximum(peaks[high], fold_rows(values, jnp.max))

        each_slot(*run_of, repeat, score)
        for high in range(2):
            top = jnp.max(peaks[high], axis=0, keepdims=True)
            peaks[high] = jnp.broadcast_to(top, peaks.shape[1:])

        def mix(slot, high, at):
            weights = jnp.exp(scores[slot] - peaks[high][0:1, :])
            totals[high] += fold_rows(weights, jnp.sum)
            mixes[high] += nn(keys_t[at, hd:, :], weights.astype(BF16))

        each_slot(*run_of, repeat, mix)
        for high, place in enumerate(place_of):
            total = jnp.sum(totals[high], axis=0, keepdims=True)
            mixed = mixes[high] / total
            attended[place] = mixed
            lse[place] = peaks[high] + jnp.log(jnp.broadcast_to(total, peaks.shape[1:]))
            part = mixed.astype(BF16)
            for half in range(2):
                out[half * 8 + (place & 1) * 4 + (place >> 1)] = part[
                    :, half * tokens : (half + 1) * tokens
                ]
        return carry

    lax.fori_loop(0, places // 2, pair, 0)


def attend_back_body(tokens, hd, repeat, coords, cuts, hvec, *refs):
    arrived, queries, keys, keys_t, attended, lse, marks = refs[:7]
    grad_own, grad_other, grad_q, bucket_out = refs[7:11]
    bias, grad_keys, table_acc, left, right, shifts, grad_queries = refs[11:]
    x_at, c_at, z_at, y_at, r_at = (coords[at] for at in range(5))
    block = 4 * tokens
    places = queries.shape[0]
    fill_bias(hvec, bias, cuts, repeat, c_at, r_at, tokens)
    grad_keys[...] = jnp.zeros_like(grad_keys)
    table_acc[...] = jnp.zeros_like(table_acc)

    def prepare(place, carry):
        query_t = queries[place]
        upstream_t = jnp.concatenate(
            [arrived[half * 8 + (place & 1) * 4 + (place >> 1)] for half in range(2)], axis=1
        )
        zero = jnp.zeros_like(query_t)
        query_pad = jnp.concatenate([query_t, zero], axis=0)
        upstream_pad = jnp.concatenate([zero, upstream_t], axis=0)
        left[place, :, 0 : 2 * tokens] = query_pad
        left[place, :, 2 * tokens :] = upstream_pad
        right[place, 0 : 2 * tokens, :] = query_pad.T
        right[place, 2 * tokens :, :] = upstream_pad.T
        shifts[place, 0:8, :] = lse[place]
        delta = jnp.sum(upstream_t.astype(F32) * attended[place], axis=0, keepdims=True)
        shifts[place, 8:16, :] = jnp.broadcast_to(delta, (8, 2 * tokens))
        return carry

    lax.fori_loop(0, places, prepare, 0)

    def pair(low, carry):
        place_of = (low, places - 1 - low)
        run_of = tuple(place * repeat + r_at for place in place_of)
        grad_queries[...] = jnp.zeros_like(grad_queries)

        def step(slot, high, at):
            place = jnp.where(high == 1, place_of[1], place_of[0])
            run = place * repeat + r_at
            rows = chunk(at, block)
            both = nn(keys[rows, :], left[place])
            values = both[:, 0 : 2 * tokens] + bias_slab(bias, place, run, at)
            probs = jnp.exp(values - shifts[place, 0:1, :])
            grad_scores = probs * (both[:, 2 * tokens :] - shifts[place, 8:9, :])
            grad_low = grad_scores.astype(BF16)
            grad_keys[rows, :] += nn(
                jnp.concatenate([grad_low, probs.astype(BF16)], axis=1), right[place]
            )
            grad_queries[high] += nn(keys_t[at, :hd, :], grad_low)
            kind = jnp.where(at == run, 2, jnp.where(at == run - 1, 1, 0))
            table_acc[kind] += grad_low.astype(F32)

        each_slot(*run_of, repeat, step)
        for high, place in enumerate(place_of):
            low_part = grad_queries[high].astype(BF16)
            for half in range(2):
                part = low_part[:, half * tokens : (half + 1) * tokens]
                dest = (x_at ^ half) * 2 + ((place & 1) ^ y_at)
                grad_q[dest * 4 + ((place >> 1) ^ z_at)] = part
        return carry

    lax.fori_loop(0, places // 2, pair, 0)

    for dest in range(4):
        x_from, y_from = x_at ^ (dest >> 1), y_at ^ (dest & 1)
        for at in range(4):
            place = (z_at ^ at) * 2 + y_from
            for rep in range(repeat):
                base = (place * repeat + rep) * block + x_from * 2 * tokens
                start = (dest * repeat + rep) * block + at * tokens
                target = slice(start, start + tokens)
                grad_own[target, :] = grad_keys[
                    pl.ds(pl.multiple_of(base + c_at * tokens, tokens), tokens), :
                ]
                grad_other[target, :] = grad_keys[
                    pl.ds(pl.multiple_of(base + (1 - c_at) * tokens, tokens), tokens), :
                ].astype(BF16)

    def tile_at(rows, half):
        row = (rows % 4) * tokens
        return table_acc[
            1 + rows // 4, row : row + tokens, half * tokens : (half + 1) * tokens
        ]

    spots = [(rows, half) for rows in range(8) for half in range(2)]
    flip = (
        lax.broadcasted_iota(jnp.int32, (tokens, tokens), 0)
        + lax.broadcasted_iota(jnp.int32, (tokens, tokens), 1)
        == tokens - 1
    ).astype(F32)
    far_even = jnp.zeros((tokens, tokens), F32)
    far_odd = jnp.zeros((tokens, tokens), F32)
    for rows, half in spots:
        diff = rows - 4 - 2 * half
        if diff <= -2:
            far_even += tile_at(rows, half)
        if diff - 1 <= -2:
            far_odd += tile_at(rows, half)
    extra = fold_rows(jnp.where(c_at == 0, far_even, far_odd), jnp.sum)
    far_rows = fold_rows(table_acc[0], jnp.sum)
    far_rows = far_rows[:, :tokens] + far_rows[:, tokens:] + extra
    total = jnp.sum(jnp.sum(far_rows, axis=0, keepdims=True), axis=1, keepdims=True)
    last = 3 * 2 * tokens
    bucket = total * marks[last : last + 1, :]
    for index, diff in enumerate((-1, 0, 1)):
        even = sum(tile_at(rows, half) for rows, half in spots if rows - 4 - 2 * half == diff)
        odd = sum(tile_at(rows, half) for rows, half in spots if rows - 5 - 2 * half == diff)
        tile = jnp.where(c_at == 0, even, odd)
        turned = jnp.dot(flip, tile, precision=HIGHEST, preferred_element_type=F32)
        wide = jnp.concatenate([turned, jnp.zeros_like(turned)], axis=1)
        wide = pltpu.roll(wide, tokens + 1, 1, stride=1, stride_axis=0)
        diagonals = jnp.broadcast_to(jnp.sum(wide, axis=0, keepdims=True), (8, 2 * tokens))
        part = marks[index * 2 * tokens : (index + 1) * 2 * tokens, :]
        bucket = bucket + jnp.dot(
            diagonals, part, precision=HIGHEST, preferred_element_type=F32
        )[0:1, :]
    bucket_out[...] = jnp.broadcast_to(bucket, bucket_out.shape)


def project_back_body(hd, coords, *refs):
    pieces, (rows_all, weights, gain), out = refs[:4], refs[4:7], refs[7]
    gain_out, pairs_t, queries_t, pairs, queries = refs[8:]
    tokens, width = out.shape[1:]
    z_at = coords[2]
    for dest in range(4):
        lanes = slice(dest * 2 * hd, (dest + 1) * 2 * hd)
        part = pieces[dest][0 : 4 * tokens, :]
        pairs[:, lanes] = part
        pairs_t[lanes, :] = part.T
        for at in range(4):
            queries_t[dest * hd : (dest + 1) * hd, at * tokens : (at + 1) * tokens] = pieces[dest][
                4 * tokens + at * hd : 4 * tokens + (at + 1) * hd, :
            ]
    queries[...] = queries_t[...].T
    grad = nn(pairs[...], weights[0 : 8 * hd, :]) + nn(queries[...], weights[8 * hd :, :])
    unit = rows_all[...].astype(F32) / gain[...]
    gain_out[...] = fold_rows(grad * unit, jnp.sum)
    for at in range(4):
        out[z_at ^ at] = grad[at * tokens : (at + 1) * tokens, :].astype(BF16)


def head_grads_body(hd, coords, pairs_t, queries_t, rows_all, keep, send):
    c_at, y_at = coords[1], coords[3]
    width = rows_all.shape[1]
    half = hd // 2
    normed = rows_all[...]
    pair_rows = nn(pairs_t[...], normed).astype(BF16)
    query_rows = nn(queries_t[...], normed).astype(BF16)
    for dest in range(4):
        other = (y_at ^ (dest & 1)) ^ c_at

        def put(target, dest=dest):
            for part in range(2):
                place = (dest >> 1) * 2 + (y_at ^ part)
                for kind, rows, first in (
                    (0, query_rows, dest * hd),
                    (1, pair_rows, dest * 2 * hd),
                    (2, pair_rows, dest * 2 * hd + hd),
                ):
                    first += part * half
                    target[place, :, kind * width : (kind + 1) * width] = rows[
                        first : first + half, :
                    ]

        pl.when(other == 0)(functools.partial(put, keep))
        pl.when(other == 1)(functools.partial(put, send))


def output_body(hd, coords, *refs):
    arrived, own_in, gain, here, other, middle_out, normed_out, weights, features = refs
    x_at, c_at, z_at, y_at = coords[0], coords[1], coords[2], coords[3]
    half, tokens = hd // 2, arrived.shape[1]
    for core, source in enumerate((here, other)):
        for dest in range(4):
            for near in range(4):
                head = ((x_at ^ (dest >> 1)) * 2 + (c_at ^ core)) * 4 + (z_at ^ near)
                start = pl.multiple_of(head * hd + (y_at ^ (dest & 1)) * half, half)
                first = (dest * 4 + near) * half
                weights[pl.ds(start, half), :] = source[first : first + half, :]
    for dest in range(4):
        for core in range(2):
            for near in range(4):
                head = ((x_at ^ (dest >> 1)) * 2 + (c_at ^ core)) * 4 + (z_at ^ near)
                start = pl.multiple_of(head * hd + (y_at ^ (dest & 1)) * half, half)
                lanes = slice((core * 4 + near) * tokens, (core * 4 + near + 1) * tokens)
                features[dest, :, lanes] = arrived[pl.ds(start, half), :]
    middle = own_in[...].astype(F32) + nn(arrived[...].T, weights[...])
    middle_out[...] = middle
    normed_out[...] = (middle * norm_scale(middle) * gain[...]).astype(BF16)


def finish_body(*refs):
    parts, own_in, grad_middle, gain, out = refs
    values = own_in[...].astype(F32)
    grad = sum(parts[at].astype(F32) for at in range(4))
    out[...] = (
        grad_middle[...] + norm_back(values, norm_scale(values), gain[...], grad)
    ).astype(BF16)


def feed_body(count, *refs):
    blocks, cot, rows = refs[:count], refs[count], refs[count + 1]
    outs = refs[-5 - count : -5]
    mid_out, gate_out, up_out, hidden_out, acc = refs[-5:]
    tokens, width = blocks[0].shape
    for at in range(count):
        mid_out[at * tokens : (at + 1) * tokens, :] = blocks[at][...]
    units = rows.shape[0]
    for start in range(0, units, 256):
        part = slice(start, min(start + 256, units))
        gate_rows = rows[part, 0:width]
        up_rows = rows[part, width : 2 * width]
        gate_act = nt(mid_out[...], gate_rows)
        up_act = nt(mid_out[...], up_rows)
        upstream = nt(cot[...], rows[part, 2 * width :])
        square = gate_act * gate_act
        curve = jnp.tanh(GELU_SCALE * gate_act * (1.0 + GELU_CUBE * square))
        half = 0.5 + 0.5 * curve
        gelu = gate_act * half
        slope = half + (0.5 * GELU_SCALE) * gate_act * (1.0 - curve * curve) * (
            1.0 + 3.0 * GELU_CUBE * square
        )
        hidden_out[:, part] = (gelu * up_act).astype(BF16)
        gate_low = (upstream * up_act * slope).astype(BF16)
        up_low = (upstream * gelu).astype(BF16)
        gate_out[:, part] = gate_low
        up_out[:, part] = up_low
        step = nn(gate_low, gate_rows) + nn(up_low, up_rows)
        if start == 0:
            acc[...] = step
        else:
            acc[...] += step
    for at in range(count):
        outs[at][...] = acc[at * tokens : (at + 1) * tokens, :].astype(BF16)


def feed_call(blocks, place, cot_all, unit_rows, kept):
    count, (tokens, width) = len(blocks), blocks[0].shape
    total, units = cot_all.shape[0], unit_rows.shape[0]
    size = count * tokens
    once = pl.Buffered(1)

    def whole(dims):
        return pl.BlockSpec(dims, lambda i: (0, 0), pipeline_mode=once)

    def mine(columns):
        return pl.BlockSpec((size, columns), lambda i: (place, 0), pipeline_mode=once)

    made = pl.pallas_call(
        functools.partial(feed_body, count),
        grid=(1,),
        in_specs=[whole((tokens, width))] * count
        + [mine(width), whole(unit_rows.shape)]
        + [pl.BlockSpec(memory_space=pl.ANY)] * len(kept),
        out_specs=[whole((tokens, width))] * count + [mine(width)] + [mine(units)] * 3,
        out_shape=[shape((tokens, width), BF16)] * count
        + [shape((total, width), BF16)]
        + [shape((total, units), BF16)] * 3,
        scratch_shapes=[pltpu.VMEM((size, width), F32)],
        input_output_aliases={count + 2 + at: count + at for at in range(len(kept))},
        compiler_params=pltpu.CompilerParams(vmem_limit_bytes=MEBI * FEED_MEBI),
        cost_estimate=pl.CostEstimate(
            flops=int(2.5e9 * count), bytes_accessed=1 << 20, transcendentals=0
        ),
    )(*blocks, cot_all, unit_rows, *kept)
    return made[:count], made[count:]


def body(
    inputs,
    cotangent,
    segment_ids,
    bucket_table,
    gain_attention,
    query_weight,
    key_weight,
    value_weight,
    output_weight,
    bucket_bias,
    gain_feedforward,
    gate_weight,
    up_weight,
    down_weight,
):
    tokens, width = inputs.shape[1:]
    repeat = lax.axis_size("r")
    x_at, c_at, z_at, y_at, r_at = (lax.axis_index(name) for name in EVERY)
    coords = jnp.stack([x_at, c_at, z_at, y_at, r_at]).astype(jnp.int32)
    bucket_count, head_count = bucket_bias.shape
    hd = width // head_count
    block = 4 * tokens
    length = segment_ids.size
    reach = (bucket_table.shape[0] - 1) // 2
    assert reach == tokens and lax.axis_size("x") == lax.axis_size("c") == 2

    cot_own = cotangent[0]
    out_rows = output_weight
    if repeat > 1:
        out_rows = lax.all_gather(out_rows, "r", axis=0, tiled=True)
    message, joined, units = kernel_call(
        pack_body,
        [
            shape((tokens + hd // 2, width), BF16),
            shape((query_weight.shape[0], 3 * width), BF16),
            shape((gate_weight.shape[0], 3 * width), BF16),
        ],
        [
            inputs[0],
            gain_attention.reshape(1, width),
            out_rows,
            query_weight,
            key_weight,
            value_weight,
            gate_weight,
            up_weight,
            down_weight,
        ],
        scalars=0,
        micros=2,
    )
    messages = from_group(message, "z")
    if repeat > 1:
        joined = lax.all_gather(joined, "r", axis=0, tiled=True)
    head_rows = from_group(joined, SQUARE)
    other_rows = swap(jnp.concatenate(head_rows, axis=0), "c", 1)

    windows = segment_ids.reshape(-1, 2 * tokens)
    cuts = jnp.sum((windows < windows[:, -1:]).astype(jnp.int32), axis=1)
    turned = bucket_table[::-1]
    low_half, high_half = turned[reach : 2 * reach], turned[:reach]
    spots = jnp.concatenate(
        [
            jnp.broadcast_to(bucket_table[:1], (reach,)),
            low_half,
            low_half,
            high_half,
            high_half,
            jnp.broadcast_to(bucket_table[2 * reach :], (reach,)),
        ]
    )
    buckets = jnp.arange(bucket_count, dtype=jnp.int32)
    onehot = (spots[:, None] == buckets[None, :]).astype(F32)
    far_onehot = (bucket_table[0] == buckets).astype(F32)
    head_at = (x_at * 2 + y_at) * 4 + z_at
    bias_col = lax.dynamic_slice_in_dim(bucket_bias, head_at, 1, 1)[:, 0]
    diag = jnp.dot(onehot, bias_col, precision=HIGHEST) - jnp.sum(far_onehot * bias_col)
    hvec = jnp.pad(diag.reshape(3, 2 * reach), ((0, 5), (0, 0)))

    messages, hvec, cuts, coords, units = lax.optimization_barrier(
        (messages, hvec, cuts, coords, units)
    )
    unit_rows = lax.all_gather(units, UNITS_GROUP, axis=0, tiled=True)
    down_piece = unit_rows[:, 2 * width :]

    made = kernel_call(
        functools.partial(qkv_body, hd),
        [shape((block + 4 * hd, 2 * hd), BF16)] * 4
        + [
            shape((block, width), BF16),
            shape((12 * hd, width), BF16),
            shape((tokens + 2 * hd, width), BF16),
        ],
        [coords, *messages, *head_rows, other_rows, cot_own, anchor(messages, 30)],
    )
    pieces, (normed_all, group_weights, sent) = made[:4], made[4:]
    pieces = to_group(pieces, SQUARE)

    own = [piece[:block] for piece in pieces]
    other = swap(jnp.concatenate(own, axis=0), "c", 1)
    if repeat == 1:
        arrays = [*pieces, other]
    else:
        own = [lax.all_gather(part, "r", axis=0, tiled=True) for part in own]
        other = other.reshape(4, block, 2 * hd)
        other = [lax.all_gather(other[at], "r", axis=0, tiled=True) for at in range(4)]
        arrays = [*pieces, *own, jnp.concatenate(other, axis=0)]
    places = 8
    out_t, lse, attended, keys, keys_t, queries = kernel_call(
        functools.partial(attend_body, tokens, hd, repeat),
        [
            shape((16, hd, tokens), BF16),
            shape((places, 8, 2 * tokens), F32),
            shape((places, hd, 2 * tokens), F32),
            shape((length, 2 * hd), BF16),
            shape((length // block, 2 * hd, block), BF16),
            shape((places, hd, 2 * tokens), BF16),
        ],
        [coords, cuts, hvec, *arrays],
        [
            pltpu.VMEM((9 * repeat, block, 2 * tokens), F32),
            pltpu.VMEM((places + 2, block, 2 * tokens), F32),
            pltpu.VMEM((places, 2 * hd, 2 * tokens), BF16),
            pltpu.VMEM((2, 8, 2 * tokens), F32),
            pltpu.VMEM((2, 8, 2 * tokens), F32),
            pltpu.VMEM((2, hd, 2 * tokens), F32),
        ],
        scalars=2,
        micros=20,
    )
    sent, _ = lax.optimization_barrier((sent, pieces))
    parts = from_group(sent, SQUARE)
    arrived = lax.all_to_all(out_t, ("x", "y", "z"), split_axis=0, concat_axis=0, tiled=True)
    parts, arrived = lax.optimization_barrier((parts, arrived))
    cot_all = jnp.concatenate([parts[at][:tokens] for at in (1, 2, 0, 3)], axis=0)
    out_here = jnp.concatenate([part[tokens:] for part in parts], axis=0)
    out_other = swap(out_here, "c", 1)

    middle, normed_mid, out_full, features = kernel_call(
        functools.partial(output_body, hd),
        [
            shape((tokens, width), F32),
            shape((tokens, width), BF16),
            shape((width, width), BF16),
            shape((4, hd // 2, 8 * tokens), BF16),
        ],
        [
            coords,
            arrived.reshape(width, tokens),
            inputs[0],
            gain_feedforward.reshape(1, width),
            out_here,
            out_other,
        ],
    )
    scale_second = norm_scale(middle)
    own, second, third, fourth = from_group(normed_mid, SQUARE)

    (grad_own_part,), kept = feed_call([own], 2, cot_all, unit_rows, [])
    grad_near, kept = feed_call([second, third], 0, cot_all, unit_rows, kept)
    (grad_last,), kept = feed_call([fourth], 3, cot_all, unit_rows, kept)
    mid_all, gate_low, up_low, hidden = kept
    grad_parts = to_group([grad_own_part, *grad_near, grad_last], SQUARE)
    unit_grads = jnp.concatenate(
        [tn(gate_low, mid_all), tn(up_low, mid_all), tn(hidden, cot_all)], axis=1
    ).astype(BF16)
    feed = nn(hidden, down_piece).astype(BF16)
    grad_parts, unit_grads, feed = lax.optimization_barrier((grad_parts, unit_grads, feed))
    grad_norm_mid = sum(part.astype(F32) for part in grad_parts)
    feed, grad_norm_mid = lax.optimization_barrier((feed, grad_norm_mid))

    grad_middle = cot_own.astype(F32) + norm_back(
        middle, scale_second, gain_feedforward, grad_norm_mid
    )
    gain_second_term = jnp.sum(grad_norm_mid * middle * scale_second, axis=0)
    grad_mid_low = grad_middle.astype(BF16)
    grad_attended = nt(out_full, grad_mid_low).astype(BF16)
    grad_arrived = lax.all_to_all(
        grad_attended.reshape(16, hd, tokens),
        ("x", "y", "z"),
        split_axis=0,
        concat_axis=0,
        tiled=True,
    )
    grad_arrived, grad_mid_low, unit_grads = lax.optimization_barrier(
        (grad_arrived, grad_mid_low, unit_grads)
    )
    grad_units = lax.psum_scatter(unit_grads, UNITS_GROUP, scatter_dimension=0, tiled=True)
    mixed = to_group(
        [
            jnp.concatenate(
                [
                    feed[order * tokens : (order + 1) * tokens],
                    grad_mid_low,
                    features[at],
                ]
            )
            for at, order in enumerate((2, 0, 1, 3))
        ],
        SQUARE,
    )

    marks = jnp.concatenate([onehot, far_onehot[None]], axis=0)
    marks = jnp.pad(marks, ((0, 7), (0, -bucket_count % 128)))
    grad_own, grad_other, grad_q, bucket_grad = kernel_call(
        functools.partial(attend_back_body, tokens, hd, repeat),
        [
            shape((4 * repeat * block, 2 * hd), F32),
            shape((4 * repeat * block, 2 * hd), BF16),
            shape((16, hd, tokens), BF16),
            shape((8, marks.shape[1]), F32),
        ],
        [coords, cuts, hvec, grad_arrived, queries, keys, keys_t, attended, lse, marks],
        [
            pltpu.VMEM((places + 2, block, 2 * tokens), F32),
            pltpu.VMEM((length, 2 * hd), F32),
            pltpu.VMEM((3, block, 2 * tokens), F32),
            pltpu.VMEM((places, 2 * hd, 4 * tokens), BF16),
            pltpu.VMEM((places, 4 * tokens, 2 * hd), BF16),
            pltpu.VMEM((places, 16, 2 * tokens), F32),
            pltpu.VMEM((2, hd, 2 * tokens), F32),
        ],
        scalars=2,
        micros=20,
    )
    mixed, grad_own = lax.optimization_barrier((mixed, grad_own))
    grad_pairs = (grad_own + swap(grad_other, "c", 1).astype(F32)).astype(BF16)
    grad_pairs = [
        grad_pairs[at * repeat * block : (at + 1) * repeat * block] for at in range(4)
    ]
    if repeat > 1:
        grad_pairs = [
            lax.psum_scatter(part, "r", scatter_dimension=0, tiled=True) for part in grad_pairs
        ]
    grad_pieces = [
        jnp.concatenate([grad_pairs[at], grad_q[4 * at : 4 * at + 4].reshape(4 * hd, tokens)])
        for at in range(4)
    ]
    mixed, grad_pieces = lax.optimization_barrier((mixed, grad_pieces))
    grad_pieces = to_group(grad_pieces, SQUARE)

    made = kernel_call(
        functools.partial(project_back_body, hd),
        [
            shape((4, tokens, width), BF16),
            shape((8, width), F32),
            shape((8 * hd, block), BF16),
            shape((4 * hd, block), BF16),
        ],
        [coords, *grad_pieces, normed_all, group_weights, gain_attention.reshape(1, width)],
        [pltpu.VMEM((block, 8 * hd), BF16), pltpu.VMEM((block, 4 * hd), BF16)],
        mebi=16,
    )
    normed_grads, gain_first_rows, pairs_t, queries_t = made
    normed_grads = lax.all_to_all(normed_grads, "z", split_axis=0, concat_axis=0, tiled=True)
    keep, send = kernel_call(
        functools.partial(head_grads_body, hd),
        [shape((4, hd // 2, 3 * width), BF16)] * 2,
        [coords, pairs_t, queries_t, normed_all],
    )
    layer_out = (middle + sum(part[:tokens].astype(F32) for part in mixed)).astype(BF16)
    grad_mid_all = jnp.concatenate([part[tokens : 2 * tokens] for part in mixed], axis=0)
    near = jnp.stack([part[2 * tokens :] for part in mixed]).reshape(4, hd // 2, 8, tokens)
    near = near.transpose(2, 1, 0, 3).reshape(4 * hd, block)
    out_grads = nn(near, grad_mid_all).astype(BF16)

    bucket_grad, keep, send, grad_units, out_grads = lax.optimization_barrier(
        (bucket_grad, keep, send, grad_units, out_grads)
    )
    out_grads = out_grads.reshape(2, 4, hd // 2, width)
    out_grads = (out_grads[0].astype(F32) + swap(out_grads[1], "c", 1).astype(F32)).astype(BF16)
    head_grads = (keep.astype(F32) + swap(send, "c", 1).astype(F32)).astype(BF16)
    head_mark = (jnp.arange(head_count) == head_at).astype(F32)
    bias_term = bucket_grad[0, :bucket_count, None] * head_mark[None, :]
    sums = jnp.concatenate([jnp.sum(gain_first_rows, axis=0), gain_second_term, bias_term.ravel()])
    sums = sums + swap(sums, "c", 1)
    sums = sum_everywhere(sums, SQUARE)
    head_grads = to_group([head_grads[at] for at in range(4)], SQUARE)
    normed_grads, head_grads, sums, out_grads = lax.optimization_barrier(
        (normed_grads, head_grads, sums, out_grads)
    )
    out_grads, sums = sum_over_z(out_grads, sums)
    head_grads = sum(part.astype(F32) for part in head_grads)
    if repeat > 1:
        sums = lax.psum(sums, "r")
        out_grads = lax.psum_scatter(
            out_grads.astype(BF16), "r", scatter_dimension=0, tiled=True
        ).astype(F32)
        head_grads = lax.psum_scatter(
            head_grads.astype(BF16), "r", scatter_dimension=0, tiled=True
        ).astype(F32)
    gain_first_grad, gain_second_grad = sums[:width], sums[width : 2 * width]
    bias_grad = sums[2 * width :].reshape(bucket_count, head_count)

    grad_inputs = kernel_call(
        finish_body,
        shape((tokens, width), BF16),
        [normed_grads, inputs[0], grad_middle, gain_attention.reshape(1, width)],
        scalars=0,
        micros=100,
        mebi=16,
    )
    unit_grads = grad_units.astype(F32)
    return (
        layer_out[None],
        grad_inputs[None],
        gain_first_grad,
        head_grads[:, :width],
        head_grads[:, width : 2 * width],
        head_grads[:, 2 * width :],
        out_grads,
        bias_grad,
        gain_second_grad,
        unit_grads[:, :width],
        unit_grads[:, width : 2 * width],
        unit_grads[:, 2 * width :],
    )


def solution(mesh):
    owners, runs = mesh.shape["ulysses"], mesh.shape["blk"]
    fine = Mesh(mesh.devices.reshape(2, owners // 2, 4, 2, runs // 8), EVERY)
    tokens = P(("z", "y", "r"), ("x", "c"), None)
    rows = P(EVERY, None)
    return jax.shard_map(
        body,
        mesh=fine,
        in_specs=(tokens, tokens) + (P(),) * 3 + (rows,) * 4 + (P(),) * 2 + (rows,) * 3,
        out_specs=(tokens, tokens, P()) + (rows,) * 4 + (P(),) * 2 + (rows,) * 3,
        check_vma=False,
    )
```

```python
import functools
import math

import jax
import jax.numpy as jnp
from jax import lax
from jax.experimental import pallas as pl
from jax.experimental.pallas import tpu as pltpu
from jax.sharding import Mesh
from jax.sharding import PartitionSpec as P

EPSILON = 1e-06
NEGATIVE = -1e30
HIGHEST = lax.Precision.HIGHEST
F32 = jnp.float32
BF16 = jnp.bfloat16
MEBI = 1024 * 1024
FEED_MEBI = 24
GELU_SCALE = math.sqrt(2.0 / math.pi)
GELU_CUBE = 0.044715
SQUARE = ("x", "y")
UNITS_GROUP = ("z", "c", "r")
EVERY = ("x", "c", "z", "y", "r")


def norm_scale(values):
    return lax.rsqrt(jnp.mean(values * values, axis=-1, keepdims=True) + EPSILON)


def norm_back(values, scaling, gain_vec, upstream):
    inner_sum = jnp.mean(values * gain_vec * upstream, axis=-1, keepdims=True)
    return scaling * gain_vec * upstream - values * scaling * scaling * scaling * inner_sum


def nt(left, right):
    return lax.dot_general(left, right, (((1,), (1,)), ((), ())), preferred_element_type=F32)


def nn(left, right):
    return lax.dot_general(left, right, (((1,), (0,)), ((), ())), preferred_element_type=F32)


def tn(left, right):
    return lax.dot_general(left, right, (((0,), (0,)), ((), ())), preferred_element_type=F32)


def swap(value, axis, mask):
    size = lax.axis_size(axis)
    return lax.ppermute(value, axis, [(at, at ^ mask) for at in range(size)])


def from_group(value, axis):
    return [value] + [swap(value, axis, mask) for mask in (1, 2, 3)]


def to_group(values, axis):
    return [values[0]] + [swap(values[mask], axis, mask) for mask in (1, 2, 3)]


def sum_everywhere(value, axis):
    first, second, third, fourth = from_group(value, axis)
    return (first + second) + (third + fourth)


def sum_over_z(rows, values):
    width = rows.shape[-1]
    lines = -(-values.size // width)
    padded = jnp.pad(values, (0, lines * width - values.size)).reshape(lines, width)
    high = lax.reduce_precision(padded, 8, 7)
    extra = jnp.concatenate([high, padded - high]).astype(BF16)
    extra = jnp.pad(extra, ((0, -2 * lines % 8), (0, 0)))
    arrived = to_group([jnp.concatenate([rows[at], extra]) for at in range(4)], "z")
    arrived = [part.astype(F32) for part in arrived]
    count = rows.shape[1]
    tails = [part[count : count + lines] + part[count + lines : count + 2 * lines] for part in arrived]
    total = (tails[0] + tails[1]) + (tails[2] + tails[3])
    return sum(part[:count] for part in arrived), total.ravel()[: values.size]


def kernel_call(body, out_shapes, inputs, scratch=(), scalars=1, micros=4, mebi=60):
    in_specs = [pl.BlockSpec(memory_space=pltpu.SMEM)] * scalars
    in_specs += [pl.BlockSpec(memory_space=pltpu.VMEM)] * (len(inputs) - scalars)
    return pl.pallas_call(
        body,
        out_shape=out_shapes,
        in_specs=in_specs,
        out_specs=jax.tree.map(lambda _: pl.BlockSpec(memory_space=pltpu.VMEM), out_shapes),
        scratch_shapes=list(scratch),
        compiler_params=pltpu.CompilerParams(vmem_limit_bytes=mebi * MEBI),
        cost_estimate=pl.CostEstimate(
            flops=int(micros * 1.15e9), bytes_accessed=1 << 20, transcendentals=0
        ),
    )(*inputs)


def shape(dims, dtype):
    return jax.ShapeDtypeStruct(dims, dtype)


def pack_body(*refs):
    own_in, gain, out_rows = refs[:3]
    heads, units = refs[3:6], refs[6:9]
    message, joined, joined_units = refs[9:]
    tokens, width = own_in.shape
    values = own_in[...].astype(F32)
    message[0:tokens, :] = (values * norm_scale(values) * gain[...]).astype(BF16)
    message[tokens:, :] = out_rows[...]
    for at in range(3):
        joined[:, at * width : (at + 1) * width] = heads[at][...]
        joined_units[:, at * width : (at + 1) * width] = units[at][...]


def anchor_body(*refs):
    refs[-1][...] = jnp.zeros_like(refs[-1])


def anchor(values, micros):
    return pl.pallas_call(
        anchor_body,
        out_shape=shape((8, 128), F32),
        in_specs=[pl.BlockSpec(memory_space=pl.ANY)] * len(values),
        out_specs=pl.BlockSpec(memory_space=pltpu.VMEM),
        cost_estimate=pl.CostEstimate(
            flops=int(micros * 1.15e9), bytes_accessed=1 << 20, transcendentals=0
        ),
    )(*values)


def qkv_body(hd, coords, *refs):
    blocks, parts, other_rows, cot_own, pieces = refs[:4], refs[4:8], refs[8], refs[9], refs[11:15]
    rows_all, weights, onward = refs[15:18]
    c_at, y_at = coords[1], coords[3]
    width, half = rows_all.shape[1], hd // 2
    tokens = rows_all.shape[0] // 4
    for at in range(4):
        rows_all[at * tokens : (at + 1) * tokens, :] = blocks[at][0:tokens, :]
        start = tokens + at * half
        onward[start : start + half, :] = blocks[at][tokens:, :]
    onward[0:tokens, :] = cot_own[...]
    for core in range(2):
        for dest in range(4):
            column = y_at ^ c_at ^ core
            place = (dest >> 1) * 2 + column
            shift = pl.multiple_of((y_at ^ (dest & 1)) * half, half)
            source = other_rows.at[dest * half : (dest + 1) * half] if core else parts[dest]
            for kind, first, step in ((0, 8 * hd, hd), (1, 0, 2 * hd), (2, hd, 2 * hd)):
                start = pl.multiple_of(first + place * step + shift, half)
                weights[pl.ds(start, half), :] = source[:, kind * width : (kind + 1) * width]
    normed = rows_all[...]
    pairs = nt(normed, weights[0 : 8 * hd, :]).astype(BF16)
    queries = nt(weights[8 * hd : 12 * hd, :], normed).astype(BF16)
    for dest in range(4):
        pieces[dest][0 : 4 * tokens, :] = pairs[:, dest * 2 * hd : (dest + 1) * 2 * hd]
        for at in range(4):
            pieces[dest][4 * tokens + at * hd : 4 * tokens + (at + 1) * hd, :] = queries[
                dest * hd : (dest + 1) * hd, at * tokens : (at + 1) * tokens
            ]


def bias_tiles(hvec, tokens):
    tiles = {}
    for at, diff in enumerate((-1, 0, 1)):
        spread = jnp.broadcast_to(hvec[at : at + 1, :], (tokens, 2 * tokens))
        tiles[diff] = pltpu.roll(spread, 0, 1, stride=1, stride_axis=0)[:, :tokens]
    return tiles


def fill_bias(hvec_ref, bias, cuts, repeat, c_at, r_at, tokens):
    tiles = bias_tiles(hvec_ref[...], tokens)
    zero = jnp.zeros((tokens, tokens), F32)
    bias[0] = jnp.zeros(bias.shape[1:], F32)
    for rows in range(8):
        for half in range(2):
            diff = rows - 4 - 2 * half
            even, odd = tiles.get(diff, zero), tiles.get(diff - 1, zero)
            row = (rows % 4) * tokens
            bias[1 + rows // 4, row : row + tokens, half * tokens : (half + 1) * tokens] = (
                jnp.where(c_at == 0, even, odd)
            )

    def mask(back, carry):
        place = bias.shape[0] - 3 - back
        allowed = allowed_mask(cuts, place * repeat + r_at, c_at, tokens)
        bias[2 + place] = jnp.where(allowed, bias[2], NEGATIVE)
        return carry

    lax.fori_loop(0, bias.shape[0] - 2, mask, 0)


def bias_slab(bias, place, run, at):
    return bias[jnp.where(at == run, 2 + place, jnp.where(at == run - 1, 1, 0))]


def allowed_mask(cuts, run, c_at, tokens):
    rows, cols = 4 * tokens, 2 * tokens
    key_at = lax.broadcasted_iota(jnp.int32, (rows, cols), 0)
    query_at = lax.broadcasted_iota(jnp.int32, (rows, cols), 1)
    key_window = key_at >= 2 * tokens
    query_window = query_at >= tokens
    key_in = jnp.where(key_window, key_at - 2 * tokens, key_at)
    query_in = jnp.where(query_window, query_at - tokens, query_at) + c_at * tokens
    cut = jnp.where(query_window, cuts[2 * run + 1], cuts[2 * run])
    inside = (key_in < cut) | (query_in >= cut)
    before = jnp.logical_and(jnp.logical_not(key_window), query_window)
    same = key_window == query_window
    return before | (same & inside)


def each_slot(run_low, run_high, repeat, step):
    def one(slot, carry):
        high = (slot > run_low).astype(jnp.int32)
        at = jnp.where(slot > run_low, slot - run_low - 1, slot)
        step(slot, high, at)
        return carry

    count = run_low + run_high + 2
    if repeat == 1:
        for slot in range(9):
            one(jnp.int32(slot), 0)
    else:
        lax.fori_loop(0, count, one, 0)


def chunk(at, block):
    return pl.ds(pl.multiple_of(at * block, block), block)


def fold_rows(values, how):
    rows, cols = values.shape
    return how(values.reshape(rows // 8, 8, cols), axis=0)


def attend_body(tokens, hd, repeat, coords, cuts, hvec, *refs):
    pieces = refs[:4]
    own, other, refs = (pieces, *refs[4:5], refs[5:]) if repeat == 1 else (refs[4:8], refs[8], refs[9:])
    out, lse, attended, keys, keys_t, queries, scores, bias, padded, peaks, totals, mixes = refs
    x_at, c_at, z_at, y_at, r_at = (coords[at] for at in range(5))
    block = 4 * tokens
    for dest in range(4):
        x_from, y_from = x_at ^ (dest >> 1), y_at ^ (dest & 1)
        for at in range(4):
            place = (z_at ^ at) * 2 + y_from
            for rep in range(repeat):
                run = place * repeat + rep
                base = run * block + x_from * 2 * tokens
                source = slice(rep * block + at * tokens, rep * block + (at + 1) * tokens)
                keys[pl.ds(pl.multiple_of(base + c_at * tokens, tokens), tokens), :] = own[dest][
                    source, :
                ]
                start = (dest * repeat + rep) * block + at * tokens
                keys[pl.ds(pl.multiple_of(base + (1 - c_at) * tokens, tokens), tokens), :] = other[
                    start : start + tokens, :
                ]
            start = block + at * hd
            queries[place, :, pl.ds(pl.multiple_of(x_from * tokens, tokens), tokens)] = pieces[
                dest
            ][start : start + hd, :]
    fill_bias(hvec, bias, cuts, repeat, c_at, r_at, tokens)

    def turn(at, carry):
        keys_t[at] = keys[chunk(at, block), :].T
        return carry

    lax.fori_loop(0, keys.shape[0] // block, turn, 0)
    places = queries.shape[0]
    padded[:, 0:hd, :] = queries[...]
    padded[:, hd:, :] = jnp.zeros_like(padded[:, hd:, :])

    def pair(low, carry):
        place_of = (low, places - 1 - low)
        run_of = tuple(place * repeat + r_at for place in place_of)
        peaks[...] = jnp.full_like(peaks, NEGATIVE)
        totals[...] = jnp.zeros_like(totals)
        mixes[...] = jnp.zeros_like(mixes)

        def score(slot, high, at):
            place = jnp.where(high == 1, place_of[1], place_of[0])
            run = place * repeat + r_at
            values = nn(keys[chunk(at, block), :], padded[place])
            values = values + bias_slab(bias, place, run, at)
            scores[slot] = values
            peaks[high] = jnp.maximum(peaks[high], fold_rows(values, jnp.max))

        each_slot(*run_of, repeat, score)
        for high in range(2):
            top = jnp.max(peaks[high], axis=0, keepdims=True)
            peaks[high] = jnp.broadcast_to(top, peaks.shape[1:])

        def mix(slot, high, at):
            weights = jnp.exp(scores[slot] - peaks[high][0:1, :])
            totals[high] += fold_rows(weights, jnp.sum)
            mixes[high] += nn(keys_t[at, hd:, :], weights.astype(BF16))

        each_slot(*run_of, repeat, mix)
        for high, place in enumerate(place_of):
            total = jnp.sum(totals[high], axis=0, keepdims=True)
            mixed = mixes[high] / total
            attended[place] = mixed
            lse[place] = peaks[high] + jnp.log(jnp.broadcast_to(total, peaks.shape[1:]))
            part = mixed.astype(BF16)
            for half in range(2):
                out[half * 8 + (place & 1) * 4 + (place >> 1)] = part[
                    :, half * tokens : (half + 1) * tokens
                ]
        return carry

    lax.fori_loop(0, places // 2, pair, 0)


def attend_back_body(tokens, hd, repeat, coords, cuts, hvec, *refs):
    arrived, queries, keys, keys_t, attended, lse, marks = refs[:7]
    grad_own, grad_other, grad_q, bucket_out = refs[7:11]
    bias, grad_keys, table_acc, left, right, shifts, grad_queries = refs[11:]
    x_at, c_at, z_at, y_at, r_at = (coords[at] for at in range(5))
    block = 4 * tokens
    places = queries.shape[0]
    fill_bias(hvec, bias, cuts, repeat, c_at, r_at, tokens)
    grad_keys[...] = jnp.zeros_like(grad_keys)
    table_acc[...] = jnp.zeros_like(table_acc)

    def prepare(place, carry):
        query_t = queries[place]
        upstream_t = jnp.concatenate(
            [arrived[half * 8 + (place & 1) * 4 + (place >> 1)] for half in range(2)], axis=1
        )
        zero = jnp.zeros_like(query_t)
        query_pad = jnp.concatenate([query_t, zero], axis=0)
        upstream_pad = jnp.concatenate([zero, upstream_t], axis=0)
        left[place, :, 0 : 2 * tokens] = query_pad
        left[place, :, 2 * tokens :] = upstream_pad
        right[place, 0 : 2 * tokens, :] = query_pad.T
        right[place, 2 * tokens :, :] = upstream_pad.T
        shifts[place, 0:8, :] = lse[place]
        delta = jnp.sum(upstream_t.astype(F32) * attended[place], axis=0, keepdims=True)
        shifts[place, 8:16, :] = jnp.broadcast_to(delta, (8, 2 * tokens))
        return carry

    lax.fori_loop(0, places, prepare, 0)

    def pair(low, carry):
        place_of = (low, places - 1 - low)
        run_of = tuple(place * repeat + r_at for place in place_of)
        grad_queries[...] = jnp.zeros_like(grad_queries)

        def step(slot, high, at):
            place = jnp.where(high == 1, place_of[1], place_of[0])
            run = place * repeat + r_at
            rows = chunk(at, block)
            both = nn(keys[rows, :], left[place])
            values = both[:, 0 : 2 * tokens] + bias_slab(bias, place, run, at)
            probs = jnp.exp(values - shifts[place, 0:1, :])
            grad_scores = probs * (both[:, 2 * tokens :] - shifts[place, 8:9, :])
            grad_low = grad_scores.astype(BF16)
            grad_keys[rows, :] += nn(
                jnp.concatenate([grad_low, probs.astype(BF16)], axis=1), right[place]
            )
            grad_queries[high] += nn(keys_t[at, :hd, :], grad_low)
            kind = jnp.where(at == run, 2, jnp.where(at == run - 1, 1, 0))
            table_acc[kind] += grad_low.astype(F32)

        each_slot(*run_of, repeat, step)
        for high, place in enumerate(place_of):
            low_part = grad_queries[high].astype(BF16)
            for half in range(2):
                part = low_part[:, half * tokens : (half + 1) * tokens]
                dest = (x_at ^ half) * 2 + ((place & 1) ^ y_at)
                grad_q[dest * 4 + ((place >> 1) ^ z_at)] = part
        return carry

    lax.fori_loop(0, places // 2, pair, 0)

    for dest in range(4):
        x_from, y_from = x_at ^ (dest >> 1), y_at ^ (dest & 1)
        for at in range(4):
            place = (z_at ^ at) * 2 + y_from
            for rep in range(repeat):
                base = (place * repeat + rep) * block + x_from * 2 * tokens
                start = (dest * repeat + rep) * block + at * tokens
                target = slice(start, start + tokens)
                grad_own[target, :] = grad_keys[
                    pl.ds(pl.multiple_of(base + c_at * tokens, tokens), tokens), :
                ]
                grad_other[target, :] = grad_keys[
                    pl.ds(pl.multiple_of(base + (1 - c_at) * tokens, tokens), tokens), :
                ].astype(BF16)

    def tile_at(rows, half):
        row = (rows % 4) * tokens
        return table_acc[
            1 + rows // 4, row : row + tokens, half * tokens : (half + 1) * tokens
        ]

    spots = [(rows, half) for rows in range(8) for half in range(2)]
    flip = (
        lax.broadcasted_iota(jnp.int32, (tokens, tokens), 0)
        + lax.broadcasted_iota(jnp.int32, (tokens, tokens), 1)
        == tokens - 1
    ).astype(F32)
    far_even = jnp.zeros((tokens, tokens), F32)
    far_odd = jnp.zeros((tokens, tokens), F32)
    for rows, half in spots:
        diff = rows - 4 - 2 * half
        if diff <= -2:
            far_even += tile_at(rows, half)
        if diff - 1 <= -2:
            far_odd += tile_at(rows, half)
    extra = fold_rows(jnp.where(c_at == 0, far_even, far_odd), jnp.sum)
    far_rows = fold_rows(table_acc[0], jnp.sum)
    far_rows = far_rows[:, :tokens] + far_rows[:, tokens:] + extra
    total = jnp.sum(jnp.sum(far_rows, axis=0, keepdims=True), axis=1, keepdims=True)
    last = 3 * 2 * tokens
    bucket = total * marks[last : last + 1, :]
    for index, diff in enumerate((-1, 0, 1)):
        even = sum(tile_at(rows, half) for rows, half in spots if rows - 4 - 2 * half == diff)
        odd = sum(tile_at(rows, half) for rows, half in spots if rows - 5 - 2 * half == diff)
        tile = jnp.where(c_at == 0, even, odd)
        turned = jnp.dot(flip, tile, precision=HIGHEST, preferred_element_type=F32)
        wide = jnp.concatenate([turned, jnp.zeros_like(turned)], axis=1)
        wide = pltpu.roll(wide, tokens + 1, 1, stride=1, stride_axis=0)
        diagonals = jnp.broadcast_to(jnp.sum(wide, axis=0, keepdims=True), (8, 2 * tokens))
        part = marks[index * 2 * tokens : (index + 1) * 2 * tokens, :]
        bucket = bucket + jnp.dot(
            diagonals, part, precision=HIGHEST, preferred_element_type=F32
        )[0:1, :]
    bucket_out[...] = jnp.broadcast_to(bucket, bucket_out.shape)


def project_back_body(hd, coords, *refs):
    pieces, (rows_all, weights, gain), out = refs[:4], refs[4:7], refs[7]
    gain_out, pairs_t, queries_t, pairs, queries = refs[8:]
    tokens, width = out.shape[1:]
    z_at = coords[2]
    for dest in range(4):
        lanes = slice(dest * 2 * hd, (dest + 1) * 2 * hd)
        part = pieces[dest][0 : 4 * tokens, :]
        pairs[:, lanes] = part
        pairs_t[lanes, :] = part.T
        for at in range(4):
            queries_t[dest * hd : (dest + 1) * hd, at * tokens : (at + 1) * tokens] = pieces[dest][
                4 * tokens + at * hd : 4 * tokens + (at + 1) * hd, :
            ]
    queries[...] = queries_t[...].T
    grad = nn(pairs[...], weights[0 : 8 * hd, :]) + nn(queries[...], weights[8 * hd :, :])
    unit = rows_all[...].astype(F32) / gain[...]
    gain_out[...] = fold_rows(grad * unit, jnp.sum)
    for at in range(4):
        out[z_at ^ at] = grad[at * tokens : (at + 1) * tokens, :].astype(BF16)


def head_grads_body(hd, coords, pairs_t, queries_t, rows_all, keep, send):
    c_at, y_at = coords[1], coords[3]
    width = rows_all.shape[1]
    half = hd // 2
    normed = rows_all[...]
    pair_rows = nn(pairs_t[...], normed).astype(BF16)
    query_rows = nn(queries_t[...], normed).astype(BF16)
    for dest in range(4):
        other = (y_at ^ (dest & 1)) ^ c_at

        def put(target, dest=dest):
            for part in range(2):
                place = (dest >> 1) * 2 + (y_at ^ part)
                for kind, rows, first in (
                    (0, query_rows, dest * hd),
                    (1, pair_rows, dest * 2 * hd),
                    (2, pair_rows, dest * 2 * hd + hd),
                ):
                    first += part * half
                    target[place, :, kind * width : (kind + 1) * width] = rows[
                        first : first + half, :
                    ]

        pl.when(other == 0)(functools.partial(put, keep))
        pl.when(other == 1)(functools.partial(put, send))


def output_body(hd, coords, *refs):
    arrived, own_in, gain, here, other, middle_out, normed_out, weights, features = refs
    x_at, c_at, z_at, y_at = coords[0], coords[1], coords[2], coords[3]
    half, tokens = hd // 2, arrived.shape[1]
    for core, source in enumerate((here, other)):
        for dest in range(4):
            for near in range(4):
                head = ((x_at ^ (dest >> 1)) * 2 + (c_at ^ core)) * 4 + (z_at ^ near)
                start = pl.multiple_of(head * hd + (y_at ^ (dest & 1)) * half, half)
                first = (dest * 4 + near) * half
                weights[pl.ds(start, half), :] = source[first : first + half, :]
    for dest in range(4):
        for core in range(2):
            for near in range(4):
                head = ((x_at ^ (dest >> 1)) * 2 + (c_at ^ core)) * 4 + (z_at ^ near)
                start = pl.multiple_of(head * hd + (y_at ^ (dest & 1)) * half, half)
                lanes = slice((core * 4 + near) * tokens, (core * 4 + near + 1) * tokens)
                features[dest, :, lanes] = arrived[pl.ds(start, half), :]
    middle = own_in[...].astype(F32) + nn(arrived[...].T, weights[...])
    middle_out[...] = middle
    normed_out[...] = (middle * norm_scale(middle) * gain[...]).astype(BF16)


def finish_body(*refs):
    parts, own_in, grad_middle, gain, out = refs
    values = own_in[...].astype(F32)
    grad = sum(parts[at].astype(F32) for at in range(4))
    out[...] = (
        grad_middle[...] + norm_back(values, norm_scale(values), gain[...], grad)
    ).astype(BF16)


def feed_body(count, *refs):
    blocks, cot, rows = refs[:count], refs[count], refs[count + 1]
    outs = refs[-5 - count : -5]
    mid_out, gate_out, up_out, hidden_out, acc = refs[-5:]
    tokens, width = blocks[0].shape
    for at in range(count):
        mid_out[at * tokens : (at + 1) * tokens, :] = blocks[at][...]
    units = rows.shape[0]
    for start in range(0, units, 256):
        part = slice(start, min(start + 256, units))
        gate_rows = rows[part, 0:width]
        up_rows = rows[part, width : 2 * width]
        gate_act = nt(mid_out[...], gate_rows)
        up_act = nt(mid_out[...], up_rows)
        upstream = nt(cot[...], rows[part, 2 * width :])
        square = gate_act * gate_act
        curve = jnp.tanh(GELU_SCALE * gate_act * (1.0 + GELU_CUBE * square))
        half = 0.5 + 0.5 * curve
        gelu = gate_act * half
        slope = half + (0.5 * GELU_SCALE) * gate_act * (1.0 - curve * curve) * (
            1.0 + 3.0 * GELU_CUBE * square
        )
        hidden_out[:, part] = (gelu * up_act).astype(BF16)
        gate_low = (upstream * up_act * slope).astype(BF16)
        up_low = (upstream * gelu).astype(BF16)
        gate_out[:, part] = gate_low
        up_out[:, part] = up_low
        step = nn(gate_low, gate_rows) + nn(up_low, up_rows)
        if start == 0:
            acc[...] = step
        else:
            acc[...] += step
    for at in range(count):
        outs[at][...] = acc[at * tokens : (at + 1) * tokens, :].astype(BF16)


def feed_call(blocks, place, cot_all, unit_rows, kept):
    count, (tokens, width) = len(blocks), blocks[0].shape
    total, units = cot_all.shape[0], unit_rows.shape[0]
    size = count * tokens
    once = pl.Buffered(1)

    def whole(dims):
        return pl.BlockSpec(dims, lambda i: (0, 0), pipeline_mode=once)

    def mine(columns):
        return pl.BlockSpec((size, columns), lambda i: (place, 0), pipeline_mode=once)

    made = pl.pallas_call(
        functools.partial(feed_body, count),
        grid=(1,),
        in_specs=[whole((tokens, width))] * count
        + [mine(width), whole(unit_rows.shape)]
        + [pl.BlockSpec(memory_space=pl.ANY)] * len(kept),
        out_specs=[whole((tokens, width))] * count + [mine(width)] + [mine(units)] * 3,
        out_shape=[shape((tokens, width), BF16)] * count
        + [shape((total, width), BF16)]
        + [shape((total, units), BF16)] * 3,
        scratch_shapes=[pltpu.VMEM((size, width), F32)],
        input_output_aliases={count + 2 + at: count + at for at in range(len(kept))},
        compiler_params=pltpu.CompilerParams(vmem_limit_bytes=MEBI * FEED_MEBI),
        cost_estimate=pl.CostEstimate(
            flops=int(2.5e9 * count), bytes_accessed=1 << 20, transcendentals=0
        ),
    )(*blocks, cot_all, unit_rows, *kept)
    return made[:count], made[count:]


def body(
    inputs,
    cotangent,
    segment_ids,
    bucket_table,
    gain_attention,
    query_weight,
    key_weight,
    value_weight,
    output_weight,
    bucket_bias,
    gain_feedforward,
    gate_weight,
    up_weight,
    down_weight,
):
    tokens, width = inputs.shape[1:]
    repeat = lax.axis_size("r")
    x_at, c_at, z_at, y_at, r_at = (lax.axis_index(name) for name in EVERY)
    coords = jnp.stack([x_at, c_at, z_at, y_at, r_at]).astype(jnp.int32)
    bucket_count, head_count = bucket_bias.shape
    hd = width // head_count
    block = 4 * tokens
    length = segment_ids.size
    reach = (bucket_table.shape[0] - 1) // 2
    assert reach == tokens and lax.axis_size("x") == lax.axis_size("c") == 2

    cot_own = cotangent[0]
    out_rows = output_weight
    if repeat > 1:
        out_rows = lax.all_gather(out_rows, "r", axis=0, tiled=True)
    message, joined, units = kernel_call(
        pack_body,
        [
            shape((tokens + hd // 2, width), BF16),
            shape((query_weight.shape[0], 3 * width), BF16),
            shape((gate_weight.shape[0], 3 * width), BF16),
        ],
        [
            inputs[0],
            gain_attention.reshape(1, width),
            out_rows,
            query_weight,
            key_weight,
            value_weight,
            gate_weight,
            up_weight,
            down_weight,
        ],
        scalars=0,
        micros=2,
    )
    messages = from_group(message, "z")
    if repeat > 1:
        joined = lax.all_gather(joined, "r", axis=0, tiled=True)
    head_rows = from_group(joined, SQUARE)
    other_rows = swap(jnp.concatenate(head_rows, axis=0), "c", 1)

    windows = segment_ids.reshape(-1, 2 * tokens)
    cuts = jnp.sum((windows < windows[:, -1:]).astype(jnp.int32), axis=1)
    turned = bucket_table[::-1]
    low_half, high_half = turned[reach : 2 * reach], turned[:reach]
    spots = jnp.concatenate(
        [
            jnp.broadcast_to(bucket_table[:1], (reach,)),
            low_half,
            low_half,
            high_half,
            high_half,
            jnp.broadcast_to(bucket_table[2 * reach :], (reach,)),
        ]
    )
    buckets = jnp.arange(bucket_count, dtype=jnp.int32)
    onehot = (spots[:, None] == buckets[None, :]).astype(F32)
    far_onehot = (bucket_table[0] == buckets).astype(F32)
    head_at = (x_at * 2 + y_at) * 4 + z_at
    bias_col = lax.dynamic_slice_in_dim(bucket_bias, head_at, 1, 1)[:, 0]
    diag = jnp.dot(onehot, bias_col, precision=HIGHEST) - jnp.sum(far_onehot * bias_col)
    hvec = jnp.pad(diag.reshape(3, 2 * reach), ((0, 5), (0, 0)))

    messages, hvec, cuts, coords, units = lax.optimization_barrier(
        (messages, hvec, cuts, coords, units)
    )
    unit_rows = lax.all_gather(units, UNITS_GROUP, axis=0, tiled=True)
    down_piece = unit_rows[:, 2 * width :]

    made = kernel_call(
        functools.partial(qkv_body, hd),
        [shape((block + 4 * hd, 2 * hd), BF16)] * 4
        + [
            shape((block, width), BF16),
            shape((12 * hd, width), BF16),
            shape((tokens + 2 * hd, width), BF16),
        ],
        [coords, *messages, *head_rows, other_rows, cot_own, anchor(messages, 30)],
    )
    pieces, (normed_all, group_weights, sent) = made[:4], made[4:]
    pieces = to_group(pieces, SQUARE)

    own = [piece[:block] for piece in pieces]
    other = swap(jnp.concatenate(own, axis=0), "c", 1)
    if repeat == 1:
        arrays = [*pieces, other]
    else:
        own = [lax.all_gather(part, "r", axis=0, tiled=True) for part in own]
        other = other.reshape(4, block, 2 * hd)
        other = [lax.all_gather(other[at], "r", axis=0, tiled=True) for at in range(4)]
        arrays = [*pieces, *own, jnp.concatenate(other, axis=0)]
    places = 8
    out_t, lse, attended, keys, keys_t, queries = kernel_call(
        functools.partial(attend_body, tokens, hd, repeat),
        [
            shape((16, hd, tokens), BF16),
            shape((places, 8, 2 * tokens), F32),
            shape((places, hd, 2 * tokens), F32),
            shape((length, 2 * hd), BF16),
            shape((length // block, 2 * hd, block), BF16),
            shape((places, hd, 2 * tokens), BF16),
        ],
        [coords, cuts, hvec, *arrays],
        [
            pltpu.VMEM((9 * repeat, block, 2 * tokens), F32),
            pltpu.VMEM((places + 2, block, 2 * tokens), F32),
            pltpu.VMEM((places, 2 * hd, 2 * tokens), BF16),
            pltpu.VMEM((2, 8, 2 * tokens), F32),
            pltpu.VMEM((2, 8, 2 * tokens), F32),
            pltpu.VMEM((2, hd, 2 * tokens), F32),
        ],
        scalars=2,
        micros=20,
    )
    sent, _ = lax.optimization_barrier((sent, pieces))
    parts = from_group(sent, SQUARE)
    arrived = lax.all_to_all(out_t, ("x", "y", "z"), split_axis=0, concat_axis=0, tiled=True)
    parts, arrived = lax.optimization_barrier((parts, arrived))
    cot_all = jnp.concatenate([parts[at][:tokens] for at in (1, 2, 0, 3)], axis=0)
    out_here = jnp.concatenate([part[tokens:] for part in parts], axis=0)
    out_other = swap(out_here, "c", 1)

    middle, normed_mid, out_full, features = kernel_call(
        functools.partial(output_body, hd),
        [
            shape((tokens, width), F32),
            shape((tokens, width), BF16),
            shape((width, width), BF16),
            shape((4, hd // 2, 8 * tokens), BF16),
        ],
        [
            coords,
            arrived.reshape(width, tokens),
            inputs[0],
            gain_feedforward.reshape(1, width),
            out_here,
            out_other,
        ],
    )
    scale_second = norm_scale(middle)
    own, second, third, fourth = from_group(normed_mid, SQUARE)

    (grad_own_part,), kept = feed_call([own], 2, cot_all, unit_rows, [])
    grad_near, kept = feed_call([second, third], 0, cot_all, unit_rows, kept)
    (grad_last,), kept = feed_call([fourth], 3, cot_all, unit_rows, kept)
    mid_all, gate_low, up_low, hidden = kept
    grad_parts = to_group([grad_own_part, *grad_near, grad_last], SQUARE)
    unit_grads = jnp.concatenate(
        [tn(gate_low, mid_all), tn(up_low, mid_all), tn(hidden, cot_all)], axis=1
    ).astype(BF16)
    feed = nn(hidden, down_piece).astype(BF16)
    grad_parts, unit_grads, feed = lax.optimization_barrier((grad_parts, unit_grads, feed))
    grad_norm_mid = sum(part.astype(F32) for part in grad_parts)
    feed, grad_norm_mid = lax.optimization_barrier((feed, grad_norm_mid))

    grad_middle = cot_own.astype(F32) + norm_back(
        middle, scale_second, gain_feedforward, grad_norm_mid
    )
    gain_second_term = jnp.sum(grad_norm_mid * middle * scale_second, axis=0)
    grad_mid_low = grad_middle.astype(BF16)
    grad_attended = nt(out_full, grad_mid_low).astype(BF16)
    grad_arrived = lax.all_to_all(
        grad_attended.reshape(16, hd, tokens),
        ("x", "y", "z"),
        split_axis=0,
        concat_axis=0,
        tiled=True,
    )
    grad_arrived, grad_mid_low, unit_grads = lax.optimization_barrier(
        (grad_arrived, grad_mid_low, unit_grads)
    )
    grad_units = lax.psum_scatter(unit_grads, UNITS_GROUP, scatter_dimension=0, tiled=True)
    mixed = to_group(
        [
            jnp.concatenate(
                [
                    feed[order * tokens : (order + 1) * tokens],
                    grad_mid_low,
                    features[at],
                ]
            )
            for at, order in enumerate((2, 0, 1, 3))
        ],
        SQUARE,
    )

    marks = jnp.concatenate([onehot, far_onehot[None]], axis=0)
    marks = jnp.pad(marks, ((0, 7), (0, -bucket_count % 128)))
    grad_own, grad_other, grad_q, bucket_grad = kernel_call(
        functools.partial(attend_back_body, tokens, hd, repeat),
        [
            shape((4 * repeat * block, 2 * hd), F32),
            shape((4 * repeat * block, 2 * hd), BF16),
            shape((16, hd, tokens), BF16),
            shape((8, marks.shape[1]), F32),
        ],
        [coords, cuts, hvec, grad_arrived, queries, keys, keys_t, attended, lse, marks],
        [
            pltpu.VMEM((places + 2, block, 2 * tokens), F32),
            pltpu.VMEM((length, 2 * hd), F32),
            pltpu.VMEM((3, block, 2 * tokens), F32),
            pltpu.VMEM((places, 2 * hd, 4 * tokens), BF16),
            pltpu.VMEM((places, 4 * tokens, 2 * hd), BF16),
            pltpu.VMEM((places, 16, 2 * tokens), F32),
            pltpu.VMEM((2, hd, 2 * tokens), F32),
        ],
        scalars=2,
        micros=40,
    )
    mixed, grad_own = lax.optimization_barrier((mixed, grad_own))
    grad_pairs = (grad_own + swap(grad_other, "c", 1).astype(F32)).astype(BF16)
    grad_pairs = [
        grad_pairs[at * repeat * block : (at + 1) * repeat * block] for at in range(4)
    ]
    if repeat > 1:
        grad_pairs = [
            lax.psum_scatter(part, "r", scatter_dimension=0, tiled=True) for part in grad_pairs
        ]
    grad_pieces = [
        jnp.concatenate([grad_pairs[at], grad_q[4 * at : 4 * at + 4].reshape(4 * hd, tokens)])
        for at in range(4)
    ]
    mixed, grad_pieces = lax.optimization_barrier((mixed, grad_pieces))
    grad_pieces = to_group(grad_pieces, SQUARE)

    made = kernel_call(
        functools.partial(project_back_body, hd),
        [
            shape((4, tokens, width), BF16),
            shape((8, width), F32),
            shape((8 * hd, block), BF16),
            shape((4 * hd, block), BF16),
        ],
        [coords, *grad_pieces, normed_all, group_weights, gain_attention.reshape(1, width)],
        [pltpu.VMEM((block, 8 * hd), BF16), pltpu.VMEM((block, 4 * hd), BF16)],
        mebi=16,
    )
    normed_grads, gain_first_rows, pairs_t, queries_t = made
    normed_grads = lax.all_to_all(normed_grads, "z", split_axis=0, concat_axis=0, tiled=True)
    keep, send = kernel_call(
        functools.partial(head_grads_body, hd),
        [shape((4, hd // 2, 3 * width), BF16)] * 2,
        [coords, pairs_t, queries_t, normed_all],
    )
    layer_out = (middle + sum(part[:tokens].astype(F32) for part in mixed)).astype(BF16)
    grad_mid_all = jnp.concatenate([part[tokens : 2 * tokens] for part in mixed], axis=0)
    near = jnp.stack([part[2 * tokens :] for part in mixed]).reshape(4, hd // 2, 8, tokens)
    near = near.transpose(2, 1, 0, 3).reshape(4 * hd, block)
    out_grads = nn(near, grad_mid_all).astype(BF16)

    bucket_grad, keep, send, grad_units, out_grads = lax.optimization_barrier(
        (bucket_grad, keep, send, grad_units, out_grads)
    )
    out_grads = out_grads.reshape(2, 4, hd // 2, width)
    out_grads = (out_grads[0].astype(F32) + swap(out_grads[1], "c", 1).astype(F32)).astype(BF16)
    head_grads = (keep.astype(F32) + swap(send, "c", 1).astype(F32)).astype(BF16)
    head_mark = (jnp.arange(head_count) == head_at).astype(F32)
    bias_term = bucket_grad[0, :bucket_count, None] * head_mark[None, :]
    sums = jnp.concatenate([jnp.sum(gain_first_rows, axis=0), gain_second_term, bias_term.ravel()])
    sums = sums + swap(sums, "c", 1)
    sums = sum_everywhere(sums, SQUARE)
    head_grads = to_group([head_grads[at] for at in range(4)], SQUARE)
    normed_grads, head_grads, sums, out_grads = lax.optimization_barrier(
        (normed_grads, head_grads, sums, out_grads)
    )
    out_grads, sums = sum_over_z(out_grads, sums)
    head_grads = sum(part.astype(F32) for part in head_grads)
    if repeat > 1:
        sums = lax.psum(sums, "r")
        out_grads = lax.psum_scatter(
            out_grads.astype(BF16), "r", scatter_dimension=0, tiled=True
        ).astype(F32)
        head_grads = lax.psum_scatter(
            head_grads.astype(BF16), "r", scatter_dimension=0, tiled=True
        ).astype(F32)
    gain_first_grad, gain_second_grad = sums[:width], sums[width : 2 * width]
    bias_grad = sums[2 * width :].reshape(bucket_count, head_count)

    grad_inputs = kernel_call(
        finish_body,
        shape((tokens, width), BF16),
        [normed_grads, inputs[0], grad_middle, gain_attention.reshape(1, width)],
        scalars=0,
        micros=100,
        mebi=16,
    )
    unit_grads = grad_units.astype(F32)
    return (
        layer_out[None],
        grad_inputs[None],
        gain_first_grad,
        head_grads[:, :width],
        head_grads[:, width : 2 * width],
        head_grads[:, 2 * width :],
        out_grads,
        bias_grad,
        gain_second_grad,
        unit_grads[:, :width],
        unit_grads[:, width : 2 * width],
        unit_grads[:, 2 * width :],
    )


def solution(mesh):
    owners, runs = mesh.shape["ulysses"], mesh.shape["blk"]
    fine = Mesh(mesh.devices.reshape(2, owners // 2, 4, 2, runs // 8), EVERY)
    tokens = P(("z", "y", "r"), ("x", "c"), None)
    rows = P(EVERY, None)
    return jax.shard_map(
        body,
        mesh=fine,
        in_specs=(tokens, tokens) + (P(),) * 3 + (rows,) * 4 + (P(),) * 2 + (rows,) * 3,
        out_specs=(tokens, tokens, P()) + (rows,) * 4 + (P(),) * 2 + (rows,) * 3,
        check_vma=False,
    )
```
